32 devices in a mesh: head: 4 (over y, x), blk: 8 (over z, core).
Axes of the slice: x: 2, y: 2, z: 4, core: 2. Of those that a mesh axis runs over, the one named last changes fastest.
Arguments:
- pre_tokens: bfloat16 [512, 2048], P('blk'), may hold values from -6 to 6
- dec_tokens: bfloat16 [12, 2048], replicated, may hold values from -6 to 6
- attn_gain: float32 [2048], replicated, may hold values from 0.25 to 1.75
- w_query: bfloat16 [2048, 2048], P(None, 'head'), may hold values from -0.125 to 0.125
- w_key: bfloat16 [2048, 2048], P(None, 'head'), may hold values from -0.125 to 0.125
- w_value: bfloat16 [2048, 2048], P(None, 'head'), may hold values from -0.125 to 0.125
- w_output: bfloat16 [2048, 2048], P('head'), may hold values from -0.125 to 0.125
- cache_keys: bfloat16 [64, 256, 2048], P('blk', None, 'head'), may hold values from -310 to 310
- cache_values: bfloat16 [64, 256, 2048], P('blk', None, 'head'), may hold values from -6 to 6
- block_request: int32 [64], P('blk'), may hold values from 0 to 13, as said below
- block_slot: int32 [64], P('blk'), may hold values from 0 to 15, as said below
- cache_lens: int32 [13], replicated, may hold values from 1 to 4096, as said below
- moe_gain: float32 [2048], replicated, may hold values from 0.25 to 1.75
- expert_ids: int32 [512, 8], P('blk'), may hold values from 0 to 15, all different within a row; in each aligned block of 64 rows (0 to 63, 64 to 127, ...) at most 64 rows name the same one
- expert_gates: bfloat16 [512, 8], P('blk'), may hold values from 0.049804688 to 0.29882812
- dec_expert_ids: int32 [12, 8], replicated, may hold values from 0 to 15, all different within a row
- dec_expert_gates: bfloat16 [12, 8], replicated, may hold values from 0.049804688 to 0.29882812
- w_gate: bfloat16 [16, 2048, 1024], P('blk', None, 'head'), may hold values from -0.125 to 0.125
- w_up: bfloat16 [16, 2048, 1024], P('blk', None, 'head'), may hold values from -0.125 to 0.125
- w_down: bfloat16 [16, 1024, 2048], P('blk', 'head'), may hold values from -0.1875 to 0.1875
Outputs:
- pre_hidden: bfloat16 [512, 2048], P('blk', 'head')
- dec_hidden: bfloat16 [12, 2048], P(None, 'head')
- new_cache: bfloat16 [2, 512, 2048], P(None, 'blk', 'head')
- dec_cache: bfloat16 [2, 12, 2048], P(None, None, 'head')
The draws below stay inside these ranges and needn't reach their ends.
Inputs may be any that keep to these rules, and one draw needn't show every extreme that they name: `block_request`: 13 marks a free block; request r owns exactly one block for each slot below ceil(cache_lens[r] / 256) and no other. `block_slot`: a block holds positions slot * 256 to slot * 256 + 255 of its request; free blocks have slot 0. `cache_lens`: requests 0 to 0 are the prefill requests, whose new tokens follow their cached ones; one request has exactly 4096 cached tokens, the others at most 1024. `expert_ids`: each row names 8 different experts; among the 64 tokens of one index of blk (aligned blocks of rows) no expert is named more than 64 times. `dec_expert_ids`: each row names 8 different experts.
All inputs are finite; a program needn't handle non-finite values.
Results may differ from the reference program's by a relative error of at most 0.0065.
The reference program's roundings to bfloat16 on the way count: a program that leaves them out, or rounds other values in their place, can miss the bound.
Values may be sent and summed in bfloat16 or wider, within the bound.
No kernel may reach another device: no remote copies, remote signals or barrier semaphores. Data moves between devices by JAX's collectives and lax.ppermute only.
A program may use at most 128 MiB of HBM per device.

```python
import math
import jax
import jax.numpy as jnp
import numpy as np
from jax import lax

D = 2048
HEADS = 16
HD = 128
FFE = 1024
TOPK = 8
TOK_DEV = 64
PRE = 1
DEC = 12
BLOCK = 256
REQS = 13
TOKENS = 512
EXPERTS = 16
CAP = 64
NBLOCKS = 64
MAXB = 16
OTHERB = 4
N_HEAD = 4
N_BLK = 8


def block_layout(key):
    base_key = jax.random.fold_in(key, 7)
    pick_key, count_key, fill_key, shuffle_key = jax.random.split(base_key, 4)
    request_ids = jnp.arange(REQS, dtype=jnp.int32)
    longest = jax.random.randint(pick_key, (), 0, REQS, dtype=jnp.int32)
    block_counts = jax.random.randint(count_key, (REQS,), 1, OTHERB + 1, dtype=jnp.int32)
    block_counts = jnp.where(request_ids == longest, MAXB, block_counts)
    last_fill = jax.random.randint(fill_key, (REQS,), 1, BLOCK + 1, dtype=jnp.int32)
    last_fill = jnp.where(request_ids == longest, BLOCK, last_fill)
    lengths = (block_counts - 1) * BLOCK + last_fill
    block_ends = jnp.cumsum(block_counts).astype(jnp.int32)
    block_starts = block_ends - block_counts
    positions = jnp.arange(NBLOCKS, dtype=jnp.int32)
    owners = jnp.sum((positions[:, None] >= block_ends[None, :]).astype(jnp.int32), axis=1)
    slot_index = jnp.where(owners < REQS, positions - block_starts[jnp.minimum(owners, REQS - 1)], 0)
    shuffled = jax.random.permutation(shuffle_key, NBLOCKS)
    return (owners[shuffled], slot_index[shuffled], lengths)


def draw_block_request(key, part):
    return block_layout(key)[0].astype(jnp.int32)


def draw_block_slot(key, part):
    return block_layout(key)[1].astype(jnp.int32)


def draw_cache_lens(key, part):
    return block_layout(key)[2].astype(jnp.int32)


def draw_cache_keys(key, part):
    normal_key = jax.random.fold_in(jax.random.fold_in(key, 3), 0)
    drawn = jnp.clip(jax.random.normal(normal_key, (NBLOCKS, BLOCK, HEADS * HD), jnp.float32), -6.0, 6.0)
    return drawn.astype(jnp.bfloat16)


def block_scale(own_key, extent, cuts, least, largest):
    def one(axis_at, blocks):
        draws = jax.random.uniform(jax.random.fold_in(jax.random.fold_in(own_key, 6), axis_at), (blocks,), jnp.float32, least / len(cuts), largest / len(cuts))
        return jnp.repeat(jnp.exp(draws), extent[axis_at] // blocks).reshape((-1,) + (1,) * (len(extent) - axis_at - 1))

    level = one(*cuts[0])
    for cut in cuts[1:]:
        level = level * one(*cut)
    return level


def distinct(stream_key, rows, number_of, top, lift):
    order = jax.random.permutation(jax.random.fold_in(stream_key, 1), number_of)
    favour = order
    for power in range(3):
        favour = favour * favour // number_of
    favour = favour * lift // number_of
    tickets = jax.random.randint(jax.random.fold_in(stream_key, 2), (rows, number_of), 0, 4096) + favour
    sure = jax.random.permutation(jax.random.fold_in(stream_key, 3), rows)[jnp.arange(number_of) % rows]
    tickets = jnp.where(jnp.arange(rows)[:, None] == sure[None, :], 1 << 14, tickets)
    score = tickets * number_of + jnp.arange(number_of)
    return lax.top_k(score.astype(jnp.int32), top)[1].astype(jnp.int32)


def routed_block(own_key, own, number, rows, count, top, bound, skew):
    ranking = jax.random.permutation(own_key, count)
    packed, usual = shares(count, rows * top, bound, skew, True), shares(count, rows * top, bound, skew, False)
    places = jnp.arange(count)

    def named(sizes, rotation):
        used = int((sizes > 0).sum())
        fixed = max(1, used // 4)
        moved = fixed + (places - fixed + rotation * (used - fixed)) % max(1, count - fixed)
        return jnp.zeros((count,), jnp.int32).at[ranking[jnp.where(places < fixed, places, moved)]].set(jnp.asarray(sizes, jnp.int32))

    sizes = jnp.where(number % 4 == 0, named(packed, number // 4), named(usual, number - number // 4 - 1))
    mixed = jax.random.permutation(jax.random.fold_in(own, 3), count)
    donor, taker = mixed[0:count // 2 * 2:2], mixed[1:count // 2 * 2:2]
    margin = jnp.minimum(sizes[donor] - 1, bound - sizes[taker]) // 2
    margin = jnp.where((donor == ranking[0]) | (taker == ranking[0]) | (sizes[taker] == 0), 0, jnp.maximum(margin, 0))
    moved = jax.random.randint(jax.random.fold_in(own, 4), (count // 2,), 0, 1 << 20) % (margin + 1)
    sizes = sizes.at[donor].add(-moved).at[taker].add(moved)
    items = jnp.searchsorted(jnp.cumsum(sizes), jnp.arange(rows * top), side="right").astype(jnp.int32)
    grid = items.reshape(top, rows).T
    grid = grid[jax.random.permutation(jax.random.fold_in(own, 1), rows)]
    rotation = jax.random.randint(jax.random.fold_in(own, 2), (rows, 1), 0, top)
    return jnp.take_along_axis(grid, (jnp.arange(top)[None, :] + rotation) % top, axis=1)


def shares(amount, total, most, lean, full):
    loads = [(1 << 20) // math.isqrt(rank ** lean) + 1 for rank in range(1, amount + 1)]
    largest = most if full else min(most, max(-(-total // amount), total * loads[0] // sum(loads)))
    least = 1 if total - largest >= amount - 1 else 0
    given, surplus = [largest] + [least] * (amount - 1), total - largest - least * (amount - 1)
    while surplus > 0:
        movable = [i for i in range(1, amount) if given[i] < largest] or [i for i in range(1, amount) if given[i] < most]
        pool, left = sum([loads[i] for i in movable]), surplus
        for i in movable:
            addition = min(most - given[i], max(1, left * loads[i] // pool), surplus)
            given[i] = given[i] + addition
            surplus = surplus - addition
    return np.array(given)


def bell_draw(own_key, dims, scale, reach, pieces=(), held_as=jnp.bfloat16):
    gain = block_scale(own_key, dims, pieces, -0.22, 0.18) if pieces else 1.0
    values = jax.random.normal(own_key, dims, jnp.float32) * scale * gain
    return jnp.minimum(jnp.maximum(values, -reach), reach).astype(held_as)


def setup_inputs(seed: int = 0) -> dict:
    seeds = jax.random.split(jax.random.key(seed), 21)
    pre_tokens = bell_draw(seeds[0], (TOKENS, D), 1.0, 6.0, ((0, 8),))
    dec_tokens = bell_draw(seeds[1], (DEC, D), 1.0, 6.0)
    attn_gain = jnp.clip(1.0 + 0.15 * jax.random.normal(seeds[2], (D,), jnp.float32), 0.25, 1.75)
    w_query = bell_draw(seeds[3], (D, HEADS * HD), D ** -0.5, 0.125, ((1, 4),))
    w_key = bell_draw(seeds[4], (D, HEADS * HD), D ** -0.5, 0.125, ((1, 4),))
    w_value = bell_draw(seeds[5], (D, HEADS * HD), D ** -0.5, 0.125, ((1, 4),))
    w_output = bell_draw(seeds[6], (HEADS * HD, D), (HEADS * HD) ** -0.5, 0.125, ((0, 4),))
    cache_keys = draw_cache_keys(jax.random.fold_in(seeds[20], 71), 0)
    cache_values = bell_draw(seeds[8], (NBLOCKS, BLOCK, HEADS * HD), 1.0, 6.0, ((0, 8), (2, 4)))
    block_request = draw_block_request(jax.random.fold_in(seeds[20], 71), 0)
    block_slot = draw_block_slot(jax.random.fold_in(seeds[20], 71), 0)
    cache_lens = draw_cache_lens(jax.random.fold_in(seeds[20], 71), 0)
    moe_gain = jnp.clip(1.0 + 0.15 * jax.random.normal(seeds[12], (D,), jnp.float32), 0.25, 1.75)
    expert_ids_keys = jax.random.split(jax.random.fold_in(seeds[13], 1), TOKENS // TOK_DEV)
    expert_ids_turns = jax.random.permutation(jax.random.fold_in(seeds[13], 3), TOKENS // TOK_DEV)
    expert_ids = jax.vmap(lambda own, number: routed_block(jax.random.fold_in(seeds[13], 2), own, number, TOK_DEV, EXPERTS, TOPK, CAP, 1))(expert_ids_keys, expert_ids_turns).reshape((TOKENS, TOPK))
    expert_gates = jnp.clip(0.049804688 + 0.24902344 * jax.random.uniform(seeds[14], (TOKENS, TOPK), jnp.float32) ** block_scale(seeds[14], (TOKENS, TOPK), ((0, 8),), -0.2, 0.2), 0.049804688, 0.29882812).astype(jnp.bfloat16)
    dec_expert_ids = distinct(seeds[15], DEC, EXPERTS, TOPK, 0)
    dec_expert_gates = jnp.clip(jax.random.uniform(seeds[16], (DEC, TOPK), jnp.float32, 0.049804688, 0.29882812), 0.049804688, 0.29882812).astype(jnp.bfloat16)
    w_gate = bell_draw(seeds[17], (EXPERTS, D, FFE), D ** -0.5, 0.125, ((0, 8), (2, 4)))
    w_up = bell_draw(seeds[18], (EXPERTS, D, FFE), D ** -0.5, 0.125, ((0, 8), (2, 4)))
    w_down = bell_draw(seeds[19], (EXPERTS, FFE, D), FFE ** -0.5, 0.1875, ((0, 8), (1, 4)))
    return {"pre_tokens": pre_tokens, "dec_tokens": dec_tokens, "attn_gain": attn_gain, "w_query": w_query, "w_key": w_key, "w_value": w_value, "w_output": w_output, "cache_keys": cache_keys, "cache_values": cache_values, "block_request": block_request, "block_slot": block_slot, "cache_lens": cache_lens, "moe_gain": moe_gain, "expert_ids": expert_ids, "expert_gates": expert_gates, "dec_expert_ids": dec_expert_ids, "dec_expert_gates": dec_expert_gates, "w_gate": w_gate, "w_up": w_up, "w_down": w_down}


eps_norm = 1e-06
rope_base = 50000.0
neg_fill = -1e+30

def rms_scale(row_data, gain_vec):
    values = row_data.astype(jnp.float32)
    meansq = lax.optimization_barrier(jnp.mean(values * values, axis=-1, keepdims=True))
    return values * lax.rsqrt(meansq + eps_norm) * gain_vec

def rotate(blocks, positions):
    half_dim = blocks.shape[-1] // 2
    frequencies = rope_base ** (-jnp.arange(half_dim, dtype=jnp.float32) / half_dim)
    angles = positions.astype(jnp.float32)[:, None] * frequencies[None, :]
    cosine = jnp.cos(angles)[:, None, :]
    sine_part = jnp.sin(angles)[:, None, :]
    first_half = blocks[..., :half_dim]
    second_half = blocks[..., half_dim:]
    return jnp.concatenate([first_half * cosine - second_half * sine_part, second_half * cosine + first_half * sine_part], axis=-1)

def project(normed, w_query, w_key, w_value, positions):
    row_count = normed.shape[0]
    queries = jnp.dot(normed, w_query, preferred_element_type=jnp.float32).reshape(row_count, HEADS, HD)
    key_rows = jnp.dot(normed, w_key, preferred_element_type=jnp.float32).reshape(row_count, HEADS, HD)
    value_rows = jnp.dot(normed, w_value, preferred_element_type=jnp.float32)
    queries = rotate(queries, positions).reshape(row_count, -1).astype(jnp.bfloat16)
    key_rows = rotate(key_rows, positions).reshape(row_count, -1).astype(jnp.bfloat16)
    return (queries, key_rows, value_rows.astype(jnp.bfloat16))

def group_stats(queries, key_rows, value_rows, live_mask):
    row_count = queries.shape[0]
    q_heads = queries.astype(jnp.float32).reshape(row_count, HEADS, HD)
    k_heads = key_rows.astype(jnp.float32).reshape(-1, HEADS, HD)
    v_heads = value_rows.astype(jnp.float32).reshape(-1, HEADS, HD)
    scores = jnp.einsum('qhd,khd->qhk', q_heads, k_heads) * HD ** (-0.5)
    masked = live_mask[:, None, :]
    highest = lax.optimization_barrier(jnp.max(jnp.where(masked, scores, neg_fill), axis=-1))
    weights = jnp.where(masked, jnp.exp(scores - highest[..., None]), 0.0)
    totals = lax.optimization_barrier(jnp.sum(weights, axis=-1))
    rounded = lax.optimization_barrier(weights.astype(jnp.bfloat16)).astype(jnp.float32)
    summed = jnp.einsum('qhk,khd->qhd', rounded, v_heads)
    return (highest, totals, summed)

def merge_pair(first_state, second_state):
    top_one, total_one, acc_one = first_state
    top_two, total_two, acc_two = second_state
    highest = jnp.maximum(top_one, top_two)
    scale_one = jnp.exp(top_one - highest)
    scale_two = jnp.exp(top_two - highest)
    return (highest, total_one * scale_one + total_two * scale_two, acc_one * scale_one[..., None] + acc_two * scale_two[..., None])

def empty_state(row_count):
    return (jnp.full((row_count, HEADS), neg_fill, jnp.float32), jnp.zeros((row_count, HEADS), jnp.float32), jnp.zeros((row_count, HEADS, HD), jnp.float32))

def finish(state_now):
    result = state_now[2] / state_now[1][..., None]
    return result.reshape(result.shape[0], -1).astype(jnp.bfloat16)

def prefill_attention(queries, new_keys, new_values, cache_keys, cache_values, block_request, block_slot, cache_lens):
    request_len = TOKENS // PRE
    offsets = jnp.arange(BLOCK, dtype=jnp.int32)
    results = []
    for request in range(PRE):
        row_block = queries[request * request_len:(request + 1) * request_len]
        group_keys = new_keys[request * request_len:(request + 1) * request_len].reshape(request_len // TOK_DEV, TOK_DEV, -1)
        group_values = new_values[request * request_len:(request + 1) * request_len].reshape(request_len // TOK_DEV, TOK_DEV, -1)

        def new_group(carried, group_pair):
            live_keys = jnp.ones((1, TOK_DEV), jnp.bool_)
            return (merge_pair(carried, group_stats(row_block, group_pair[0], group_pair[1], live_keys)), None)
        carried, _ = lax.scan(new_group, empty_state(request_len), (group_keys, group_values))
        length_limit = cache_lens[request]

        def cache_block(inner_state, block_index):

            def add_block(current):
                key_positions = block_slot[block_index] * BLOCK + offsets
                live_keys = (key_positions < length_limit)[None, :]
                return merge_pair(current, group_stats(row_block, cache_keys[block_index], cache_values[block_index], live_keys))
            return (lax.cond(block_request[block_index] == request, add_block, lambda current: current, inner_state), None)
        carried, _ = lax.scan(cache_block, carried, jnp.arange(NBLOCKS, dtype=jnp.int32))
        results.append(finish(carried))
    return jnp.concatenate(results, axis=0)

def decode_attention(queries, new_keys, new_values, cache_keys, cache_values, block_request, block_slot, cache_lens):
    targets = PRE + jnp.arange(DEC, dtype=jnp.int32)
    offsets = jnp.arange(BLOCK, dtype=jnp.int32)
    own_mask = jnp.arange(DEC)[:, None] == jnp.arange(DEC)[None, :]
    carried = group_stats(queries, new_keys, new_values, own_mask)

    def cache_block(inner_state, block_index):
        block_owner = block_request[block_index]
        length_limit = cache_lens[jnp.minimum(block_owner, REQS - 1)]
        key_positions = block_slot[block_index] * BLOCK + offsets
        live_keys = (targets[:, None] == block_owner) & (key_positions < length_limit)[None, :]
        return (merge_pair(inner_state, group_stats(queries, cache_keys[block_index], cache_values[block_index], live_keys)), None)
    carried, _ = lax.scan(cache_block, carried, jnp.arange(NBLOCKS, dtype=jnp.int32))
    return finish(carried)

def expert_rows(row_data, gate_weight, up_weight, down_weight):
    gate_part = jnp.dot(row_data, gate_weight, preferred_element_type=jnp.float32)
    up_part = jnp.dot(row_data, up_weight, preferred_element_type=jnp.float32)
    active = (jax.nn.silu(gate_part) * up_part).astype(jnp.bfloat16)
    quarter = FFE // N_HEAD
    summed = jnp.zeros((row_data.shape[0], D), jnp.float32)
    for part_index in range(N_HEAD):
        part_out = jnp.dot(active[:, part_index * quarter:(part_index + 1) * quarter], down_weight[part_index * quarter:(part_index + 1) * quarter], preferred_element_type=jnp.float32)
        summed = summed + lax.optimization_barrier(part_out.astype(jnp.bfloat16)).astype(jnp.float32)
    return summed

def prefill_experts(row_data, chosen_ids, gate_vals, w_gate, w_up, w_down):
    capacity = N_BLK * CAP
    slot_ids = jnp.arange(capacity, dtype=jnp.int32)

    def one_expert(carried, expert):
        chosen = chosen_ids == expert
        member = jnp.any(chosen, axis=1)
        weight = lax.optimization_barrier(jnp.sum(jnp.where(chosen, gate_vals.astype(jnp.float32), 0.0), axis=1))
        counts = jnp.cumsum(member.astype(jnp.int32), dtype=jnp.int32)
        picked = jnp.minimum(jnp.searchsorted(counts, slot_ids + 1).astype(jnp.int32), TOKENS - 1)
        in_use = slot_ids < counts[-1]
        outputs = expert_rows(row_data[picked], w_gate[expert], w_up[expert], w_down[expert])
        scaled = outputs * jnp.where(in_use, weight[picked], 0.0)[:, None]
        return (carried.at[picked].add(scaled), None)
    combined, _ = lax.scan(one_expert, jnp.zeros((TOKENS, D), jnp.float32), jnp.arange(EXPERTS, dtype=jnp.int32))
    return combined

def decode_experts(row_data, chosen_ids, gate_vals, w_gate, w_up, w_down):

    def one_expert(carried, expert):
        weight = lax.optimization_barrier(jnp.sum(jnp.where(chosen_ids == expert, gate_vals.astype(jnp.float32), 0.0), axis=1))
        return (carried + weight[:, None] * expert_rows(row_data, w_gate[expert], w_up[expert], w_down[expert]), None)
    combined, _ = lax.scan(one_expert, jnp.zeros((DEC, D), jnp.float32), jnp.arange(EXPERTS, dtype=jnp.int32))
    return combined

def reference(pre_tokens, dec_tokens, attn_gain, w_query, w_key, w_value, w_output, cache_keys, cache_values, block_request, block_slot, cache_lens, moe_gain, expert_ids, expert_gates, dec_expert_ids, dec_expert_gates, w_gate, w_up, w_down):
    request_len = TOKENS // PRE
    token_index = jnp.arange(TOKENS, dtype=jnp.int32)
    pre_positions = cache_lens[token_index // request_len] + token_index % request_len
    dec_positions = cache_lens[PRE:]
    normed_pre = rms_scale(pre_tokens, attn_gain).astype(jnp.bfloat16)
    normed_dec = rms_scale(dec_tokens, attn_gain).astype(jnp.bfloat16)
    query_pre, key_pre, value_pre = project(normed_pre, w_query, w_key, w_value, pre_positions)
    query_dec, key_dec, value_dec = project(normed_dec, w_query, w_key, w_value, dec_positions)
    attn_pre = prefill_attention(query_pre, key_pre, value_pre, cache_keys, cache_values, block_request, block_slot, cache_lens)
    attn_dec = decode_attention(query_dec, key_dec, value_dec, cache_keys, cache_values, block_request, block_slot, cache_lens)
    mid_pre = pre_tokens.astype(jnp.float32) + jnp.dot(attn_pre, w_output, preferred_element_type=jnp.float32)
    mid_dec = dec_tokens.astype(jnp.float32) + jnp.dot(attn_dec, w_output, preferred_element_type=jnp.float32)
    moe_in_pre = rms_scale(mid_pre, moe_gain).astype(jnp.bfloat16)
    moe_in_dec = rms_scale(mid_dec, moe_gain).astype(jnp.bfloat16)
    moe_pre = prefill_experts(moe_in_pre, expert_ids, expert_gates, w_gate, w_up, w_down)
    moe_dec = decode_experts(moe_in_dec, dec_expert_ids, dec_expert_gates, w_gate, w_up, w_down)
    return ((mid_pre + moe_pre).astype(jnp.bfloat16), (mid_dec + moe_dec).astype(jnp.bfloat16), jnp.stack([key_pre, value_pre]), jnp.stack([key_dec, value_dec]))
```

```python
import functools

import jax
import jax.numpy as jnp
from jax import lax
from jax.experimental import pallas as pl
from jax.experimental.pallas import tpu as pltpu
from jax.sharding import PartitionSpec as P

HD = 128
PRE = 1
DEC = 12
REQS = 13
DPAD = 16
TILE = 256

eps_norm = 1e-06
rope_base = 50000.0
neg_fill = -1e30
bf16 = jnp.bfloat16
f32 = jnp.float32


def rms_scale(row_data, gain_vec):
    values = row_data.astype(f32)
    meansq = jnp.mean(values * values, axis=-1, keepdims=True)
    return values * lax.rsqrt(meansq + eps_norm) * gain_vec


def rotate(flat, cosine, sine):
    rows = flat.shape[0]
    blocks = flat.reshape(rows, -1, HD)
    first = blocks[..., : HD // 2]
    second = blocks[..., HD // 2 :]
    return jnp.concatenate(
        [first * cosine - second * sine, second * cosine + first * sine], axis=-1
    ).reshape(rows, -1)


def swap(value, axis, mask):
    count = lax.axis_size(axis)
    return lax.ppermute(value, axis, [(i, i ^ mask) for i in range(count)])


def span(index, size):
    return pl.ds(pl.multiple_of(index * size, size), size)


def lanes(head):
    return slice(head * HD, (head + 1) * HD)


def group(query, keys, values, live):
    scores = lax.dot_general(
        query, keys, (((1,), (1,)), ((), ())), preferred_element_type=f32
    ) * HD ** (-0.5)
    top = jnp.max(scores if live is None else jnp.where(live, scores, neg_fill), axis=-1, keepdims=True)
    weights = jnp.exp(scores - top)
    if live is not None:
        weights = jnp.where(live, weights, 0.0)
    total = jnp.sum(weights, axis=-1, keepdims=True)
    acc = jnp.dot(weights.astype(bf16), values, preferred_element_type=f32)
    return top, total, acc


def attention_kernel(
    owner_ref,
    live_ref,
    first_ref,
    query_a,
    query_b,
    query_d,
    key_new,
    value_new,
    key_dec,
    value_dec,
    cache_k,
    cache_v,
    keep,
    send,
    tops,
    totals,
):
    step = pl.program_id(0)
    half = query_a.shape[0]
    heads = query_a.shape[1] // HD
    tile = min(TILE, half)
    sides = ((query_a, keep, 0), (query_b, send, half))

    def over_tiles(body):
        for side in sides:
            if half == tile:
                body(side, 0)
            else:

                @pl.loop(0, half // tile)
                def _(index):
                    body(side, pl.multiple_of(index * tile, tile))

    def merge(acc_ref, row, size, state_row, head, found):
        top, total, acc = found
        rows = pl.ds(row, size)
        state = pl.ds(state_row, size)
        old_top = tops[head, state, :]
        best = jnp.maximum(old_top, top)
        old_scale = jnp.exp(old_top - best)
        scale = jnp.exp(top - best)
        tops[head, state, :] = best
        totals[head, state, :] = totals[head, state, :] * old_scale + total * scale
        acc_ref[rows, lanes(head)] = acc_ref[rows, lanes(head)] * old_scale + acc * scale

    @pl.when(step == 0)
    def _():
        def start(side, row):
            query, acc_ref, base = side
            for head in range(heads):
                top, total, acc = group(
                    query[pl.ds(row, tile), lanes(head)],
                    key_new[:, lanes(head)],
                    value_new[:, lanes(head)],
                    None,
                )
                tops[head, pl.ds(base + row, tile), :] = top
                totals[head, pl.ds(base + row, tile), :] = total
                acc_ref[pl.ds(row, tile), lanes(head)] = acc

        over_tiles(start)
        mine = first_ref[0] == 1
        for head in range(heads):
            own = jnp.sum(
                query_d[:, lanes(head)].astype(f32) * key_dec[:, lanes(head)].astype(f32),
                axis=-1,
                keepdims=True,
            ) * HD ** (-0.5)
            tops[head, pl.ds(2 * half, DPAD), :] = jnp.where(mine, own, neg_fill)
            totals[head, pl.ds(2 * half, DPAD), :] = jnp.where(
                mine, jnp.ones_like(own), jnp.zeros_like(own)
            )
            keep[pl.ds(half, DPAD), lanes(head)] = jnp.where(
                mine, value_dec[:, lanes(head)].astype(f32), 0.0
            )

    owner = owner_ref[step]
    count = live_ref[step]

    @pl.when(owner < PRE)
    def _():
        live = lax.broadcasted_iota(jnp.int32, (tile, cache_k.shape[1]), 1) < count

        def add(side, row):
            query, acc_ref, base = side
            for head in range(heads):
                found = group(
                    query[pl.ds(row, tile), lanes(head)],
                    cache_k[0, :, lanes(head)],
                    cache_v[0, :, lanes(head)],
                    live,
                )
                merge(acc_ref, row, tile, base + row, head, found)

        over_tiles(add)

    @pl.when((owner >= PRE) & (owner < REQS))
    def _():
        shape = (DPAD, cache_k.shape[1])
        live = (lax.broadcasted_iota(jnp.int32, shape, 1) < count) & (
            lax.broadcasted_iota(jnp.int32, shape, 0) == owner - PRE
        )
        for head in range(heads):
            found = group(
                query_d[:, lanes(head)],
                cache_k[0, :, lanes(head)],
                cache_v[0, :, lanes(head)],
                live,
            )
            merge(keep, half, DPAD, 2 * half, head, found)

    @pl.when(step == pl.num_programs(0) - 1)
    def _():
        width = heads * HD
        for ref, base in ((keep, 0), (send, half)):
            for row, size, state in ((0, half, base), (half, DPAD, 2 * half)):
                place = lax.broadcasted_iota(jnp.int32, (size, HD), 1)
                packed = jnp.zeros((size, HD), f32)
                for head in range(heads):
                    packed = jnp.where(place == head, tops[head, pl.ds(state, size), :], packed)
                    packed = jnp.where(
                        place == heads + head, totals[head, pl.ds(state, size), :], packed
                    )
                ref[pl.ds(row, size), width : width + HD] = packed
        send[pl.ds(half, DPAD), :width] = keep[pl.ds(half, DPAD), :width]


def attention(queries, query_d, new, dec, cache_keys, cache_values, owner, count, first):
    query_a, query_b = queries
    half, width = query_a.shape
    heads = width // HD
    blocks, block_len = cache_keys.shape[:2]
    whole = lambda arr: pl.BlockSpec(arr.shape, lambda *_: (0,) * arr.ndim)
    block = pl.BlockSpec((1, block_len, width), lambda i, *_: (i, 0, 0))
    fixed = (query_a, query_b, query_d, *new, *dec)
    shape = jax.ShapeDtypeStruct((half + DPAD, width + HD), f32)
    return pl.pallas_call(
        attention_kernel,
        out_shape=(shape, shape),
        grid_spec=pltpu.PrefetchScalarGridSpec(
            num_scalar_prefetch=3,
            grid=(blocks,),
            in_specs=[*(whole(arr) for arr in fixed), block, block],
            out_specs=(whole(shape), whole(shape)),
            scratch_shapes=[
                pltpu.VMEM((heads, 2 * half + DPAD, 1), f32),
                pltpu.VMEM((heads, 2 * half + DPAD, 1), f32),
            ],
        ),
        compiler_params=pltpu.CompilerParams(
            dimension_semantics=("arbitrary",), vmem_limit_bytes=40 << 20
        ),
        name="attention",
    )(owner, count, first, *fixed, cache_keys, cache_values)


def merge_core_kernel(mine, other, *outs):
    rows, full = mine.shape
    width = full - HD
    heads = width // HD
    place = lax.broadcasted_iota(jnp.int32, (rows, HD), 1)
    packed = jnp.zeros((rows, HD), f32)
    stats_a = mine[:, width:]
    stats_b = other[:, width:]
    tok = (rows - DPAD) // len(outs)

    def put(where, value):
        for index, out in enumerate(outs):
            out[0:tok, where] = value[index * tok : (index + 1) * tok]
            out[tok : tok + DPAD, where] = value[rows - DPAD :]

    for head in range(heads):
        top_a, top_b = stats_a[:, head : head + 1], stats_b[:, head : head + 1]
        sum_a = stats_a[:, heads + head : heads + head + 1]
        sum_b = stats_b[:, heads + head : heads + head + 1]
        best = jnp.maximum(top_a, top_b)
        scale_a = jnp.exp(top_a - best)
        scale_b = jnp.exp(top_b - best)
        packed = jnp.where(place == head, best, packed)
        packed = jnp.where(place == heads + head, sum_a * scale_a + sum_b * scale_b, packed)
        put(lanes(head), (mine[:, lanes(head)] * scale_a + other[:, lanes(head)] * scale_b).astype(bf16))
    high = packed.astype(bf16).astype(f32)
    middle = (packed - high).astype(bf16).astype(f32)
    low = (packed - high) - middle
    coded = high + pltpu.roll(middle, 2 * heads, 1) + pltpu.roll(low, 4 * heads, 1)
    put(slice(width, full), coded.astype(bf16))


def merge_core(mine, other, parts):
    rows, full = mine.shape
    tok = (rows - DPAD) // parts
    shape = jax.ShapeDtypeStruct((tok + DPAD, full), bf16)
    return pl.pallas_call(
        merge_core_kernel,
        out_shape=(shape,) * parts,
        compiler_params=pltpu.CompilerParams(vmem_limit_bytes=40 << 20),
        name="merge_core",
    )(mine, other)


def tree_sum(values):
    values = list(values)
    while len(values) > 1:
        values = [a + b for a, b in zip(values[::2], values[1::2])]
    return values[0]


def project_kernel(parts, head_ref, *refs):
    pieces = refs[:parts]
    weight = refs[parts]
    outs = refs[parts + 1 :]
    rows, full = pieces[0].shape
    width = full - HD
    heads = width // HD
    columns = outs[0].shape[1]
    stats = []
    for piece in pieces:
        coded = piece[:, width:].astype(f32)
        stats.append(
            (coded + pltpu.roll(coded, HD - 2 * heads, 1)) + pltpu.roll(coded, HD - 4 * heads, 1)
        )
    attended = []
    for head in range(heads):
        tops = [s[:, head : head + 1] for s in stats]
        best = functools.reduce(jnp.maximum, tops)
        scales = [jnp.exp(top - best) for top in tops]
        total = tree_sum([s[:, heads + head : heads + head + 1] * c for s, c in zip(stats, scales)])
        acc = tree_sum([piece[:, lanes(head)].astype(f32) * c for piece, c in zip(pieces, scales)])
        attended.append((acc / total).astype(bf16))
    attended = jnp.concatenate(attended, axis=1)
    for offset, out in enumerate(outs):
        place = lax.bitwise_xor(head_ref[0], offset)
        out[...] = jnp.dot(attended, weight[:, span(place, columns)], preferred_element_type=f32)


def project_out(pieces, w_output, head_index, head_count):
    rows = pieces[0].shape[0]
    columns = w_output.shape[1] // head_count
    shape = jax.ShapeDtypeStruct((rows, columns), f32)
    vmem = pl.BlockSpec(memory_space=pltpu.VMEM)
    return pl.pallas_call(
        functools.partial(project_kernel, len(pieces)),
        out_shape=(shape,) * head_count,
        in_specs=[pl.BlockSpec(memory_space=pltpu.SMEM)] + [vmem] * (len(pieces) + 1),
        out_specs=(vmem,) * head_count,
        compiler_params=pltpu.CompilerParams(vmem_limit_bytes=32 << 20),
        name="project_out",
    )(head_index, *pieces, w_output)


def experts_kernel(chunks, head_ref, *refs):
    own = refs[:chunks]
    other = refs[chunks : 2 * chunks]
    gates_own, gates_other, w_gate, w_up, w_down = refs[2 * chunks : 2 * chunks + 5]
    keep = refs[2 * chunks + 5 : 3 * chunks + 5]
    send = refs[3 * chunks + 5 :]
    experts = w_gate.shape[0]
    width = own[0].shape[1]
    half = own[0].shape[0] - DPAD
    tile = min(TILE, half)
    places = [lax.bitwise_xor(head_ref[0], offset) for offset in range(chunks)]

    def run(parts, gates, row, size):
        rows = pl.ds(row, size)
        total = [None] * chunks
        for expert in range(experts):
            gate = up = None
            for part, place in zip(parts, places):
                data = part[rows, :]
                g = jnp.dot(data, w_gate[expert, span(place, width), :], preferred_element_type=f32)
                u = jnp.dot(data, w_up[expert, span(place, width), :], preferred_element_type=f32)
                gate = g if gate is None else gate + g
                up = u if up is None else up + u
            act = (gate / (1.0 + jnp.exp(-gate)) * up).astype(bf16)
            factor = gates[rows, expert : expert + 1]
            for index, place in enumerate(places):
                down = jnp.dot(act, w_down[expert, :, span(place, width)], preferred_element_type=f32)
                down = down.astype(bf16).astype(f32) * factor
                total[index] = down if total[index] is None else total[index] + down
        return total

    for row in range(0, half, tile):
        for index, value in enumerate(run(other, gates_other, row, tile)):
            send[index][row : row + tile, :] = value.astype(bf16)
    for row in range(0, half, tile):
        size = tile + (DPAD if row + tile == half else 0)
        for index, value in enumerate(run(own, gates_own, row, size)):
            value = value.astype(bf16)
            keep[index][row : row + size, :] = value
            if size > tile:
                send[index][half : half + DPAD, :] = value[tile:]


def run_experts(own, other, gates_own, gates_other, w_gate, w_up, w_down, head_index):
    chunks = len(own)
    shape = jax.ShapeDtypeStruct(own[0].shape, bf16)
    vmem = pl.BlockSpec(memory_space=pltpu.VMEM)
    outs = pl.pallas_call(
        functools.partial(experts_kernel, chunks),
        out_shape=(shape,) * (2 * chunks),
        in_specs=[pl.BlockSpec(memory_space=pltpu.SMEM)] + [vmem] * (2 * chunks + 5),
        out_specs=(vmem,) * (2 * chunks),
        compiler_params=pltpu.CompilerParams(vmem_limit_bytes=48 << 20),
        name="experts",
    )(head_index, *own, *other, gates_own, gates_other, w_gate, w_up, w_down)
    return outs[:chunks], outs[chunks:]


def per_device(
    pre_tokens,
    dec_tokens,
    attn_gain,
    w_query,
    w_key,
    w_value,
    w_output,
    cache_keys,
    cache_values,
    block_request,
    block_slot,
    cache_lens,
    moe_gain,
    expert_ids,
    expert_gates,
    dec_expert_ids,
    dec_expert_gates,
    w_gate,
    w_up,
    w_down,
):
    tok, model_width = pre_tokens.shape
    blk_count = lax.axis_size("blk")
    blk_index = lax.axis_index("blk")
    head_count = lax.axis_size("head")
    head_index = lax.axis_index("head")
    chips = blk_count // 2
    head_scalar = head_index.reshape(1).astype(jnp.int32)
    part_width = model_width // head_count

    request_len = tok * blk_count // PRE
    first_row = blk_index * tok
    request_ids = jnp.arange(REQS, dtype=jnp.int32)
    my_request = first_row // request_len
    my_length = jnp.sum(jnp.where(request_ids == my_request, cache_lens, 0))
    pre_positions = my_length + first_row - my_request * request_len + jnp.arange(tok, dtype=jnp.int32)
    positions = jnp.concatenate(
        [pre_positions, cache_lens[PRE : PRE + DEC], jnp.zeros((DPAD - DEC,), jnp.int32)]
    )
    frequencies = rope_base ** (-jnp.arange(HD // 2, dtype=f32) / (HD // 2))
    angles = positions.astype(f32)[:, None] * frequencies[None, :]
    cosine = jnp.cos(angles)[:, None, :]
    sine = jnp.sin(angles)[:, None, :]

    tokens = jnp.concatenate(
        [pre_tokens, dec_tokens, jnp.zeros((DPAD - DEC, model_width), bf16)], axis=0
    )
    normed = rms_scale(tokens, attn_gain).astype(bf16)
    query = rotate(jnp.dot(normed, w_query, preferred_element_type=f32), cosine, sine).astype(bf16)
    key = rotate(jnp.dot(normed, w_key, preferred_element_type=f32), cosine, sine).astype(bf16)
    value = jnp.dot(normed, w_value, preferred_element_type=f32).astype(bf16)
    new_cache = jnp.stack([key[:tok], value[:tok]])
    dec_cache = jnp.stack([key[tok : tok + DEC], value[tok : tok + DEC]])

    def gather_chips(piece):
        return [piece] + [swap(piece, "blk", 2 * o) for o in range(1, chips)]

    query_a = jnp.concatenate(gather_chips(query[:tok]), axis=0)
    query_b = swap(query_a, "blk", 1)

    experts_all = w_gate.shape[0] * blk_count
    expert_range = jnp.arange(experts_all, dtype=jnp.int32)

    def gate_table(ids, gates):
        return jnp.sum(
            jnp.where(ids[:, :, None] == expert_range, gates.astype(f32)[:, :, None], 0.0), axis=1
        )

    table = gate_table(expert_ids, expert_gates).astype(bf16)
    table_a = jnp.concatenate(gather_chips(table), axis=0)
    table_b = swap(table_a, "blk", 1)
    table_d = jnp.concatenate(
        [
            gate_table(dec_expert_ids, dec_expert_gates).astype(bf16),
            jnp.zeros((DPAD - DEC, experts_all), bf16),
        ],
        axis=0,
    )

    def local_gates(rows):
        mine = blk_index * w_gate.shape[0] + jnp.arange(w_gate.shape[0], dtype=jnp.int32)
        return jnp.sum(
            jnp.where(expert_range[None, None, :] == mine[None, :, None], rows.astype(f32)[:, None, :], 0.0),
            axis=2,
        )

    gates_own = local_gates(jnp.concatenate([table_a, table_d], axis=0))
    gates_other = local_gates(table_b)

    lengths = jnp.sum(jnp.where(request_ids[None, :] == block_request[:, None], cache_lens[None, :], 0), axis=1)
    count = jnp.clip(lengths - block_slot * cache_keys.shape[1], 0, cache_keys.shape[1]).astype(jnp.int32)
    first = (blk_index == 0).astype(jnp.int32).reshape(1)
    keep, send = attention(
        (query_a, query_b),
        query[tok:],
        (key[:tok], value[:tok]),
        (key[tok:], value[tok:]),
        cache_keys,
        cache_values,
        block_request,
        count,
        first,
    )
    pieces = merge_core(keep, swap(send, "blk", 1), chips)
    pieces = [pieces[0]] + [swap(pieces[o], "blk", 2 * o) for o in range(1, chips)]
    partial = project_out(pieces, w_output, head_scalar, head_count)
    arrived = [partial[0]] + [swap(partial[o], "head", o) for o in range(1, head_count)]

    def own_columns(arr):
        return lax.dynamic_slice_in_dim(arr, head_index * part_width, part_width, arr.ndim - 1)

    mid = own_columns(tokens).astype(f32) + tree_sum(arrived)
    square = jnp.sum(mid * mid, axis=1)[None, :]
    square = tree_sum([square] + [swap(square, "head", o) for o in range(1, head_count)])
    scale = lax.rsqrt(square[0][:, None] / model_width + eps_norm)
    moe_in = (mid * scale * own_columns(moe_gain)).astype(bf16)

    rows_own = jnp.concatenate([*gather_chips(moe_in[:tok]), moe_in[tok:]], axis=0)
    own = [rows_own] + [swap(rows_own, "head", o) for o in range(1, head_count)]
    other = [swap(chunk, "blk", 1) for chunk in own]
    keep, send = run_experts(own, other, gates_own, gates_other, w_gate, w_up, w_down, head_scalar)
    summed = [
        (a.astype(f32) + swap(b, "blk", 1).astype(f32)).astype(bf16) for a, b in zip(keep, send)
    ]
    summed = [summed[0]] + [swap(summed[o], "head", o) for o in range(1, head_count)]
    half = tok * chips
    merged = tree_sum([s.astype(f32) for s in summed]).astype(bf16)
    final = [
        jnp.concatenate([merged[o * tok : (o + 1) * tok], merged[half:]], axis=0) for o in range(chips)
    ]
    final = [final[0]] + [swap(final[o], "blk", 2 * o) for o in range(1, chips)]
    hidden = (mid + tree_sum([s.astype(f32) for s in final])).astype(bf16)
    return (hidden[:tok], hidden[tok : tok + DEC], new_cache, dec_cache)


def solution(mesh):
    placed = (
        P("blk", None),
        P(),
        P(),
        P(None, "head"),
        P(None, "head"),
        P(None, "head"),
        P("head", None),
        P("blk", None, "head"),
        P("blk", None, "head"),
        P("blk"),
        P("blk"),
        P(),
        P(),
        P("blk", None),
        P("blk", None),
        P(),
        P(),
        P("blk", None, "head"),
        P("blk", None, "head"),
        P("blk", "head", None),
    )
    return jax.shard_map(
        per_device,
        mesh=mesh,
        in_specs=placed,
        out_specs=(
            P("blk", "head"),
            P(None, "head"),
            P(None, "blk", "head"),
            P(None, None, "head"),
        ),
        check_vma=False,
    )
```

```python
import functools

import jax
import jax.numpy as jnp
from jax import lax
from jax.experimental import pallas as pl
from jax.experimental.pallas import tpu as pltpu
from jax.sharding import PartitionSpec as P

HD = 128
PRE = 1
DEC = 12
REQS = 13
DPAD = 16
TILE = 256

eps_norm = 1e-06
rope_base = 50000.0
neg_fill = -1e30
bf16 = jnp.bfloat16
f32 = jnp.float32


def swap(value, axis, mask):
    count = lax.axis_size(axis)
    return lax.ppermute(value, axis, [(i, i ^ mask) for i in range(count)])


def span(index, size):
    return pl.ds(pl.multiple_of(index * size, size), size)


def lanes(head):
    return slice(head * HD, (head + 1) * HD)


def tree_sum(values):
    values = list(values)
    while len(values) > 1:
        values = [a + b for a, b in zip(values[::2], values[1::2])]
    return values[0]


VMEM = pl.BlockSpec(memory_space=pltpu.VMEM)
SMEM = pl.BlockSpec(memory_space=pltpu.SMEM)
HBM = pl.BlockSpec(memory_space=pltpu.HBM)


def call(body, outs, ins, args, name, limit, scratch=(), cost=None):
    args = [
        pltpu.with_memory_space_constraint(arg, pltpu.HBM) if spec is HBM else arg
        for spec, arg in zip(ins, args)
    ]
    return pl.pallas_call(
        body,
        out_shape=tuple(jax.ShapeDtypeStruct(shape, dtype) for shape, dtype in outs),
        in_specs=list(ins),
        out_specs=tuple(VMEM for _ in outs),
        scratch_shapes=list(scratch),
        compiler_params=pltpu.CompilerParams(vmem_limit_bytes=limit << 20),
        cost_estimate=cost,
        name=name,
    )(*args)


def turn(flat, cosine, sine):
    heads = []
    for head in range(flat.shape[1] // HD):
        block = flat[:, lanes(head)]
        heads.append(block * cosine + pltpu.roll(block, HD // 2, 1) * sine)
    return jnp.concatenate(heads, axis=1).astype(bf16)


def gate_lanes(ids, gates, width):
    names = ids[...]
    values = gates[...].astype(f32)
    place = lax.broadcasted_iota(jnp.int32, (width, names.shape[1]), 0)
    table = jnp.zeros(place.shape, f32)
    for k in range(names.shape[0]):
        table = jnp.where(place == names[k : k + 1], values[k : k + 1], table)
    shape = (width, width)
    eye = lax.broadcasted_iota(jnp.int32, shape, 0) == lax.broadcasted_iota(jnp.int32, shape, 1)
    return lax.dot_general(
        table.astype(bf16),
        eye.astype(f32).astype(bf16),
        (((0,), (0,)), ((), ())),
        preferred_element_type=f32,
    ).astype(bf16)


def query_kernel(
    pre, dec, gain, weight_hbm, cosine, sine, ids, gates, dec_ids, dec_gates,
    message, query_d, table_d, normed, weight, sem,
):
    copy = pltpu.make_async_copy(weight_hbm, weight, sem)
    copy.start()
    tok = pre.shape[0]
    width = weight.shape[1]

    def norm(rows):
        values = rows.astype(f32)
        meansq = jnp.mean(values * values, axis=-1, keepdims=True)
        return (values * lax.rsqrt(meansq + eps_norm) * gain[...]).astype(bf16)

    normed[0:tok, :] = norm(pre[...])
    normed[tok:, :] = jnp.zeros_like(normed[tok:, :])
    normed[tok : tok + DEC, :] = norm(dec[...])
    message[:, width:] = gate_lanes(ids, gates, message.shape[1] - width)
    table_d[...] = jnp.zeros_like(table_d)
    table_d[0:DEC, :] = gate_lanes(dec_ids, dec_gates, table_d.shape[1])
    copy.wait()
    query = jnp.dot(normed[...], weight[...], preferred_element_type=f32)
    query = turn(query, cosine[...], sine[...])
    message[:, :width] = query[:tok]
    query_d[...] = query[tok:]


def key_kernel(
    normed, key_hbm, value_hbm, cosine, sine, new, dec, key_d, value_d, w_key, w_value, sems
):
    tok = new.shape[1]
    copies = [
        pltpu.make_async_copy(key_hbm, w_key, sems.at[0]),
        pltpu.make_async_copy(value_hbm, w_value, sems.at[1]),
    ]
    for copy in copies:
        copy.start()
    for copy in copies:
        copy.wait()
    key = turn(jnp.dot(normed[...], w_key[...], preferred_element_type=f32), cosine[...], sine[...])
    value = jnp.dot(normed[...], w_value[...], preferred_element_type=f32).astype(bf16)
    for index, (rows, padded) in enumerate(((key, key_d), (value, value_d))):
        new[index] = rows[:tok]
        dec[index] = rows[tok : tok + DEC]
        padded[...] = rows[tok:]


def group(query, keys, values, live):
    scores = lax.dot_general(
        query, keys, (((1,), (1,)), ((), ())), preferred_element_type=f32
    ) * HD ** (-0.5)
    top = jnp.max(jnp.where(live, scores, neg_fill), axis=-1, keepdims=True)
    weights = jnp.where(live, jnp.exp(scores - top), 0.0)
    total = jnp.sum(weights, axis=-1, keepdims=True)
    acc = jnp.dot(weights.astype(bf16), values, preferred_element_type=f32)
    return top, total, acc


def group_turned(query, keys, values, live):
    scores = lax.dot_general(
        keys, query, (((1,), (1,)), ((), ())), preferred_element_type=f32
    ) * HD ** (-0.5)
    top = jnp.max(
        scores if live is None else jnp.where(live, scores, neg_fill), axis=0, keepdims=True
    )
    weights = jnp.exp(scores - top)
    if live is not None:
        weights = jnp.where(live, weights, 0.0)
    total = jnp.sum(weights, axis=0, keepdims=True)
    acc = lax.dot_general(
        values, weights.astype(bf16), (((0,), (0,)), ((), ())), preferred_element_type=f32
    )
    return top, total, acc


def attention_kernel(
    owner_ref, slot_ref, lens_ref, blk_ref, query_a, query_b, query_d, new, key_dec, value_dec,
    cache_k, cache_v, keep, send, dec, key_buf, value_buf, tops, totals, sems,
):
    blocks, block_len, width = cache_k.shape
    heads = width // HD
    half = query_a.shape[0]
    tile = min(TILE, half)
    sides = ((query_a, keep), (query_b, send))

    def copies(index):
        return (
            pltpu.make_async_copy(cache_k.at[index], key_buf.at[index], sems.at[0, index]),
            pltpu.make_async_copy(cache_v.at[index], value_buf.at[index], sems.at[1, index]),
        )

    for index in range(blocks):
        for copy in copies(index):
            copy.start()

    def over_tiles(body):
        for query, state in sides:
            for row in range(0, half, tile):
                for head in range(heads):
                    body(query[row : row + tile, lanes(head)], state, slice(row, row + tile), head)

    def start(query, state, columns, head):
        top, total, acc = group_turned(query, new[0, :, lanes(head)], new[1, :, lanes(head)], None)
        state[width + head : width + head + 1, columns] = top
        state[width + heads + head : width + heads + head + 1, columns] = total
        state[lanes(head), columns] = acc

    over_tiles(start)
    mine = blk_ref[0] == 0
    for head in range(heads):
        own = jnp.sum(
            query_d[:, lanes(head)].astype(f32) * key_dec[:, lanes(head)].astype(f32),
            axis=-1,
            keepdims=True,
        ) * HD ** (-0.5)
        tops[head] = jnp.where(mine, own, neg_fill)
        totals[head] = jnp.where(mine, jnp.ones_like(own), jnp.zeros_like(own))
        dec[:, lanes(head)] = jnp.where(mine, value_dec[:, lanes(head)].astype(f32), 0.0)

    @pl.loop(0, blocks)
    def _(index):
        for copy in copies(index):
            copy.wait()
        owner = owner_ref[index]
        length = lens_ref[jnp.minimum(owner, REQS - 1)]
        count = jnp.clip(length - slot_ref[index] * block_len, 0, block_len)

        def add(live, query, state, columns, head):
            top, total, acc = group_turned(
                query, key_buf[index, :, lanes(head)], value_buf[index, :, lanes(head)], live
            )
            top_row = slice(width + head, width + head + 1)
            total_row = slice(width + heads + head, width + heads + head + 1)
            old_top = state[top_row, columns]
            best = jnp.maximum(old_top, top)
            old_scale = jnp.exp(old_top - best)
            scale = jnp.exp(top - best)
            state[top_row, columns] = best
            state[total_row, columns] = state[total_row, columns] * old_scale + total * scale
            state[lanes(head), columns] = state[lanes(head), columns] * old_scale + acc * scale

        @pl.when((owner < PRE) & (count == block_len))
        def _():
            over_tiles(functools.partial(add, None))

        @pl.when((owner < PRE) & (count < block_len))
        def _():
            live = lax.broadcasted_iota(jnp.int32, (block_len, tile), 0) < count
            over_tiles(functools.partial(add, live))

        @pl.when((owner >= PRE) & (owner < REQS))
        def _():
            shape = (DPAD, block_len)
            live = (lax.broadcasted_iota(jnp.int32, shape, 1) < count) & (
                lax.broadcasted_iota(jnp.int32, shape, 0) == owner - PRE
            )
            for head in range(heads):
                top, total, acc = group(
                    query_d[:, lanes(head)],
                    key_buf[index, :, lanes(head)],
                    value_buf[index, :, lanes(head)],
                    live,
                )
                old_top = tops[head]
                best = jnp.maximum(old_top, top)
                old_scale = jnp.exp(old_top - best)
                scale = jnp.exp(top - best)
                tops[head] = best
                totals[head] = totals[head] * old_scale + total * scale
                dec[:, lanes(head)] = dec[:, lanes(head)] * old_scale + acc * scale

    place = lax.broadcasted_iota(jnp.int32, (DPAD, HD), 1)
    packed = jnp.zeros((DPAD, HD), f32)
    for head in range(heads):
        packed = jnp.where(place == head, tops[head], packed)
        packed = jnp.where(place == heads + head, totals[head], packed)
    dec[:, width:] = packed


def attention(query_a, query_b, query_d, new, key_d, value_d, cache_keys, cache_values, scalars):
    half = query_a.shape[0]
    blocks, block_len, width = cache_keys.shape
    heads = width // HD
    state = ((width + 2 * heads, half), f32)
    return call(
        attention_kernel,
        (state, state, ((DPAD, width + HD), f32)),
        [SMEM] * 4 + [VMEM] * 6 + [HBM] * 2,
        (*scalars, query_a, query_b, query_d, new, key_d, value_d, cache_keys, cache_values),
        "attention",
        24,
        [
            pltpu.VMEM((blocks, block_len, width), bf16),
            pltpu.VMEM((blocks, block_len, width), bf16),
            pltpu.VMEM((heads, DPAD, 1), f32),
            pltpu.VMEM((heads, DPAD, 1), f32),
            pltpu.SemaphoreType.DMA((2, blocks)),
        ],
    )


def split(values):
    high = values.astype(bf16).astype(f32)
    middle = (values - high).astype(bf16).astype(f32)
    return high, middle, (values - high) - middle


def merge_core_kernel(mine, other, dec_mine, dec_other, *outs):
    full = dec_mine.shape[1]
    width = full - HD
    heads = width // HD
    half = mine.shape[1]
    tok = half // len(outs)

    def put(where, turned, dec):
        value = turned.T.astype(bf16)
        for index, out in enumerate(outs):
            out[0:tok, where] = value[index * tok : (index + 1) * tok]
            out[tok : tok + DPAD, where] = dec.astype(bf16)

    place = lax.broadcasted_iota(jnp.int32, (DPAD, HD), 1)
    packed = jnp.zeros((DPAD, HD), f32)
    stats_a = dec_mine[:, width:]
    stats_b = dec_other[:, width:]
    top_rows = slice(width, width + heads)
    total_rows = slice(width + heads, width + 2 * heads)
    best = jnp.maximum(mine[top_rows, :], other[top_rows, :])
    scale_a = jnp.exp(mine[top_rows, :] - best)
    scale_b = jnp.exp(other[top_rows, :] - best)
    total = mine[total_rows, :] * scale_a + other[total_rows, :] * scale_b
    for head in range(heads):
        one = slice(head, head + 1)
        two = slice(heads + head, heads + head + 1)
        turned = mine[lanes(head), :] * scale_a[one] + other[lanes(head), :] * scale_b[one]
        dec_best = jnp.maximum(stats_a[:, one], stats_b[:, one])
        dec_a = jnp.exp(stats_a[:, one] - dec_best)
        dec_b = jnp.exp(stats_b[:, one] - dec_best)
        packed = jnp.where(place == head, dec_best, packed)
        packed = jnp.where(place == heads + head, stats_a[:, two] * dec_a + stats_b[:, two] * dec_b, packed)
        put(lanes(head), turned, dec_mine[:, lanes(head)] * dec_a + dec_other[:, lanes(head)] * dec_b)
    coded = [*split(jnp.concatenate([best, total], axis=0))]
    coded.append(jnp.zeros((HD - 6 * heads, half), f32))
    high, middle, low = split(packed)
    put(
        slice(width, full),
        jnp.concatenate(coded, axis=0),
        high + pltpu.roll(middle, 2 * heads, 1) + pltpu.roll(low, 4 * heads, 1),
    )


def merge_core(mine, other, dec_mine, dec_other, parts):
    full = dec_mine.shape[1]
    tok = mine.shape[1] // parts
    return call(
        merge_core_kernel,
        (((tok + DPAD, full), bf16),) * parts,
        [VMEM] * 4,
        (mine, other, dec_mine, dec_other),
        "merge_core",
        12,
    )


def project_kernel(parts, head_ref, *refs):
    pieces = refs[:parts]
    weight_hbm = refs[parts]
    weight, sem = refs[-2:]
    outs = refs[parts + 1 : -2]
    copy = pltpu.make_async_copy(weight_hbm, weight, sem)
    copy.start()
    rows, full = pieces[0].shape
    width = full - HD
    heads = width // HD
    columns = outs[0].shape[1]
    stats = []
    for piece in pieces:
        coded = piece[:, width:].astype(f32)
        stats.append(
            (coded + pltpu.roll(coded, HD - 2 * heads, 1)) + pltpu.roll(coded, HD - 4 * heads, 1)
        )
    attended = []
    for head in range(heads):
        tops = [s[:, head : head + 1] for s in stats]
        best = functools.reduce(jnp.maximum, tops)
        scales = [jnp.exp(top - best) for top in tops]
        total = tree_sum([s[:, heads + head : heads + head + 1] * c for s, c in zip(stats, scales)])
        acc = tree_sum([piece[:, lanes(head)].astype(f32) * c for piece, c in zip(pieces, scales)])
        attended.append((acc / total).astype(bf16))
    attended = jnp.concatenate(attended, axis=1)
    copy.wait()
    for offset, out in enumerate(outs):
        place = lax.bitwise_xor(head_ref[0], offset)
        out[...] = jnp.dot(attended, weight[:, span(place, columns)], preferred_element_type=f32)


def project_out(pieces, w_output, head_index, head_count):
    rows = pieces[0].shape[0]
    columns = w_output.shape[1] // head_count
    return call(
        functools.partial(project_kernel, len(pieces)),
        (((rows, columns), f32),) * head_count,
        [SMEM] + [VMEM] * len(pieces) + [HBM],
        (head_index, *pieces, w_output),
        "project_out",
        12,
        [pltpu.VMEM(w_output.shape, bf16), pltpu.SemaphoreType.DMA],
    )


def mid_kernel(head_ref, pre, dec, *refs):
    parts, (mid, square) = refs[:-2], refs[-2:]
    tok, width = pre.shape[0], mid.shape[1]
    here = span(head_ref[0], width)
    total = tree_sum([part[...] for part in parts])
    mid[0:tok, :] = pre[:, here].astype(f32) + total[:tok]
    mid[tok : tok + DEC, :] = dec[:, here].astype(f32) + total[tok : tok + DEC]
    mid[tok + DEC :, :] = jnp.zeros_like(mid[tok + DEC :, :])
    values = mid[...]
    values = values * values
    square[...] = tree_sum([values[:, lanes(part)] for part in range(width // HD)])


def norm_kernel(model_width, head_ref, mid, gain, *refs):
    squares, (tokens, dec) = refs[:-2], refs[-2:]
    tok, width = tokens.shape
    total = jnp.sum(tree_sum([square[...] for square in squares]), axis=-1, keepdims=True)
    scaled = mid[...] * lax.rsqrt(total / model_width + eps_norm) * gain[:, span(head_ref[0], width)]
    scaled = scaled.astype(bf16)
    tokens[...] = scaled[:tok]
    dec[...] = scaled[tok:]


def experts_kernel(chunks, scalar_ref, *refs):
    data = refs[:chunks]
    query, table_d = refs[chunks : chunks + 2]
    table = query.at[:, query.shape[1] - table_d.shape[1] :]
    hbm = refs[chunks + 2 : chunks + 8]
    outs = refs[chunks + 8 : 2 * chunks + 8]
    bufs = refs[2 * chunks + 8 : 2 * chunks + 11]
    gates, first, second, sems = refs[2 * chunks + 11 :]
    each = hbm[0].shape[0]
    experts = 2 * each
    rows, width = data[0].shape
    half = rows - DPAD
    tile = min(TILE, half)
    places = [lax.bitwise_xor(scalar_ref[0], offset) for offset in range(chunks)]

    def copies(expert):
        source = hbm[:3] if expert < each else hbm[3:]
        return [
            pltpu.make_async_copy(src.at[expert % each], buf.at[expert], sems.at[kind, expert])
            for kind, (src, buf) in enumerate(zip(source, bufs))
        ]

    for expert in range(experts):
        for copy in copies(expert):
            copy.start()
    w_gate, w_up, w_down = bufs
    for expert in range(experts):
        number = lax.bitwise_xor(scalar_ref[1], expert // each) * each + expert % each
        for ref, row in ((table, 0), (table_d, half)):
            place = lax.broadcasted_iota(jnp.int32, ref.shape, 1)
            found = jnp.where(place == number, ref[...].astype(f32), 0.0)
            gates[expert, row : row + ref.shape[0], :] = jnp.sum(found, axis=-1, keepdims=True)
    for expert in range(experts):
        for copy in copies(expert):
            copy.wait()
        total = first if expert < each else second
        for row in range(0, half, tile):
            size = tile + (DPAD if row + tile == half else 0)
            gate = up = None
            for part, place in zip(data, places):
                block = part[row : row + size, :]
                g = jnp.dot(block, w_gate[expert, span(place, width), :], preferred_element_type=f32)
                u = jnp.dot(block, w_up[expert, span(place, width), :], preferred_element_type=f32)
                gate = g if gate is None else gate + g
                up = u if up is None else up + u
            act = (gate / (1.0 + jnp.exp(-gate)) * up).astype(bf16)
            factor = gates[expert, row : row + size, :]
            for index, place in enumerate(places):
                down = jnp.dot(act, w_down[expert, :, span(place, width)], preferred_element_type=f32)
                down = down.astype(bf16).astype(f32) * factor
                if expert % each:
                    down = total[index, row : row + size, :] + down
                if expert == experts - 1:
                    down = first[index, row : row + size, :] + down
                    outs[index][row : row + size, :] = down.astype(bf16)
                else:
                    total[index, row : row + size, :] = down


def run_experts(data, query, table_d, own, other, scalars):
    chunks = len(data)
    rows, width = data[0].shape
    experts = 2 * own[0].shape[0]
    return call(
        functools.partial(experts_kernel, chunks),
        (((rows, width), bf16),) * chunks,
        [SMEM] + [VMEM] * (chunks + 2) + [HBM] * 6,
        (scalars, *data, query, table_d, *own, *other),
        "experts",
        32,
        [pltpu.VMEM((experts, *w.shape[1:]), bf16) for w in own]
        + [
            pltpu.VMEM((experts, rows, 1), f32),
            pltpu.VMEM((chunks, rows, width), f32),
            pltpu.VMEM((chunks, rows, width), f32),
            pltpu.SemaphoreType.DMA((3, experts)),
        ],
    )


def head_sum_kernel(parts, *refs):
    total = tree_sum([ref[...].astype(f32) for ref in refs[:parts]]).astype(bf16)
    outs = refs[parts:]
    half = total.shape[0] - DPAD
    tok = half // len(outs)
    for index, out in enumerate(outs):
        out[0:tok, :] = total[index * tok : (index + 1) * tok]
        out[tok:, :] = total[half:]


def final_kernel(mid, *refs):
    parts, (hidden, dec) = refs[:-2], refs[-2:]
    tok = hidden.shape[0]
    total = mid[...] + tree_sum([part[...].astype(f32) for part in parts])
    hidden[...] = total[:tok].astype(bf16)
    dec[...] = total[tok : tok + DEC].astype(bf16)


def per_device(
    pre_tokens, dec_tokens, attn_gain, w_query, w_key, w_value, w_output, cache_keys, cache_values,
    block_request, block_slot, cache_lens, moe_gain, expert_ids, expert_gates, dec_expert_ids,
    dec_expert_gates, w_gate, w_up, w_down,
):
    tok, model_width = pre_tokens.shape
    width = w_query.shape[1]
    blk_count = lax.axis_size("blk")
    blk_index = lax.axis_index("blk").astype(jnp.int32)
    head_count = lax.axis_size("head")
    head_index = lax.axis_index("head").astype(jnp.int32)
    chips = blk_count // 2
    head_scalar = head_index.reshape(1)
    scalars = jnp.stack([head_index, blk_index])
    part_width = model_width // head_count
    tables = -(-w_gate.shape[0] * blk_count // HD) * HD
    rows = tok + DPAD

    row = jnp.arange(rows, dtype=jnp.int32)
    request = jnp.maximum(row - tok + PRE, 0)[:, None] == jnp.arange(REQS, dtype=jnp.int32)
    positions = jnp.sum(jnp.where(request, cache_lens, 0), axis=1)
    positions = positions + jnp.where(row < tok, blk_index * tok + row, 0)
    frequencies = rope_base ** (-jnp.arange(HD // 2, dtype=f32) / (HD // 2))
    angles = positions.astype(f32)[:, None] * frequencies[None, :]
    cosine = jnp.cos(angles)
    sine = jnp.sin(angles)
    cosine = jnp.concatenate([cosine, cosine], axis=1)
    sine = jnp.concatenate([-sine, sine], axis=1)

    message, query_d, table_d, normed = call(
        query_kernel,
        (
            ((tok, width + tables), bf16),
            ((DPAD, width), bf16),
            ((DPAD, tables), bf16),
            ((rows, model_width), bf16),
        ),
        [VMEM] * 3 + [HBM] + [VMEM] * 6,
        (
            pre_tokens, dec_tokens, attn_gain[None, :], w_query, cosine, sine,
            expert_ids.T, expert_gates.T, dec_expert_ids.T, dec_expert_gates.T,
        ),
        "queries",
        16,
        [pltpu.VMEM(w_query.shape, bf16), pltpu.SemaphoreType.DMA],
    )

    def exchange(pieces, axis, step):
        return [pieces[0]] + [swap(pieces[o], axis, step * o) for o in range(1, len(pieces))]

    new_cache, dec_cache, key_d, value_d = call(
        key_kernel,
        (
            ((2, tok, width), bf16),
            ((2, DEC, width), bf16),
            ((DPAD, width), bf16),
            ((DPAD, width), bf16),
        ),
        [VMEM] + [HBM] * 2 + [VMEM] * 2,
        (normed, w_key, w_value, cosine, sine),
        "keys",
        16,
        [
            pltpu.VMEM(w_key.shape, bf16),
            pltpu.VMEM(w_value.shape, bf16),
            pltpu.SemaphoreType.DMA((2,)),
        ],
        pl.CostEstimate(
            flops=4 * rows * model_width * width,
            transcendentals=0,
            bytes_accessed=4 * model_width * width,
        ),
    )
    gate_other = swap(w_gate, "blk", 1)
    pieces = exchange([message] * chips, "blk", 2)
    new_cache, *pieces = lax.optimization_barrier((new_cache, *pieces))
    query_a = jnp.concatenate(pieces, axis=0)
    query_b = swap(query_a, "blk", 1)
    query_b, gate_other, up_source = lax.optimization_barrier((query_b, gate_other, w_up))
    up_other = swap(up_source, "blk", 1)

    keep, send, dec = attention(
        query_a, query_b, query_d, new_cache, key_d, value_d, cache_keys, cache_values,
        (block_request, block_slot, cache_lens, blk_index.reshape(1)),
    )
    send, up_other = lax.optimization_barrier((send, up_other))
    pieces = merge_core(keep, swap(send, "blk", 1), dec, swap(dec, "blk", 1), chips)
    *pieces, down_source = lax.optimization_barrier((*pieces, w_down))
    down_other = swap(down_source, "blk", 1)
    pieces = exchange(pieces, "blk", 2)
    partial = exchange(project_out(pieces, w_output, head_scalar, head_count), "head", 1)
    mid, square = call(
        mid_kernel,
        (((rows, part_width), f32), ((rows, HD), f32)),
        [SMEM] + [VMEM] * (2 + head_count),
        (head_scalar, pre_tokens, dec_tokens, *partial),
        "mid",
        8,
    )
    squares = exchange([square] * head_count, "head", 1)
    moe_tok, moe_dec = call(
        functools.partial(norm_kernel, model_width),
        (((tok, part_width), bf16), ((DPAD, part_width), bf16)),
        [SMEM] + [VMEM] * (2 + head_count),
        (head_scalar, mid, moe_gain[None, :], *squares),
        "moe_norm",
        8,
    )
    gathered = jnp.concatenate([*exchange([moe_tok] * chips, "blk", 2), moe_dec], axis=0)
    data = exchange([gathered] * head_count, "head", 1)
    results = run_experts(
        data, query_a, table_d, (w_gate, w_up, w_down), (gate_other, up_other, down_other), scalars
    )
    results = exchange(results, "head", 1)
    final = call(
        functools.partial(head_sum_kernel, head_count),
        (((rows, part_width), bf16),) * chips,
        [VMEM] * head_count,
        results,
        "head_sum",
        8,
    )
    final = exchange(final, "blk", 2)
    hidden, dec_hidden = call(
        final_kernel,
        (((tok, part_width), bf16), ((DEC, part_width), bf16)),
        [VMEM] * (1 + chips),
        (mid, *final),
        "final",
        8,
    )
    return (hidden, dec_hidden, new_cache, dec_cache)


def solution(mesh):
    placed = (
        P("blk", None),
        P(),
        P(),
        P(None, "head"),
        P(None, "head"),
        P(None, "head"),
        P("head", None),
        P("blk", None, "head"),
        P("blk", None, "head"),
        P("blk"),
        P("blk"),
        P(),
        P(),
        P("blk", None),
        P("blk", None),
        P(),
        P(),
        P("blk", None, "head"),
        P("blk", None, "head"),
        P("blk", "head", None),
    )
    return jax.shard_map(
        per_device,
        mesh=mesh,
        in_specs=placed,
        out_specs=(
            P("blk", "head"),
            P(None, "head"),
            P(None, "blk", "head"),
            P(None, None, "head"),
        ),
        check_vma=False,
    )
```

```python
import functools

import jax
import jax.numpy as jnp
from jax import lax
from jax.experimental import pallas as pl
from jax.experimental.pallas import tpu as pltpu
from jax.sharding import PartitionSpec as P

HD = 128
PRE = 1
DEC = 12
REQS = 13
DPAD = 16
TILE = 256

eps_norm = 1e-06
rope_base = 50000.0
neg_fill = -1e30
LOG2E = 1.4426950408889634
bf16 = jnp.bfloat16
f32 = jnp.float32


def swap(value, axis, mask):
    count = lax.axis_size(axis)
    return lax.ppermute(value, axis, [(i, i ^ mask) for i in range(count)])


def span(index, size):
    return pl.ds(pl.multiple_of(index * size, size), size)


def lanes(head):
    return slice(head * HD, (head + 1) * HD)


def tree_sum(values):
    values = list(values)
    while len(values) > 1:
        values = [a + b for a, b in zip(values[::2], values[1::2])]
    return values[0]


VMEM = pl.BlockSpec(memory_space=pltpu.VMEM)
SMEM = pl.BlockSpec(memory_space=pltpu.SMEM)
HBM = pl.BlockSpec(memory_space=pltpu.HBM)


def call(body, outs, ins, args, name, limit, scratch=(), cost=None):
    args = [
        pltpu.with_memory_space_constraint(arg, pltpu.HBM) if spec is HBM else arg
        for spec, arg in zip(ins, args)
    ]
    return pl.pallas_call(
        body,
        out_shape=tuple(jax.ShapeDtypeStruct(shape, dtype) for shape, dtype in outs),
        in_specs=list(ins),
        out_specs=tuple(VMEM for _ in outs),
        scratch_shapes=list(scratch),
        compiler_params=pltpu.CompilerParams(vmem_limit_bytes=limit << 20),
        cost_estimate=cost,
        name=name,
    )(*args)


def turn(flat, cosine, sine):
    heads = []
    for head in range(flat.shape[1] // HD):
        block = flat[:, lanes(head)]
        heads.append(block * cosine + pltpu.roll(block, HD // 2, 1) * sine)
    return jnp.concatenate(heads, axis=1).astype(bf16)


def gate_lanes(ids, gates, width):
    names = ids[...]
    values = gates[...].astype(f32)
    place = lax.broadcasted_iota(jnp.int32, (width, names.shape[1]), 0)
    table = jnp.zeros(place.shape, f32)
    for k in range(names.shape[0]):
        table = jnp.where(place == names[k : k + 1], values[k : k + 1], table)
    shape = (width, width)
    eye = lax.broadcasted_iota(jnp.int32, shape, 0) == lax.broadcasted_iota(jnp.int32, shape, 1)
    return lax.dot_general(
        table.astype(bf16),
        eye.astype(f32).astype(bf16),
        (((0,), (0,)), ((), ())),
        preferred_element_type=f32,
    )


def query_kernel(
    pre_hbm, dec_hbm, gain_hbm, weight_hbm, ids_hbm, gates_hbm, dec_ids_hbm, dec_gates_hbm, cosine, sine,
    message, query_d, table_d, normed, dec_pad,
    pre, dec, gain, weight, ids, gates, dec_ids, dec_gates, rows, sems,
):
    sources = (pre_hbm, dec_hbm, gain_hbm, ids_hbm, gates_hbm, dec_ids_hbm, dec_gates_hbm)
    targets = (pre, dec, gain, ids, gates, dec_ids, dec_gates)
    copies = [
        pltpu.make_async_copy(source, target, sems.at[index])
        for index, (source, target) in enumerate(zip(sources, targets))
    ]
    depth = weight.shape[0] // 4
    for part in range(4):
        here = pl.ds(part * depth, depth)
        copies.append(
            pltpu.make_async_copy(weight_hbm.at[here], weight.at[here], sems.at[len(sources) + part])
        )
    for copy in copies:
        copy.start()
    tok = pre.shape[0]
    width = weight.shape[1]
    heads = dec_pad.shape[0] // 8
    share = DEC // heads
    for copy in copies[:7]:
        copy.wait()

    def norm(values):
        meansq = jnp.mean(values * values, axis=-1, keepdims=True)
        return (values * lax.rsqrt(meansq + eps_norm) * gain[...]).astype(bf16)

    dec_rows = dec[...].astype(f32)
    normed[0:tok, :] = norm(pre[...].astype(f32))
    normed[tok:, :] = jnp.zeros_like(normed[tok:, :])
    normed[tok : tok + DEC, :] = norm(dec_rows)
    dec_table = gate_lanes(dec_ids, dec_gates, table_d.shape[1])
    message[:, width:] = gate_lanes(ids, gates, message.shape[1] - width).astype(bf16)
    for out, source in ((dec_pad, dec_rows), (table_d, dec_table)):
        rows[...] = jnp.zeros_like(rows)
        for head in range(heads):
            rows[8 * head : 8 * head + share, : source.shape[1]] = source[share * head : share * (head + 1)]
        out[...] = rows[:, : source.shape[1]].astype(out.dtype)
    for copy in copies[7:]:
        copy.wait()
    query = jnp.dot(normed[...], weight[...], preferred_element_type=f32)
    query = turn(query, cosine[...], sine[...])
    message[:, :width] = query[:tok]
    query_d[...] = query[tok:]


def key_kernel(
    normed, key_hbm, value_hbm, cosine, sine, new, dec, key_n, value_n, key_d, value_d, w_key, w_value, sems
):
    tok = new.shape[1]
    copies = [
        pltpu.make_async_copy(key_hbm, w_key, sems.at[0]),
        pltpu.make_async_copy(value_hbm, w_value, sems.at[1]),
    ]
    for copy in copies:
        copy.start()
    for copy in copies:
        copy.wait()
    key = turn(jnp.dot(normed[...], w_key[...], preferred_element_type=f32), cosine[...], sine[...])
    value = jnp.dot(normed[...], w_value[...], preferred_element_type=f32).astype(bf16)
    for index, (rows, plain, padded) in enumerate(((key, key_n, key_d), (value, value_n, value_d))):
        new[index] = rows[:tok]
        plain[...] = rows[:tok]
        dec[index] = rows[tok : tok + DEC]
        padded[...] = rows[tok:]


def group(query, keys, values, live):
    scores = lax.dot_general(
        query, keys, (((1,), (1,)), ((), ())), preferred_element_type=f32
    ) * HD ** (-0.5)
    top = jnp.max(jnp.where(live, scores, neg_fill), axis=-1, keepdims=True)
    weights = jnp.where(live, jnp.exp(scores - top), 0.0)
    total = jnp.sum(weights, axis=-1, keepdims=True)
    acc = jnp.dot(weights.astype(bf16), values, preferred_element_type=f32)
    return top, total, acc


def group_turned(query, keys, values, live):
    scores = lax.dot_general(
        keys, query, (((1,), (1,)), ((), ())), preferred_element_type=f32
    )
    top = jnp.max(
        scores if live is None else jnp.where(live, scores, neg_fill), axis=0, keepdims=True
    )
    weights = jnp.exp2((scores - top) * (HD ** (-0.5) * LOG2E))
    top = top * HD ** (-0.5)
    if live is not None:
        weights = jnp.where(live, weights, 0.0)
    total = jnp.sum(weights, axis=0, keepdims=True)
    acc = lax.dot_general(
        values, weights.astype(bf16), (((0,), (0,)), ((), ())), preferred_element_type=f32
    )
    return top, total, acc


def attention_kernel(
    owner_ref, slot_ref, lens_ref, blk_ref, query_a, query_b, query_d, key_new, value_new, key_dec, value_dec,
    cache_k, cache_v, keep, send, dec, key_buf, value_buf, tops, totals, sems,
):
    blocks, block_len, width = cache_k.shape
    heads = width // HD
    half = query_a.shape[0]
    tile = min(TILE, half)
    sides = ((query_a, keep), (query_b, send))

    def copies(index):
        return (
            pltpu.make_async_copy(cache_k.at[index], key_buf.at[index], sems.at[0, index]),
            pltpu.make_async_copy(cache_v.at[index], value_buf.at[index], sems.at[1, index]),
        )

    for index in range(blocks):
        for copy in copies(index):
            copy.start()

    def over_tiles(body):
        for query, state in sides:
            for row in range(0, half, tile):
                for head in range(heads):
                    body(query[row : row + tile, lanes(head)], state, slice(row, row + tile), head)

    def start(query, state, columns, head):
        top, total, acc = group_turned(query, key_new[:, lanes(head)], value_new[:, lanes(head)], None)
        state[width + head : width + head + 1, columns] = top
        state[width + heads + head : width + heads + head + 1, columns] = total
        state[lanes(head), columns] = acc

    over_tiles(start)
    mine = blk_ref[0] == 0
    for head in range(heads):
        own = jnp.sum(
            query_d[:, lanes(head)].astype(f32) * key_dec[:, lanes(head)].astype(f32),
            axis=-1,
            keepdims=True,
        ) * HD ** (-0.5)
        tops[head] = jnp.where(mine, own, neg_fill)
        totals[head] = jnp.where(mine, jnp.ones_like(own), jnp.zeros_like(own))
        dec[:, lanes(head)] = jnp.where(mine, value_dec[:, lanes(head)].astype(f32), 0.0)

    @pl.loop(0, blocks)
    def _(index):
        for copy in copies(index):
            copy.wait()
        owner = owner_ref[index]
        length = lens_ref[jnp.minimum(owner, REQS - 1)]
        count = jnp.clip(length - slot_ref[index] * block_len, 0, block_len)

        def add(live, query, state, columns, head):
            top, total, acc = group_turned(
                query, key_buf[index, :, lanes(head)], value_buf[index, :, lanes(head)], live
            )
            top_row = slice(width + head, width + head + 1)
            total_row = slice(width + heads + head, width + heads + head + 1)
            old_top = state[top_row, columns]
            best = jnp.maximum(old_top, top)
            old_scale = jnp.exp(old_top - best)
            scale = jnp.exp(top - best)
            state[top_row, columns] = best
            state[total_row, columns] = state[total_row, columns] * old_scale + total * scale
            state[lanes(head), columns] = state[lanes(head), columns] * old_scale + acc * scale

        @pl.when((owner < PRE) & (count == block_len))
        def _():
            over_tiles(functools.partial(add, None))

        @pl.when((owner < PRE) & (count < block_len))
        def _():
            live = lax.broadcasted_iota(jnp.int32, (block_len, tile), 0) < count
            over_tiles(functools.partial(add, live))

        @pl.when((owner >= PRE) & (owner < REQS))
        def _():
            shape = (DPAD, block_len)
            live = (lax.broadcasted_iota(jnp.int32, shape, 1) < count) & (
                lax.broadcasted_iota(jnp.int32, shape, 0) == owner - PRE
            )
            for head in range(heads):
                top, total, acc = group(
                    query_d[:, lanes(head)],
                    key_buf[index, :, lanes(head)],
                    value_buf[index, :, lanes(head)],
                    live,
                )
                old_top = tops[head]
                best = jnp.maximum(old_top, top)
                old_scale = jnp.exp(old_top - best)
                scale = jnp.exp(top - best)
                tops[head] = best
                totals[head] = totals[head] * old_scale + total * scale
                dec[:, lanes(head)] = dec[:, lanes(head)] * old_scale + acc * scale

    place = lax.broadcasted_iota(jnp.int32, (DPAD, HD), 1)
    packed = jnp.zeros((DPAD, HD), f32)
    for head in range(heads):
        packed = jnp.where(place == head, tops[head], packed)
        packed = jnp.where(place == heads + head, totals[head], packed)
    dec[:, width:] = packed


def attention(query_a, query_b, query_d, new, cache_keys, cache_values, scalars):
    half = query_a.shape[0]
    blocks, block_len, width = cache_keys.shape
    heads = width // HD
    state = ((width + 2 * heads, half), f32)
    return call(
        attention_kernel,
        (state, state, ((DPAD, width + HD), f32)),
        [SMEM] * 4 + [VMEM] * 7 + [HBM] * 2,
        (*scalars, query_a, query_b, query_d, *new, cache_keys, cache_values),
        "attention",
        24,
        [
            pltpu.VMEM((blocks, block_len, width), bf16),
            pltpu.VMEM((blocks, block_len, width), bf16),
            pltpu.VMEM((heads, DPAD, 1), f32),
            pltpu.VMEM((heads, DPAD, 1), f32),
            pltpu.SemaphoreType.DMA((2, blocks)),
        ],
    )


def split(values):
    high = values.astype(bf16).astype(f32)
    middle = (values - high).astype(bf16).astype(f32)
    return high, middle, (values - high) - middle


def merge_core_kernel(mine, other, dec_mine, dec_other, *outs):
    full = dec_mine.shape[1]
    width = full - HD
    heads = width // HD
    half = mine.shape[1]
    tok = half // len(outs)

    def put(where, turned, dec):
        value = turned.T.astype(bf16)
        for index, out in enumerate(outs):
            out[0:tok, where] = value[index * tok : (index + 1) * tok]
            out[tok : tok + DPAD, where] = dec.astype(bf16)

    place = lax.broadcasted_iota(jnp.int32, (DPAD, HD), 1)
    packed = jnp.zeros((DPAD, HD), f32)
    stats_a = dec_mine[:, width:]
    stats_b = dec_other[:, width:]
    top_rows = slice(width, width + heads)
    total_rows = slice(width + heads, width + 2 * heads)
    best = jnp.maximum(mine[top_rows, :], other[top_rows, :])
    scale_a = jnp.exp(mine[top_rows, :] - best)
    scale_b = jnp.exp(other[top_rows, :] - best)
    total = mine[total_rows, :] * scale_a + other[total_rows, :] * scale_b
    for head in range(heads):
        one = slice(head, head + 1)
        two = slice(heads + head, heads + head + 1)
        turned = mine[lanes(head), :] * scale_a[one] + other[lanes(head), :] * scale_b[one]
        dec_best = jnp.maximum(stats_a[:, one], stats_b[:, one])
        dec_a = jnp.exp(stats_a[:, one] - dec_best)
        dec_b = jnp.exp(stats_b[:, one] - dec_best)
        packed = jnp.where(place == head, dec_best, packed)
        packed = jnp.where(place == heads + head, stats_a[:, two] * dec_a + stats_b[:, two] * dec_b, packed)
        put(lanes(head), turned, dec_mine[:, lanes(head)] * dec_a + dec_other[:, lanes(head)] * dec_b)
    coded = [*split(jnp.concatenate([best, total], axis=0))]
    coded.append(jnp.zeros((HD - 6 * heads, half), f32))
    high, middle, low = split(packed)
    put(
        slice(width, full),
        jnp.concatenate(coded, axis=0),
        high + pltpu.roll(middle, 2 * heads, 1) + pltpu.roll(low, 4 * heads, 1),
    )


def merge_core(mine, other, dec_mine, dec_other, parts):
    full = dec_mine.shape[1]
    tok = mine.shape[1] // parts
    return call(
        merge_core_kernel,
        (((tok + DPAD, full), bf16),) * parts,
        [VMEM] * 4,
        (mine, other, dec_mine, dec_other),
        "merge_core",
        12,
    )


def load_kernel(count, *refs):
    sources, targets, sems = refs[:count], refs[count + 1 : -1], refs[-1]
    copies = []
    for source, target in zip(sources, targets):
        depth = source.shape[-2] // 4
        for lead in range(source.shape[0]) if len(source.shape) == 3 else (None,):
            for part in range(4):
                here = pl.ds(part * depth, depth)
                where = here if lead is None else (lead, here)
                copies.append(
                    pltpu.make_async_copy(source.at[where], target.at[where], sems.at[len(copies)])
                )
    for copy in copies:
        copy.start()
    for copy in copies:
        copy.wait()


def load(arrays, after, name):
    size = sum(arr.size for arr in arrays) * 2
    count = sum(4 * (arr.shape[0] if arr.ndim == 3 else 1) for arr in arrays)
    return call(
        functools.partial(load_kernel, len(arrays)),
        tuple((arr.shape, arr.dtype) for arr in arrays),
        [HBM] * len(arrays) + [VMEM],
        (*arrays, after),
        name,
        1,
        [pltpu.SemaphoreType.DMA((count,))],
        pl.CostEstimate(flops=0, transcendentals=0, bytes_accessed=2 * size),
    )


def project_kernel(parts, head_ref, *refs):
    pieces = refs[:parts]
    weight = refs[parts]
    outs = refs[parts + 1 : -2]
    arranged, product = refs[-2:]
    rows, full = pieces[0].shape
    width = full - HD
    heads = width // HD
    group_rows = outs[0].shape[0]
    places = len(outs)
    share = (rows - DPAD) // places
    dec_share = DEC // places
    stats = []
    for piece in pieces:
        coded = piece[:, width:].astype(f32)
        stats.append(
            (coded + pltpu.roll(coded, HD - 2 * heads, 1)) + pltpu.roll(coded, HD - 4 * heads, 1)
        )
    arranged[...] = jnp.zeros_like(arranged)
    for head in range(heads):
        tops = [s[:, head : head + 1] for s in stats]
        best = functools.reduce(jnp.maximum, tops)
        scales = [jnp.exp(top - best) for top in tops]
        total = tree_sum([s[:, heads + head : heads + head + 1] * c for s, c in zip(stats, scales)])
        acc = tree_sum([piece[:, lanes(head)].astype(f32) * c for piece, c in zip(pieces, scales)])
        attended = acc / total
        for place in range(places):
            row = group_rows * place
            arranged[row : row + share, lanes(head)] = attended[share * place : share * (place + 1)]
            start = rows - DPAD + dec_share * place
            arranged[row + share : row + share + dec_share, lanes(head)] = attended[start : start + dec_share]
    product[...] = jnp.dot(arranged[...].astype(bf16), weight[...], preferred_element_type=f32)
    for offset, out in enumerate(outs):
        out[...] = product[span(lax.bitwise_xor(head_ref[0], offset), group_rows), :].astype(out.dtype)


def project_out(pieces, w_output, head_index, head_count):
    rows = pieces[0].shape[0]
    share = (rows - DPAD) // head_count + 8
    width, columns = w_output.shape
    return call(
        functools.partial(project_kernel, len(pieces)),
        (((share, columns), f32),) + (((share, columns), bf16),) * (head_count - 1),
        [SMEM] + [VMEM] * (len(pieces) + 1),
        (head_index, *pieces, w_output),
        "project_out",
        8,
        [pltpu.VMEM((share * head_count, width), f32), pltpu.VMEM((share * head_count, columns), f32)],
    )


def norm_kernel(parts, head_ref, pre_hbm, dec_pad, gain, *refs):
    arrived = refs[:parts]
    tokens, dec = refs[parts : parts + 2]
    mids = refs[parts + 2 : 2 * parts + 2]
    rows, mid, sem = refs[2 * parts + 2 :]
    share = rows.shape[0]
    head = head_ref[0]
    copy = pltpu.make_async_copy(pre_hbm.at[span(head, share)], rows, sem)
    copy.start()
    total = tree_sum([part[...].astype(f32) for part in arrived])
    copy.wait()
    mid[0:share, :] = rows[...].astype(f32) + total[:share]
    mid[share:, :] = dec_pad[span(head, 8), :] + total[share:]
    for offset, out in enumerate(mids):
        out[...] = mid[:, span(lax.bitwise_xor(head, offset), out.shape[1])]
    values = mid[...]
    meansq = jnp.mean(values * values, axis=-1, keepdims=True)
    scaled = values * lax.rsqrt(meansq + eps_norm) * gain[...]
    tokens[...] = scaled[:share].astype(bf16)
    dec[...] = scaled[share:].astype(bf16)


def experts_kernel(offsets, chunks, chips, scalar_ref, *refs):
    count = len(offsets)
    data = refs[:count]
    query, table_d = refs[count : count + 2]
    weights = refs[count + 2 : count + 8]
    outs = refs[count + 8 : count + 8 + chunks]
    rows_in, table = refs[count + 8 + chunks :]
    each = weights[0].shape[0]
    experts = 2 * each
    piece, depth = data[0].shape
    width = depth // chunks
    long = piece - 8
    share = long // chips
    tok = share * chunks
    base = query.shape[1] - table_d.shape[1]
    rows = count * piece
    tile = rows if rows <= 320 else piece
    places = [lax.bitwise_xor(scalar_ref[0], offset) for offset in range(chunks)]
    for index, offset in enumerate(offsets):
        rows_in[long * index : long * (index + 1), :] = data[index][:long, :]
        row = long * count + 8 * index
        rows_in[row : row + 8, :] = data[index][long:, :]
        table[row : row + 8, :] = table_d[span(places[offset], 8), :]
        for chip in range(chips):
            row = long * index + share * chip
            start = pl.multiple_of(tok * chip + share * places[offset], share)
            table[row : row + share, :] = query[pl.ds(start, share), base:].astype(f32)
    lane = lax.broadcasted_iota(jnp.int32, (tile, table.shape[1]), 1)
    found = {}
    for row in range(0, rows, tile):
        here = slice(row, row + tile)
        block = rows_in[here, :]
        for expert in range(experts):
            w_gate, w_up, _ = weights[:3] if expert < each else weights[3:]
            local = expert % each
            number = lax.bitwise_xor(scalar_ref[1], expert // each) * each + local
            gate = jnp.dot(block, w_gate[local], preferred_element_type=f32)
            up = jnp.dot(block, w_up[local], preferred_element_type=f32)
            act = (gate / (1.0 + jnp.exp(-gate)) * up).astype(bf16)
            factor = jnp.sum(jnp.where(lane == number, table[here, :], 0.0), axis=-1, keepdims=True)
            found[row, expert] = act, factor
    dec_share = DEC // chunks
    for out, place in zip(outs, places):
        values = []
        for row in range(0, rows, tile):
            sums = []
            for first in (0, each):
                total = None
                for expert in range(first, first + each):
                    act, factor = found[row, expert]
                    w_down = weights[2 if first == 0 else 5]
                    down = jnp.dot(
                        act, w_down[expert % each, :, span(place, width)], preferred_element_type=f32
                    )
                    down = down.astype(bf16).astype(f32) * factor
                    total = down if total is None else total + down
                sums.append(total)
            values.append(sums[0] + sums[1])
        value = values[0] if len(values) == 1 else jnp.concatenate(values, axis=0)
        out[: long * count, :] = value[: long * count].astype(bf16)
        out[long * count :, :] = jnp.zeros_like(out[long * count :, :])
        for index in range(count):
            start = long * count + 8 * index
            row = long * count + dec_share * index
            out[row : row + dec_share, :] = value[start : start + dec_share].astype(bf16)


def run_experts(data, offsets, query, table_d, weights, scalars, chips, chunks, name):
    count = len(data)
    piece, depth = data[0].shape
    width = depth // chunks
    tail = -(-(DEC // chunks) * count // 8) * 8
    return list(
        call(
            functools.partial(experts_kernel, offsets, chunks, chips),
            ((((piece - 8) * count + tail, width), bf16),) * chunks,
            [SMEM] + [VMEM] * (count + 8),
            (scalars, *data, query, table_d, *weights),
            name,
            28,
            [
                pltpu.VMEM((count * piece, depth), bf16),
                pltpu.VMEM((count * piece, table_d.shape[1]), f32),
            ],
            pl.CostEstimate(
                flops=12 * count * piece * depth * weights[0].shape[2],
                transcendentals=0,
                bytes_accessed=2 * sum(w.size for w in weights),
            ),
        )
    )


def head_sum_kernel(parts, share, *refs):
    early, late, outs = refs[:parts], refs[parts : 2 * parts], refs[2 * parts :]
    chips = len(outs)
    long = share * chips
    tok = share * parts
    dec_share = DEC // parts
    for out in outs:
        out[tok:, :] = jnp.zeros_like(out[tok:, :])
    for mine in range(parts):
        found, found_d = [], []
        for sender in range(parts):
            index = mine ^ sender
            source, count = early[sender], parts - 1
            if index == parts - 1:
                source, index, count = late[sender], 0, 1
            found.append(source[long * index : long * (index + 1), :].astype(f32))
            row = long * count + dec_share * index
            found_d.append(source[row : row + dec_share, :].astype(f32))
        total = tree_sum(found).astype(bf16)
        total_d = tree_sum(found_d).astype(bf16)
        for chip, out in enumerate(outs):
            out[share * mine : share * (mine + 1), :] = total[share * chip : share * (chip + 1)]
            out[tok + dec_share * mine : tok + dec_share * (mine + 1), :] = total_d


def final_kernel(parts, head_ref, *refs):
    mids, pieces = refs[:parts], refs[parts:-4]
    hidden, dec, packed, placed = refs[-4:]
    tok = hidden.shape[0]
    share = tok // parts
    dec_share = DEC // parts
    total = tree_sum([piece[...].astype(f32) for piece in pieces])
    packed[...] = jnp.zeros_like(packed)
    for offset, mid in enumerate(mids):
        place = lax.bitwise_xor(head_ref[0], offset)
        hidden[span(place, share), :] = (
            mid[0:share, :] + total[share * offset : share * (offset + 1)]
        ).astype(bf16)
        start = tok + dec_share * offset
        packed[8 * offset : 8 * offset + dec_share, :] = (
            mid[share : share + dec_share, :] + total[start : start + dec_share]
        )
        placed[span(place, 8), :] = packed[8 * offset : 8 * offset + 8, :]
    for place in range(parts):
        dec[dec_share * place : dec_share * (place + 1), :] = placed[
            8 * place : 8 * place + dec_share, :
        ].astype(bf16)


def per_device(
    pre_tokens, dec_tokens, attn_gain, w_query, w_key, w_value, w_output, cache_keys, cache_values,
    block_request, block_slot, cache_lens, moe_gain, expert_ids, expert_gates, dec_expert_ids,
    dec_expert_gates, w_gate, w_up, w_down,
):
    tok, model_width = pre_tokens.shape
    width = w_query.shape[1]
    blk_count = lax.axis_size("blk")
    blk_index = lax.axis_index("blk").astype(jnp.int32)
    head_count = lax.axis_size("head")
    head_index = lax.axis_index("head").astype(jnp.int32)
    chips = blk_count // 2
    head_scalar = head_index.reshape(1)
    scalars = jnp.stack([head_index, blk_index])
    part_width = model_width // head_count
    tables = -(-w_gate.shape[0] * blk_count // HD) * HD
    rows = tok + DPAD

    row = jnp.arange(rows, dtype=jnp.int32)
    request = jnp.maximum(row - tok + PRE, 0)[:, None] == jnp.arange(REQS, dtype=jnp.int32)
    positions = jnp.sum(jnp.where(request, cache_lens, 0), axis=1)
    positions = positions + jnp.where(row < tok, blk_index * tok + row, 0)
    frequencies = rope_base ** (-jnp.arange(HD // 2, dtype=f32) / (HD // 2))
    angles = positions.astype(f32)[:, None] * frequencies[None, :]
    cosine = jnp.cos(angles)
    sine = jnp.sin(angles)
    cosine = jnp.concatenate([cosine, cosine], axis=1)
    sine = jnp.concatenate([-sine, sine], axis=1)

    dec_rows = 8 * head_count
    sources = (
        pre_tokens, dec_tokens, attn_gain[None, :], w_query,
        expert_ids.T, expert_gates.T, dec_expert_ids.T, dec_expert_gates.T,
    )
    message, query_d, table_d, normed, dec_pad = call(
        query_kernel,
        (
            ((tok, width + tables), bf16),
            ((DPAD, width), bf16),
            ((dec_rows, tables), f32),
            ((rows, model_width), bf16),
            ((dec_rows, model_width), f32),
        ),
        [HBM] * 8 + [VMEM] * 2,
        (*sources, cosine, sine),
        "queries",
        16,
        [
            *(pltpu.VMEM(source.shape, source.dtype) for source in sources),
            pltpu.VMEM((dec_rows, model_width), f32),
            pltpu.SemaphoreType.DMA((len(sources) + 3,)),
        ],
    )

    def exchange(pieces, axis, step):
        return [pieces[0]] + [swap(pieces[o], axis, step * o) for o in range(1, len(pieces))]

    new_cache, dec_cache, *new = call(
        key_kernel,
        (
            ((2, tok, width), bf16),
            ((2, DEC, width), bf16),
            ((tok, width), bf16),
            ((tok, width), bf16),
            ((DPAD, width), bf16),
            ((DPAD, width), bf16),
        ),
        [VMEM] + [HBM] * 2 + [VMEM] * 2,
        (normed, w_key, w_value, cosine, sine),
        "keys",
        16,
        [
            pltpu.VMEM(w_key.shape, bf16),
            pltpu.VMEM(w_value.shape, bf16),
            pltpu.SemaphoreType.DMA((2,)),
        ],
        pl.CostEstimate(
            flops=4 * rows * model_width * width,
            transcendentals=0,
            bytes_accessed=4 * model_width * width,
        ),
    )
    gate_other = swap(w_gate, "blk", 1)
    pieces = exchange([message] * chips, "blk", 2)
    new_cache, *pieces = lax.optimization_barrier((new_cache, *pieces))
    query_a = jnp.concatenate(pieces, axis=0)
    query_b = swap(query_a, "blk", 1)
    query_b, gate_other = lax.optimization_barrier((query_b, gate_other))

    keep, send, dec = attention(
        query_a, query_b, query_d, new, cache_keys, cache_values,
        (block_request, block_slot, cache_lens, blk_index.reshape(1)),
    )
    pieces = merge_core(keep, swap(send, "blk", 1), dec, swap(dec, "blk", 1), chips)
    *pieces, up_source = lax.optimization_barrier((*pieces, w_up))
    up_other = swap(up_source, "blk", 1)
    (weight,) = load((w_output,), pieces[0], "load_output")
    pieces = exchange(pieces, "blk", 2)
    pieces[-1], weight, up_other = lax.optimization_barrier((pieces[-1], weight, up_other))
    partial = project_out(pieces, weight, head_scalar, head_count)
    *partial, down_source = lax.optimization_barrier((*partial, w_down))
    down_other = swap(down_source, "blk", 1)
    partial = exchange(partial, "head", 1)
    partial[-1], down_other = lax.optimization_barrier((partial[-1], down_other))
    share = tok // head_count
    moe_tok, moe_dec, *mids = call(
        functools.partial(norm_kernel, head_count),
        (
            ((share, model_width), bf16),
            ((8, model_width), bf16),
            *(((share + 8, part_width), f32),) * head_count,
        ),
        [SMEM, HBM] + [VMEM] * (2 + head_count),
        (head_scalar, pre_tokens, dec_pad, moe_gain[None, :], *partial),
        "moe_norm",
        8,
        [
            pltpu.VMEM((share, model_width), bf16),
            pltpu.VMEM((share + 8, model_width), f32),
            pltpu.SemaphoreType.DMA,
        ],
    )
    spread = exchange([moe_tok] * chips, "blk", 2)
    mids[1:-1] = [swap(mids[o], "head", o) for o in range(1, head_count - 1)]
    spread[-1], *mids[1:-1] = lax.optimization_barrier((spread[-1], *mids[1:-1]))
    gathered = jnp.concatenate([*spread, moe_dec], axis=0)
    data = exchange([gathered] * head_count, "head", 1)
    weights = load((w_gate, w_up, w_down), gathered, "load_experts")
    data[1], *weights = lax.optimization_barrier((data[1], *weights))
    weights = (*weights, gate_other, up_other, down_other)
    offsets = tuple(range(head_count))
    shared = (query_a, table_d, weights, scalars, chips, head_count)
    early = run_experts(data[:-1], offsets[:-1], *shared, "experts_early")
    late = run_experts(data[-1:], offsets[-1:], *shared, "experts_late")
    early = exchange(early, "head", 1)
    late = exchange(late, "head", 1)
    final = call(
        functools.partial(head_sum_kernel, head_count, share),
        (((rows, part_width), bf16),) * chips,
        [VMEM] * (2 * head_count),
        (*early, *late),
        "head_sum",
        8,
    )
    final = list(final)
    *final, mids[-1] = lax.optimization_barrier((*final, mids[-1]))
    final = exchange(final, "blk", 2)
    mids[-1] = swap(mids[-1], "head", head_count - 1)
    hidden, dec_hidden = call(
        functools.partial(final_kernel, head_count),
        (((tok, part_width), bf16), ((DEC, part_width), bf16)),
        [SMEM] + [VMEM] * (head_count + chips),
        (head_scalar, *mids, *final),
        "final",
        8,
        [pltpu.VMEM((dec_rows, part_width), f32), pltpu.VMEM((dec_rows, part_width), f32)],
    )
    return (hidden, dec_hidden, new_cache, dec_cache)


def solution(mesh):
    placed = (
        P("blk", None),
        P(),
        P(),
        P(None, "head"),
        P(None, "head"),
        P(None, "head"),
        P("head", None),
        P("blk", None, "head"),
        P("blk", None, "head"),
        P("blk"),
        P("blk"),
        P(),
        P(),
        P("blk", None),
        P("blk", None),
        P(),
        P(),
        P("blk", None, "head"),
        P("blk", None, "head"),
        P("blk", "head", None),
    )
    return jax.shard_map(
        per_device,
        mesh=mesh,
        in_specs=placed,
        out_specs=(
            P("blk", "head"),
            P(None, "head"),
            P(None, "blk", "head"),
            P(None, None, "head"),
        ),
        check_vma=False,
    )
```

```python
import functools

import jax
import jax.numpy as jnp
from jax import lax
from jax.experimental import pallas as pl
from jax.experimental.pallas import tpu as pltpu
from jax.sharding import PartitionSpec as P

HD = 128
PRE = 1
DEC = 12
REQS = 13
DPAD = 16
TILE = 256

eps_norm = 1e-06
rope_base = 50000.0
neg_fill = -1e30
LOG2E = 1.4426950408889634
bf16 = jnp.bfloat16
f32 = jnp.float32


def swap(value, axis, mask):
    count = lax.axis_size(axis)
    return lax.ppermute(value, axis, [(i, i ^ mask) for i in range(count)])


def span(index, size):
    return pl.ds(pl.multiple_of(index * size, size), size)


def lanes(head):
    return slice(head * HD, (head + 1) * HD)


def tree_sum(values):
    values = list(values)
    while len(values) > 1:
        values = [a + b for a, b in zip(values[::2], values[1::2])]
    return values[0]


VMEM = pl.BlockSpec(memory_space=pltpu.VMEM)
SMEM = pl.BlockSpec(memory_space=pltpu.SMEM)
HBM = pl.BlockSpec(memory_space=pltpu.HBM)


def call(body, outs, ins, args, name, limit, scratch=(), cost=None):
    args = [
        pltpu.with_memory_space_constraint(arg, pltpu.HBM) if spec is HBM else arg
        for spec, arg in zip(ins, args)
    ]
    return pl.pallas_call(
        body,
        out_shape=tuple(jax.ShapeDtypeStruct(shape, dtype) for shape, dtype in outs),
        in_specs=list(ins),
        out_specs=tuple(VMEM for _ in outs),
        scratch_shapes=list(scratch),
        compiler_params=pltpu.CompilerParams(vmem_limit_bytes=limit << 20),
        cost_estimate=cost,
        name=name,
    )(*args)


def turn(flat, cosine, sine):
    heads = []
    for head in range(flat.shape[1] // HD):
        block = flat[:, lanes(head)]
        heads.append(block * cosine + pltpu.roll(block, HD // 2, 1) * sine)
    return jnp.concatenate(heads, axis=1).astype(bf16)


def gate_lanes(ids, gates, width):
    names = ids[...]
    values = gates[...].astype(f32)
    place = lax.broadcasted_iota(jnp.int32, (width, names.shape[1]), 0)
    table = jnp.zeros(place.shape, f32)
    for k in range(names.shape[0]):
        table = jnp.where(place == names[k : k + 1], values[k : k + 1], table)
    shape = (width, width)
    eye = lax.broadcasted_iota(jnp.int32, shape, 0) == lax.broadcasted_iota(jnp.int32, shape, 1)
    return lax.dot_general(
        table.astype(bf16),
        eye.astype(f32).astype(bf16),
        (((0,), (0,)), ((), ())),
        preferred_element_type=f32,
    )


def query_kernel(
    pre_hbm, dec_hbm, gain_hbm, weight_hbm, ids_hbm, gates_hbm, dec_ids_hbm, dec_gates_hbm, cosine, sine,
    message, query_d, table_d, normed, dec_pad,
    pre, dec, gain, weight, ids, gates, dec_ids, dec_gates, rows, sems,
):
    sources = (pre_hbm, dec_hbm, gain_hbm, ids_hbm, gates_hbm, dec_ids_hbm, dec_gates_hbm)
    targets = (pre, dec, gain, ids, gates, dec_ids, dec_gates)
    copies = [
        pltpu.make_async_copy(source, target, sems.at[index])
        for index, (source, target) in enumerate(zip(sources, targets))
    ]
    depth = weight.shape[0] // 4
    for part in range(4):
        here = pl.ds(part * depth, depth)
        copies.append(
            pltpu.make_async_copy(weight_hbm.at[here], weight.at[here], sems.at[len(sources) + part])
        )
    for copy in copies:
        copy.start()
    tok = pre.shape[0]
    width = weight.shape[1]
    heads = dec_pad.shape[0] // 8
    share = DEC // heads
    for copy in copies[:7]:
        copy.wait()

    def norm(values):
        meansq = jnp.mean(values * values, axis=-1, keepdims=True)
        return (values * lax.rsqrt(meansq + eps_norm) * gain[...]).astype(bf16)

    dec_rows = dec[...].astype(f32)
    normed[0:tok, :] = norm(pre[...].astype(f32))
    normed[tok:, :] = jnp.zeros_like(normed[tok:, :])
    normed[tok : tok + DEC, :] = norm(dec_rows)
    dec_table = gate_lanes(dec_ids, dec_gates, table_d.shape[1])
    message[:, width:] = gate_lanes(ids, gates, message.shape[1] - width).astype(bf16)
    for out, source in ((dec_pad, dec_rows), (table_d, dec_table)):
        rows[...] = jnp.zeros_like(rows)
        for head in range(heads):
            rows[8 * head : 8 * head + share, : source.shape[1]] = source[share * head : share * (head + 1)]
        out[...] = rows[:, : source.shape[1]].astype(out.dtype)
    for copy in copies[7:]:
        copy.wait()
    query = jnp.dot(normed[...], weight[...], preferred_element_type=f32)
    query = turn(query, cosine[...], sine[...])
    message[:, :width] = query[:tok]
    query_d[...] = query[tok:]


def key_kernel(
    normed, key_hbm, value_hbm, cosine, sine, new, dec, key_n, value_n, key_d, value_d, w_key, w_value, sems
):
    tok = new.shape[1]
    copies = [
        pltpu.make_async_copy(key_hbm, w_key, sems.at[0]),
        pltpu.make_async_copy(value_hbm, w_value, sems.at[1]),
    ]
    for copy in copies:
        copy.start()
    for copy in copies:
        copy.wait()
    key = turn(jnp.dot(normed[...], w_key[...], preferred_element_type=f32), cosine[...], sine[...])
    value = jnp.dot(normed[...], w_value[...], preferred_element_type=f32).astype(bf16)
    for index, (rows, plain, padded) in enumerate(((key, key_n, key_d), (value, value_n, value_d))):
        new[index] = rows[:tok]
        plain[...] = rows[:tok]
        dec[index] = rows[tok : tok + DEC]
        padded[...] = rows[tok:]


def group_turned(keys, turned_query, turned_values, live):
    scores = jnp.dot(keys, turned_query, preferred_element_type=f32)
    top = jnp.max(
        scores if live is None else jnp.where(live, scores, neg_fill), axis=0, keepdims=True
    )
    weights = jnp.exp2((scores - top) * (HD ** (-0.5) * LOG2E))
    if live is not None:
        weights = jnp.where(live, weights, 0.0)
    total = jnp.sum(weights, axis=0, keepdims=True)
    acc = jnp.dot(turned_values, weights.astype(bf16), preferred_element_type=f32)
    return top * HD ** (-0.5), total, acc


def turned(values):
    return values.astype(f32).T.astype(bf16)


def attention_kernel(
    owner_ref, slot_ref, lens_ref, blk_ref, query_a, query_b, query_d, key_new, value_new, key_dec, value_dec,
    cache_k, cache_v, keep, send, dec, key_buf, value_buf, turn_a, turn_b, spread, dec_acc, dec_stats, sems,
):
    blocks, block_len, width = cache_k.shape
    heads = width // HD
    half = query_a.shape[0]
    tile = min(TILE, half)
    sides = ((turn_a, keep), (turn_b, send))

    def copies(index):
        return (
            pltpu.make_async_copy(cache_k.at[index], key_buf.at[index], sems.at[0, index]),
            pltpu.make_async_copy(cache_v.at[index], value_buf.at[index], sems.at[1, index]),
        )

    for index in range(blocks):
        for copy in copies(index):
            copy.start()

    for query, turn_ref in ((query_a, turn_a), (query_b, turn_b)):
        for row in range(0, half, tile):
            turn_ref[:, row : row + tile] = turned(query[row : row + tile, :width])

    def over_tiles(keys, values, body):
        for head in range(heads):
            key_head = keys[:, lanes(head)]
            value_head = turned(values[:, lanes(head)])
            for query, state in sides:
                for row in range(0, half, tile):
                    columns = slice(row, row + tile)
                    body(key_head, query[lanes(head), columns], value_head, state, columns, head)

    def start(keys, query, values, state, columns, head):
        top, total, acc = group_turned(keys, query, values, None)
        state[width + head : width + head + 1, columns] = top
        state[width + heads + head : width + heads + head + 1, columns] = total
        state[lanes(head), columns] = acc

    over_tiles(key_new, value_new, start)

    lines = lax.broadcasted_iota(jnp.int32, (DPAD, width), 1)
    spread[...] = jnp.zeros_like(spread)
    for head in range(heads):
        here = (lines >= head * HD) & (lines < (head + 1) * HD)
        spread[head * DPAD : (head + 1) * DPAD, :] = jnp.where(
            here, query_d[...].astype(f32), 0.0
        ).astype(bf16)
    dec_acc[...] = jnp.zeros_like(dec_acc)
    dec_stats[0:1, :] = jnp.full((1, HD), neg_fill, f32)
    dec_stats[1:, :] = jnp.zeros_like(dec_stats[1:, :])

    @pl.loop(0, blocks)
    def _(index):
        for copy in copies(index):
            copy.wait()
        owner = owner_ref[index]
        length = lens_ref[jnp.minimum(owner, REQS - 1)]
        count = jnp.clip(length - slot_ref[index] * block_len, 0, block_len)

        def add(live, keys, query, values, state, columns, head):
            top, total, acc = group_turned(keys, query, values, live)
            top_row = slice(width + head, width + head + 1)
            total_row = slice(width + heads + head, width + heads + head + 1)
            old_top = state[top_row, columns]
            best = jnp.maximum(old_top, top)
            old_scale = jnp.exp(old_top - best)
            scale = jnp.exp(top - best)
            state[top_row, columns] = best
            state[total_row, columns] = state[total_row, columns] * old_scale + total * scale
            state[lanes(head), columns] = state[lanes(head), columns] * old_scale + acc * scale

        @pl.when((owner < PRE) & (count == block_len))
        def _():
            over_tiles(key_buf.at[index], value_buf.at[index], functools.partial(add, None))

        @pl.when((owner < PRE) & (count < block_len))
        def _():
            live = lax.broadcasted_iota(jnp.int32, (block_len, tile), 0) < count
            over_tiles(key_buf.at[index], value_buf.at[index], functools.partial(add, live))

        @pl.when((owner >= PRE) & (owner < REQS))
        def _():
            shape = (block_len, HD)
            lane = lax.broadcasted_iota(jnp.int32, shape, 1)
            live = (lax.broadcasted_iota(jnp.int32, shape, 0) < count) & (
                lax.rem(lane, DPAD) == owner - PRE
            ) & (lane < heads * DPAD)
            scores = lax.dot_general(
                key_buf[index], spread[...], (((1,), (1,)), ((), ())), preferred_element_type=f32
            )
            top = jnp.max(jnp.where(live, scores, neg_fill), axis=0, keepdims=True)
            weights = jnp.where(live, jnp.exp2((scores - top) * (HD ** (-0.5) * LOG2E)), 0.0)
            top = top * HD ** (-0.5)
            total = jnp.sum(weights, axis=0, keepdims=True)
            mixed = lax.dot_general(
                value_buf[index], weights.astype(bf16), (((0,), (0,)), ((), ())), preferred_element_type=f32
            )
            place = lax.broadcasted_iota(jnp.int32, (HD, HD), 1)
            acc = jnp.zeros((HD, HD), f32)
            for head in range(heads):
                here = (place >= head * DPAD) & (place < (head + 1) * DPAD)
                acc = jnp.where(here, mixed[lanes(head)], acc)
            old_top = dec_stats[0:1, :]
            best = jnp.maximum(old_top, top)
            old_scale = jnp.exp(old_top - best)
            scale = jnp.exp(top - best)
            dec_stats[0:1, :] = best
            dec_stats[1:2, :] = dec_stats[1:2, :] * old_scale + total * scale
            dec_acc[...] = dec_acc[...] * old_scale + acc * scale

    mine = blk_ref[0] == 0
    plain = dec_acc[...].T
    stats = jnp.concatenate([dec_stats[...], jnp.zeros((HD - 8, HD), f32)], axis=0).T
    place = lax.broadcasted_iota(jnp.int32, (DPAD, HD), 1)
    packed = jnp.zeros((DPAD, HD), f32)
    for head in range(heads):
        rows = slice(head * DPAD, (head + 1) * DPAD)
        own = jnp.sum(
            query_d[:, lanes(head)].astype(f32) * key_dec[:, lanes(head)].astype(f32),
            axis=-1,
            keepdims=True,
        ) * HD ** (-0.5)
        own = jnp.where(mine, own, neg_fill)
        top = stats[rows, 0:1]
        best = jnp.maximum(top, own)
        scale = jnp.exp(top - best)
        own_scale = jnp.where(mine, jnp.exp(own - best), 0.0)
        packed = jnp.where(place == head, best, packed)
        packed = jnp.where(place == heads + head, stats[rows, 1:2] * scale + own_scale, packed)
        dec[:, lanes(head)] = plain[rows] * scale + value_dec[:, lanes(head)].astype(f32) * own_scale
    dec[:, width:] = packed


def attention(query_a, query_b, query_d, new, cache_keys, cache_values, scalars):
    half = query_a.shape[0]
    blocks, block_len, width = cache_keys.shape
    heads = width // HD
    state = ((width + 2 * heads, half), f32)
    return call(
        attention_kernel,
        (state, state, ((DPAD, width + HD), f32)),
        [SMEM] * 4 + [VMEM] * 7 + [HBM] * 2,
        (*scalars, query_a, query_b, query_d, *new, cache_keys, cache_values),
        "attention",
        24,
        [
            pltpu.VMEM((blocks, block_len, width), bf16),
            pltpu.VMEM((blocks, block_len, width), bf16),
            pltpu.VMEM((width, half), bf16),
            pltpu.VMEM((width, half), bf16),
            pltpu.VMEM((HD, width), bf16),
            pltpu.VMEM((HD, HD), f32),
            pltpu.VMEM((8, HD), f32),
            pltpu.SemaphoreType.DMA((2, blocks)),
        ],
    )


def split(values):
    high = values.astype(bf16).astype(f32)
    middle = (values - high).astype(bf16).astype(f32)
    return high, middle, (values - high) - middle


def merge_core_kernel(mine, other, dec_mine, dec_other, *outs):
    full = dec_mine.shape[1]
    width = full - HD
    heads = width // HD
    half = mine.shape[1]
    tok = half // len(outs)

    def put(where, turned, dec):
        value = turned.T.astype(bf16)
        for index, out in enumerate(outs):
            out[0:tok, where] = value[index * tok : (index + 1) * tok]
            out[tok : tok + DPAD, where] = dec.astype(bf16)

    place = lax.broadcasted_iota(jnp.int32, (DPAD, HD), 1)
    packed = jnp.zeros((DPAD, HD), f32)
    stats_a = dec_mine[:, width:]
    stats_b = dec_other[:, width:]
    top_rows = slice(width, width + heads)
    total_rows = slice(width + heads, width + 2 * heads)
    best = jnp.maximum(mine[top_rows, :], other[top_rows, :])
    scale_a = jnp.exp(mine[top_rows, :] - best)
    scale_b = jnp.exp(other[top_rows, :] - best)
    total = mine[total_rows, :] * scale_a + other[total_rows, :] * scale_b
    for head in range(heads):
        one = slice(head, head + 1)
        two = slice(heads + head, heads + head + 1)
        turned = mine[lanes(head), :] * scale_a[one] + other[lanes(head), :] * scale_b[one]
        dec_best = jnp.maximum(stats_a[:, one], stats_b[:, one])
        dec_a = jnp.exp(stats_a[:, one] - dec_best)
        dec_b = jnp.exp(stats_b[:, one] - dec_best)
        packed = jnp.where(place == head, dec_best, packed)
        packed = jnp.where(place == heads + head, stats_a[:, two] * dec_a + stats_b[:, two] * dec_b, packed)
        put(lanes(head), turned, dec_mine[:, lanes(head)] * dec_a + dec_other[:, lanes(head)] * dec_b)
    coded = [*split(jnp.concatenate([best, total], axis=0))]
    coded.append(jnp.zeros((HD - 6 * heads, half), f32))
    high, middle, low = split(packed)
    put(
        slice(width, full),
        jnp.concatenate(coded, axis=0),
        high + pltpu.roll(middle, 2 * heads, 1) + pltpu.roll(low, 4 * heads, 1),
    )


def merge_core(mine, other, dec_mine, dec_other, parts):
    full = dec_mine.shape[1]
    tok = mine.shape[1] // parts
    return call(
        merge_core_kernel,
        (((tok + DPAD, full), bf16),) * parts,
        [VMEM] * 4,
        (mine, other, dec_mine, dec_other),
        "merge_core",
        12,
    )


def load_kernel(count, *refs):
    sources, targets, sems = refs[:count], refs[count + 1 : -1], refs[-1]
    copies = []
    for source, target in zip(sources, targets):
        depth = source.shape[-2] // 4
        for lead in range(source.shape[0]) if len(source.shape) == 3 else (None,):
            for part in range(4):
                here = pl.ds(part * depth, depth)
                where = here if lead is None else (lead, here)
                copies.append(
                    pltpu.make_async_copy(source.at[where], target.at[where], sems.at[len(copies)])
                )
    for copy in copies:
        copy.start()
    for copy in copies:
        copy.wait()


def load(arrays, after, name):
    size = sum(arr.size for arr in arrays) * 2
    count = sum(4 * (arr.shape[0] if arr.ndim == 3 else 1) for arr in arrays)
    return call(
        functools.partial(load_kernel, len(arrays)),
        tuple((arr.shape, arr.dtype) for arr in arrays),
        [HBM] * len(arrays) + [VMEM],
        (*arrays, after),
        name,
        1,
        [pltpu.SemaphoreType.DMA((count,))],
        pl.CostEstimate(flops=0, transcendentals=0, bytes_accessed=2 * size),
    )


def project_kernel(parts, head_ref, *refs):
    pieces = refs[:parts]
    weight = refs[parts]
    outs = refs[parts + 1 : -2]
    arranged, product = refs[-2:]
    rows, full = pieces[0].shape
    width = full - HD
    heads = width // HD
    group_rows = outs[0].shape[0]
    places = len(outs)
    share = (rows - DPAD) // places
    dec_share = DEC // places
    stats = []
    for piece in pieces:
        coded = piece[:, width:].astype(f32)
        stats.append(
            (coded + pltpu.roll(coded, HD - 2 * heads, 1)) + pltpu.roll(coded, HD - 4 * heads, 1)
        )
    arranged[...] = jnp.zeros_like(arranged)
    for head in range(heads):
        tops = [s[:, head : head + 1] for s in stats]
        best = functools.reduce(jnp.maximum, tops)
        scales = [jnp.exp(top - best) for top in tops]
        total = tree_sum([s[:, heads + head : heads + head + 1] * c for s, c in zip(stats, scales)])
        acc = tree_sum([piece[:, lanes(head)].astype(f32) * c for piece, c in zip(pieces, scales)])
        attended = acc / total
        for place in range(places):
            row = group_rows * place
            arranged[row : row + share, lanes(head)] = attended[share * place : share * (place + 1)]
            start = rows - DPAD + dec_share * place
            arranged[row + share : row + share + dec_share, lanes(head)] = attended[start : start + dec_share]
    product[...] = jnp.dot(arranged[...].astype(bf16), weight[...], preferred_element_type=f32)
    for offset, out in enumerate(outs):
        out[...] = product[span(lax.bitwise_xor(head_ref[0], offset), group_rows), :].astype(out.dtype)


def project_out(pieces, w_output, head_index, head_count):
    rows = pieces[0].shape[0]
    share = (rows - DPAD) // head_count + 8
    width, columns = w_output.shape
    return call(
        functools.partial(project_kernel, len(pieces)),
        (((share, columns), f32),) + (((share, columns), bf16),) * (head_count - 1),
        [SMEM] + [VMEM] * (len(pieces) + 1),
        (head_index, *pieces, w_output),
        "project_out",
        8,
        [pltpu.VMEM((share * head_count, width), f32), pltpu.VMEM((share * head_count, columns), f32)],
    )


def norm_kernel(parts, head_ref, pre_hbm, dec_pad, gain, *refs):
    arrived = refs[:parts]
    tokens, dec = refs[parts : parts + 2]
    mids = refs[parts + 2 : 2 * parts + 2]
    rows, mid, sem = refs[2 * parts + 2 :]
    share = rows.shape[0]
    head = head_ref[0]
    copy = pltpu.make_async_copy(pre_hbm.at[span(head, share)], rows, sem)
    copy.start()
    total = tree_sum([part[...].astype(f32) for part in arrived])
    copy.wait()
    mid[0:share, :] = rows[...].astype(f32) + total[:share]
    mid[share:, :] = dec_pad[span(head, 8), :] + total[share:]
    for offset, out in enumerate(mids):
        out[...] = mid[:, span(lax.bitwise_xor(head, offset), out.shape[1])]
    values = mid[...]
    meansq = jnp.mean(values * values, axis=-1, keepdims=True)
    scaled = values * lax.rsqrt(meansq + eps_norm) * gain[...]
    tokens[...] = scaled[:share].astype(bf16)
    dec[...] = scaled[share:].astype(bf16)


def experts_kernel(offsets, chunks, chips, scalar_ref, *refs):
    count = len(offsets)
    data = refs[:count]
    query, table_d = refs[count : count + 2]
    weights = refs[count + 2 : count + 8]
    outs = refs[count + 8 : count + 8 + chunks]
    rows_in, table = refs[count + 8 + chunks :]
    each = weights[0].shape[0]
    experts = 2 * each
    piece, depth = data[0].shape
    width = depth // chunks
    long = piece - 8
    share = long // chips
    tok = share * chunks
    base = query.shape[1] - table_d.shape[1]
    rows = count * piece
    tile = rows if rows <= 320 else piece
    places = [lax.bitwise_xor(scalar_ref[0], offset) for offset in range(chunks)]
    for index, offset in enumerate(offsets):
        rows_in[long * index : long * (index + 1), :] = data[index][:long, :]
        row = long * count + 8 * index
        rows_in[row : row + 8, :] = data[index][long:, :]
        table[row : row + 8, :] = table_d[span(places[offset], 8), :]
        for chip in range(chips):
            row = long * index + share * chip
            start = pl.multiple_of(tok * chip + share * places[offset], share)
            table[row : row + share, :] = query[pl.ds(start, share), base:].astype(f32)
    lane = lax.broadcasted_iota(jnp.int32, (tile, table.shape[1]), 1)
    found = {}
    for row in range(0, rows, tile):
        here = slice(row, row + tile)
        block = rows_in[here, :]
        for expert in range(experts):
            w_gate, w_up, _ = weights[:3] if expert < each else weights[3:]
            local = expert % each
            number = lax.bitwise_xor(scalar_ref[1], expert // each) * each + local
            gate = jnp.dot(block, w_gate[local], preferred_element_type=f32)
            up = jnp.dot(block, w_up[local], preferred_element_type=f32)
            act = (gate / (1.0 + jnp.exp(-gate)) * up).astype(bf16)
            factor = jnp.sum(jnp.where(lane == number, table[here, :], 0.0), axis=-1, keepdims=True)
            found[row, expert] = act, factor
    dec_share = DEC // chunks
    for out, place in zip(outs, places):
        values = []
        for row in range(0, rows, tile):
            sums = []
            for first in (0, each):
                total = None
                for expert in range(first, first + each):
                    act, factor = found[row, expert]
                    w_down = weights[2 if first == 0 else 5]
                    down = jnp.dot(
                        act, w_down[expert % each, :, span(place, width)], preferred_element_type=f32
                    )
                    down = down.astype(bf16).astype(f32) * factor
                    total = down if total is None else total + down
                sums.append(total)
            values.append(sums[0] + sums[1])
        value = values[0] if len(values) == 1 else jnp.concatenate(values, axis=0)
        out[: long * count, :] = value[: long * count].astype(bf16)
        out[long * count :, :] = jnp.zeros_like(out[long * count :, :])
        for index in range(count):
            start = long * count + 8 * index
            row = long * count + dec_share * index
            out[row : row + dec_share, :] = value[start : start + dec_share].astype(bf16)


def run_experts(data, offsets, query, table_d, weights, scalars, chips, chunks, name):
    count = len(data)
    piece, depth = data[0].shape
    width = depth // chunks
    tail = -(-(DEC // chunks) * count // 8) * 8
    return list(
        call(
            functools.partial(experts_kernel, offsets, chunks, chips),
            ((((piece - 8) * count + tail, width), bf16),) * chunks,
            [SMEM] + [VMEM] * (count + 8),
            (scalars, *data, query, table_d, *weights),
            name,
            28,
            [
                pltpu.VMEM((count * piece, depth), bf16),
                pltpu.VMEM((count * piece, table_d.shape[1]), f32),
            ],
            pl.CostEstimate(
                flops=12 * count * piece * depth * weights[0].shape[2],
                transcendentals=0,
                bytes_accessed=2 * sum(w.size for w in weights),
            ),
        )
    )


def head_sum_kernel(parts, share, *refs):
    early, late, outs = refs[:parts], refs[parts : 2 * parts], refs[2 * parts :]
    chips = len(outs)
    long = share * chips
    tok = share * parts
    dec_share = DEC // parts
    for out in outs:
        out[tok:, :] = jnp.zeros_like(out[tok:, :])
    for mine in range(parts):
        found, found_d = [], []
        for sender in range(parts):
            index = mine ^ sender
            source, count = early[sender], parts - 1
            if index == parts - 1:
                source, index, count = late[sender], 0, 1
            found.append(source[long * index : long * (index + 1), :].astype(f32))
            row = long * count + dec_share * index
            found_d.append(source[row : row + dec_share, :].astype(f32))
        total = tree_sum(found).astype(bf16)
        total_d = tree_sum(found_d).astype(bf16)
        for chip, out in enumerate(outs):
            out[share * mine : share * (mine + 1), :] = total[share * chip : share * (chip + 1)]
            out[tok + dec_share * mine : tok + dec_share * (mine + 1), :] = total_d


def final_kernel(parts, head_ref, *refs):
    mids, pieces = refs[:parts], refs[parts:-4]
    hidden, dec, packed, placed = refs[-4:]
    tok = hidden.shape[0]
    share = tok // parts
    dec_share = DEC // parts
    total = tree_sum([piece[...].astype(f32) for piece in pieces])
    packed[...] = jnp.zeros_like(packed)
    for offset, mid in enumerate(mids):
        place = lax.bitwise_xor(head_ref[0], offset)
        hidden[span(place, share), :] = (
            mid[0:share, :] + total[share * offset : share * (offset + 1)]
        ).astype(bf16)
        start = tok + dec_share * offset
        packed[8 * offset : 8 * offset + dec_share, :] = (
            mid[share : share + dec_share, :] + total[start : start + dec_share]
        )
        placed[span(place, 8), :] = packed[8 * offset : 8 * offset + 8, :]
    for place in range(parts):
        dec[dec_share * place : dec_share * (place + 1), :] = placed[
            8 * place : 8 * place + dec_share, :
        ].astype(bf16)


def per_device(
    pre_tokens, dec_tokens, attn_gain, w_query, w_key, w_value, w_output, cache_keys, cache_values,
    block_request, block_slot, cache_lens, moe_gain, expert_ids, expert_gates, dec_expert_ids,
    dec_expert_gates, w_gate, w_up, w_down,
):
    tok, model_width = pre_tokens.shape
    width = w_query.shape[1]
    blk_count = lax.axis_size("blk")
    blk_index = lax.axis_index("blk").astype(jnp.int32)
    head_count = lax.axis_size("head")
    head_index = lax.axis_index("head").astype(jnp.int32)
    chips = blk_count // 2
    head_scalar = head_index.reshape(1)
    scalars = jnp.stack([head_index, blk_index])
    part_width = model_width // head_count
    tables = -(-w_gate.shape[0] * blk_count // HD) * HD
    rows = tok + DPAD

    row = jnp.arange(rows, dtype=jnp.int32)
    request = jnp.maximum(row - tok + PRE, 0)[:, None] == jnp.arange(REQS, dtype=jnp.int32)
    positions = jnp.sum(jnp.where(request, cache_lens, 0), axis=1)
    positions = positions + jnp.where(row < tok, blk_index * tok + row, 0)
    frequencies = rope_base ** (-jnp.arange(HD // 2, dtype=f32) / (HD // 2))
    angles = positions.astype(f32)[:, None] * frequencies[None, :]
    cosine = jnp.cos(angles)
    sine = jnp.sin(angles)
    cosine = jnp.concatenate([cosine, cosine], axis=1)
    sine = jnp.concatenate([-sine, sine], axis=1)

    dec_rows = 8 * head_count
    sources = (
        pre_tokens, dec_tokens, attn_gain[None, :], w_query,
        expert_ids.T, expert_gates.T, dec_expert_ids.T, dec_expert_gates.T,
    )
    message, query_d, table_d, normed, dec_pad = call(
        query_kernel,
        (
            ((tok, width + tables), bf16),
            ((DPAD, width), bf16),
            ((dec_rows, tables), f32),
            ((rows, model_width), bf16),
            ((dec_rows, model_width), f32),
        ),
        [HBM] * 8 + [VMEM] * 2,
        (*sources, cosine, sine),
        "queries",
        16,
        [
            *(pltpu.VMEM(source.shape, source.dtype) for source in sources),
            pltpu.VMEM((dec_rows, model_width), f32),
            pltpu.SemaphoreType.DMA((len(sources) + 3,)),
        ],
    )

    def exchange(pieces, axis, step):
        return [pieces[0]] + [swap(pieces[o], axis, step * o) for o in range(1, len(pieces))]

    new_cache, dec_cache, *new = call(
        key_kernel,
        (
            ((2, tok, width), bf16),
            ((2, DEC, width), bf16),
            ((tok, width), bf16),
            ((tok, width), bf16),
            ((DPAD, width), bf16),
            ((DPAD, width), bf16),
        ),
        [VMEM] + [HBM] * 2 + [VMEM] * 2,
        (normed, w_key, w_value, cosine, sine),
        "keys",
        16,
        [
            pltpu.VMEM(w_key.shape, bf16),
            pltpu.VMEM(w_value.shape, bf16),
            pltpu.SemaphoreType.DMA((2,)),
        ],
        pl.CostEstimate(
            flops=4 * rows * model_width * width,
            transcendentals=0,
            bytes_accessed=4 * model_width * width,
        ),
    )
    gate_other = swap(w_gate, "blk", 1)
    pieces = exchange([message] * chips, "blk", 2)
    new_cache, *pieces = lax.optimization_barrier((new_cache, *pieces))
    query_a = jnp.concatenate(pieces, axis=0)
    query_b = swap(query_a, "blk", 1)
    query_b, gate_other = lax.optimization_barrier((query_b, gate_other))

    keep, send, dec = attention(
        query_a, query_b, query_d, new, cache_keys, cache_values,
        (block_request, block_slot, cache_lens, blk_index.reshape(1)),
    )
    pieces = merge_core(keep, swap(send, "blk", 1), dec, swap(dec, "blk", 1), chips)
    *pieces, up_source = lax.optimization_barrier((*pieces, w_up))
    up_other = swap(up_source, "blk", 1)
    (weight,) = load((w_output,), pieces[0], "load_output")
    pieces = exchange(pieces, "blk", 2)
    pieces[-1], weight, up_other = lax.optimization_barrier((pieces[-1], weight, up_other))
    partial = project_out(pieces, weight, head_scalar, head_count)
    *partial, down_source = lax.optimization_barrier((*partial, w_down))
    down_other = swap(down_source, "blk", 1)
    partial = exchange(partial, "head", 1)
    partial[-1], down_other = lax.optimization_barrier((partial[-1], down_other))
    share = tok // head_count
    moe_tok, moe_dec, *mids = call(
        functools.partial(norm_kernel, head_count),
        (
            ((share, model_width), bf16),
            ((8, model_width), bf16),
            *(((share + 8, part_width), f32),) * head_count,
        ),
        [SMEM, HBM] + [VMEM] * (2 + head_count),
        (head_scalar, pre_tokens, dec_pad, moe_gain[None, :], *partial),
        "moe_norm",
        8,
        [
            pltpu.VMEM((share, model_width), bf16),
            pltpu.VMEM((share + 8, model_width), f32),
            pltpu.SemaphoreType.DMA,
        ],
    )
    spread = exchange([moe_tok] * chips, "blk", 2)
    mids[1:-1] = [swap(mids[o], "head", o) for o in range(1, head_count - 1)]
    spread[-1], *mids[1:-1] = lax.optimization_barrier((spread[-1], *mids[1:-1]))
    gathered = jnp.concatenate([*spread, moe_dec], axis=0)
    data = exchange([gathered] * head_count, "head", 1)
    weights = load((w_gate, w_up, w_down), gathered, "load_experts")
    data[1], *weights = lax.optimization_barrier((data[1], *weights))
    weights = (*weights, gate_other, up_other, down_other)
    offsets = tuple(range(head_count))
    shared = (query_a, table_d, weights, scalars, chips, head_count)
    early = run_experts(data[:-1], offsets[:-1], *shared, "experts_early")
    late = run_experts(data[-1:], offsets[-1:], *shared, "experts_late")
    early = exchange(early, "head", 1)
    late = exchange(late, "head", 1)
    final = call(
        functools.partial(head_sum_kernel, head_count, share),
        (((rows, part_width), bf16),) * chips,
        [VMEM] * (2 * head_count),
        (*early, *late),
        "head_sum",
        8,
    )
    final = list(final)
    *final, mids[-1] = lax.optimization_barrier((*final, mids[-1]))
    final = exchange(final, "blk", 2)
    mids[-1] = swap(mids[-1], "head", head_count - 1)
    hidden, dec_hidden = call(
        functools.partial(final_kernel, head_count),
        (((tok, part_width), bf16), ((DEC, part_width), bf16)),
        [SMEM] + [VMEM] * (head_count + chips),
        (head_scalar, *mids, *final),
        "final",
        8,
        [pltpu.VMEM((dec_rows, part_width), f32), pltpu.VMEM((dec_rows, part_width), f32)],
    )
    return (hidden, dec_hidden, new_cache, dec_cache)


def solution(mesh):
    placed = (
        P("blk", None),
        P(),
        P(),
        P(None, "head"),
        P(None, "head"),
        P(None, "head"),
        P("head", None),
        P("blk", None, "head"),
        P("blk", None, "head"),
        P("blk"),
        P("blk"),
        P(),
        P(),
        P("blk", None),
        P("blk", None),
        P(),
        P(),
        P("blk", None, "head"),
        P("blk", None, "head"),
        P("blk", "head", None),
    )
    return jax.shard_map(
        per_device,
        mesh=mesh,
        in_specs=placed,
        out_specs=(
            P("blk", "head"),
            P(None, "head"),
            P(None, "blk", "head"),
            P(None, None, "head"),
        ),
        check_vma=False,
    )
```

```python
import functools

import jax
import jax.numpy as jnp
from jax import lax
from jax.experimental import pallas as pl
from jax.experimental.pallas import tpu as pltpu
from jax.sharding import PartitionSpec as P

HD = 128
PRE = 1
DEC = 12
REQS = 13
DPAD = 16
TILE = 256

eps_norm = 1e-06
rope_base = 50000.0
neg_fill = -1e30
LOG2E = 1.4426950408889634
bf16 = jnp.bfloat16
f32 = jnp.float32


def swap(value, axis, mask):
    count = lax.axis_size(axis)
    return lax.ppermute(value, axis, [(i, i ^ mask) for i in range(count)])


def span(index, size):
    return pl.ds(pl.multiple_of(index * size, size), size)


def lanes(head):
    return slice(head * HD, (head + 1) * HD)


def tree_sum(values):
    values = list(values)
    while len(values) > 1:
        values = [a + b for a, b in zip(values[::2], values[1::2])]
    return values[0]


VMEM = pl.BlockSpec(memory_space=pltpu.VMEM)
SMEM = pl.BlockSpec(memory_space=pltpu.SMEM)
HBM = pl.BlockSpec(memory_space=pltpu.HBM)


def call(body, outs, ins, args, name, limit, scratch=(), cost=None):
    args = [
        pltpu.with_memory_space_constraint(arg, pltpu.HBM) if spec is HBM else arg
        for spec, arg in zip(ins, args)
    ]
    return pl.pallas_call(
        body,
        out_shape=tuple(jax.ShapeDtypeStruct(shape, dtype) for shape, dtype in outs),
        in_specs=list(ins),
        out_specs=tuple(VMEM for _ in outs),
        scratch_shapes=list(scratch),
        compiler_params=pltpu.CompilerParams(vmem_limit_bytes=limit << 20),
        cost_estimate=cost,
        name=name,
    )(*args)


def turn(flat, cosine, sine):
    heads = []
    for head in range(flat.shape[1] // HD):
        block = flat[:, lanes(head)]
        heads.append(block * cosine + pltpu.roll(block, HD // 2, 1) * sine)
    return jnp.concatenate(heads, axis=1).astype(bf16)


def gate_lanes(ids, gates, width):
    names = ids[...]
    values = gates[...].astype(f32)
    place = lax.broadcasted_iota(jnp.int32, (width, names.shape[1]), 0)
    table = jnp.zeros(place.shape, f32)
    for k in range(names.shape[0]):
        table = jnp.where(place == names[k : k + 1], values[k : k + 1], table)
    shape = (width, width)
    eye = lax.broadcasted_iota(jnp.int32, shape, 0) == lax.broadcasted_iota(jnp.int32, shape, 1)
    return lax.dot_general(
        table.astype(bf16),
        eye.astype(f32).astype(bf16),
        (((0,), (0,)), ((), ())),
        preferred_element_type=f32,
    )


def query_kernel(
    pre_hbm, dec_hbm, gain_hbm, weight_hbm, ids_hbm, gates_hbm, dec_ids_hbm, dec_gates_hbm, cosine, sine,
    message, query_d, table_d, normed, dec_pad,
    pre, dec, gain, weight, ids, gates, dec_ids, dec_gates, rows, sems,
):
    sources = (pre_hbm, dec_hbm, gain_hbm, ids_hbm, gates_hbm, dec_ids_hbm, dec_gates_hbm)
    targets = (pre, dec, gain, ids, gates, dec_ids, dec_gates)
    copies = [
        pltpu.make_async_copy(source, target, sems.at[index])
        for index, (source, target) in enumerate(zip(sources, targets))
    ]
    depth = weight.shape[0] // 4
    for part in range(4):
        here = pl.ds(part * depth, depth)
        copies.append(
            pltpu.make_async_copy(weight_hbm.at[here], weight.at[here], sems.at[len(sources) + part])
        )
    for copy in copies:
        copy.start()
    tok = pre.shape[0]
    width = weight.shape[1]
    heads = dec_pad.shape[0] // 8
    share = DEC // heads
    for copy in copies[:7]:
        copy.wait()

    def norm(values):
        meansq = jnp.mean(values * values, axis=-1, keepdims=True)
        return (values * lax.rsqrt(meansq + eps_norm) * gain[...]).astype(bf16)

    dec_rows = dec[...].astype(f32)
    normed[0:tok, :] = norm(pre[...].astype(f32))
    normed[tok:, :] = jnp.zeros_like(normed[tok:, :])
    normed[tok : tok + DEC, :] = norm(dec_rows)
    dec_table = gate_lanes(dec_ids, dec_gates, table_d.shape[1])
    message[:, width:] = gate_lanes(ids, gates, message.shape[1] - width).astype(bf16)
    for out, source in ((dec_pad, dec_rows), (table_d, dec_table)):
        rows[...] = jnp.zeros_like(rows)
        for head in range(heads):
            rows[8 * head : 8 * head + share, : source.shape[1]] = source[share * head : share * (head + 1)]
        out[...] = rows[:, : source.shape[1]].astype(out.dtype)
    for copy in copies[7:]:
        copy.wait()
    query = jnp.dot(normed[...], weight[...], preferred_element_type=f32)
    query = turn(query, cosine[...], sine[...])
    message[:, :width] = query[:tok]
    query_d[...] = query[tok:]


def key_kernel(
    normed, key_hbm, value_hbm, cosine, sine, new, dec, key_n, value_n, key_d, value_d, w_key, w_value, sems
):
    tok = new.shape[1]
    copies = [
        pltpu.make_async_copy(key_hbm, w_key, sems.at[0]),
        pltpu.make_async_copy(value_hbm, w_value, sems.at[1]),
    ]
    for copy in copies:
        copy.start()
    for copy in copies:
        copy.wait()
    key = turn(jnp.dot(normed[...], w_key[...], preferred_element_type=f32), cosine[...], sine[...])
    value = jnp.dot(normed[...], w_value[...], preferred_element_type=f32).astype(bf16)
    for index, (rows, plain, padded) in enumerate(((key, key_n, key_d), (value, value_n, value_d))):
        new[index] = rows[:tok]
        plain[...] = rows[:tok]
        dec[index] = rows[tok : tok + DEC]
        padded[...] = rows[tok:]


def group_turned(keys, turned_query, turned_values, live):
    scores = jnp.dot(keys, turned_query, preferred_element_type=f32)
    top = jnp.max(
        scores if live is None else jnp.where(live, scores, neg_fill), axis=0, keepdims=True
    )
    weights = jnp.exp2((scores - top) * (HD ** (-0.5) * LOG2E))
    if live is not None:
        weights = jnp.where(live, weights, 0.0)
    total = jnp.sum(weights, axis=0, keepdims=True)
    acc = jnp.dot(turned_values, weights.astype(bf16), preferred_element_type=f32)
    return top * HD ** (-0.5), total, acc


def turned(values):
    return values.astype(f32).T.astype(bf16)


def attention_kernel(
    owner_ref, slot_ref, lens_ref, blk_ref, query_a, query_b, query_d, key_new, value_new, key_dec, value_dec,
    cache_k, cache_v, keep, send, dec, key_buf, value_buf, turn_a, turn_b, spread, dec_acc, dec_stats, sems,
):
    blocks, block_len, width = cache_k.shape
    heads = width // HD
    half = query_a.shape[0]
    tile = min(TILE, half)
    sides = ((turn_a, keep), (turn_b, send))

    def copies(index):
        return (
            pltpu.make_async_copy(cache_k.at[index], key_buf.at[index], sems.at[0, index]),
            pltpu.make_async_copy(cache_v.at[index], value_buf.at[index], sems.at[1, index]),
        )

    for index in range(blocks):
        for copy in copies(index):
            copy.start()

    for query, turn_ref in ((query_a, turn_a), (query_b, turn_b)):
        for row in range(0, half, tile):
            turn_ref[:, row : row + tile] = turned(query[row : row + tile, :width])

    def over_tiles(keys, values, body):
        for head in range(heads):
            key_head = keys[:, lanes(head)]
            value_head = turned(values[:, lanes(head)])
            for query, state in sides:
                for row in range(0, half, tile):
                    columns = slice(row, row + tile)
                    body(key_head, query[lanes(head), columns], value_head, state, columns, head)

    def start(keys, query, values, state, columns, head):
        top, total, acc = group_turned(keys, query, values, None)
        state[width + head : width + head + 1, columns] = top
        state[width + heads + head : width + heads + head + 1, columns] = total
        state[lanes(head), columns] = acc

    over_tiles(key_new, value_new, start)

    lines = lax.broadcasted_iota(jnp.int32, (DPAD, width), 1)
    spread[...] = jnp.zeros_like(spread)
    for head in range(heads):
        here = (lines >= head * HD) & (lines < (head + 1) * HD)
        spread[head * DPAD : (head + 1) * DPAD, :] = jnp.where(
            here, query_d[...].astype(f32), 0.0
        ).astype(bf16)
    dec_acc[...] = jnp.zeros_like(dec_acc)
    dec_stats[0:1, :] = jnp.full((1, HD), neg_fill, f32)
    dec_stats[1:, :] = jnp.zeros_like(dec_stats[1:, :])

    @pl.loop(0, blocks)
    def _(index):
        for copy in copies(index):
            copy.wait()
        owner = owner_ref[index]
        length = lens_ref[jnp.minimum(owner, REQS - 1)]
        count = jnp.clip(length - slot_ref[index] * block_len, 0, block_len)

        def add(live, keys, query, values, state, columns, head):
            top, total, acc = group_turned(keys, query, values, live)
            top_row = slice(width + head, width + head + 1)
            total_row = slice(width + heads + head, width + heads + head + 1)
            old_top = state[top_row, columns]
            best = jnp.maximum(old_top, top)
            old_scale = jnp.exp(old_top - best)
            scale = jnp.exp(top - best)
            state[top_row, columns] = best
            state[total_row, columns] = state[total_row, columns] * old_scale + total * scale
            state[lanes(head), columns] = state[lanes(head), columns] * old_scale + acc * scale

        @pl.when((owner < PRE) & (count == block_len))
        def _():
            over_tiles(key_buf.at[index], value_buf.at[index], functools.partial(add, None))

        @pl.when((owner < PRE) & (count < block_len))
        def _():
            live = lax.broadcasted_iota(jnp.int32, (block_len, tile), 0) < count
            over_tiles(key_buf.at[index], value_buf.at[index], functools.partial(add, live))

        @pl.when((owner >= PRE) & (owner < REQS))
        def _():
            shape = (block_len, HD)
            lane = lax.broadcasted_iota(jnp.int32, shape, 1)
            live = (lax.broadcasted_iota(jnp.int32, shape, 0) < count) & (
                lax.rem(lane, DPAD) == owner - PRE
            ) & (lane < heads * DPAD)
            scores = lax.dot_general(
                key_buf[index], spread[...], (((1,), (1,)), ((), ())), preferred_element_type=f32
            )
            top = jnp.max(jnp.where(live, scores, neg_fill), axis=0, keepdims=True)
            weights = jnp.where(live, jnp.exp2((scores - top) * (HD ** (-0.5) * LOG2E)), 0.0)
            top = top * HD ** (-0.5)
            total = jnp.sum(weights, axis=0, keepdims=True)
            mixed = lax.dot_general(
                value_buf[index], weights.astype(bf16), (((0,), (0,)), ((), ())), preferred_element_type=f32
            )
            place = lax.broadcasted_iota(jnp.int32, (HD, HD), 1)
            acc = jnp.zeros((HD, HD), f32)
            for head in range(heads):
                here = (place >= head * DPAD) & (place < (head + 1) * DPAD)
                acc = jnp.where(here, mixed[lanes(head)], acc)
            old_top = dec_stats[0:1, :]
            best = jnp.maximum(old_top, top)
            old_scale = jnp.exp(old_top - best)
            scale = jnp.exp(top - best)
            dec_stats[0:1, :] = best
            dec_stats[1:2, :] = dec_stats[1:2, :] * old_scale + total * scale
            dec_acc[...] = dec_acc[...] * old_scale + acc * scale

    mine = blk_ref[0] == 0
    plain = dec_acc[...].T
    stats = jnp.concatenate([dec_stats[...], jnp.zeros((HD - 8, HD), f32)], axis=0).T
    place = lax.broadcasted_iota(jnp.int32, (DPAD, HD), 1)
    packed = jnp.zeros((DPAD, HD), f32)
    for head in range(heads):
        rows = slice(head * DPAD, (head + 1) * DPAD)
        own = jnp.sum(
            query_d[:, lanes(head)].astype(f32) * key_dec[:, lanes(head)].astype(f32),
            axis=-1,
            keepdims=True,
        ) * HD ** (-0.5)
        own = jnp.where(mine, own, neg_fill)
        top = stats[rows, 0:1]
        best = jnp.maximum(top, own)
        scale = jnp.exp(top - best)
        own_scale = jnp.where(mine, jnp.exp(own - best), 0.0)
        packed = jnp.where(place == head, best, packed)
        packed = jnp.where(place == heads + head, stats[rows, 1:2] * scale + own_scale, packed)
        dec[:, lanes(head)] = plain[rows] * scale + value_dec[:, lanes(head)].astype(f32) * own_scale
    dec[:, width:] = packed


def attention(query_a, query_b, query_d, new, cache_keys, cache_values, scalars):
    half = query_a.shape[0]
    blocks, block_len, width = cache_keys.shape
    heads = width // HD
    state = ((width + 2 * heads, half), f32)
    return call(
        attention_kernel,
        (state, state, ((DPAD, width + HD), f32)),
        [SMEM] * 4 + [VMEM] * 7 + [HBM] * 2,
        (*scalars, query_a, query_b, query_d, *new, cache_keys, cache_values),
        "attention",
        24,
        [
            pltpu.VMEM((blocks, block_len, width), bf16),
            pltpu.VMEM((blocks, block_len, width), bf16),
            pltpu.VMEM((width, half), bf16),
            pltpu.VMEM((width, half), bf16),
            pltpu.VMEM((HD, width), bf16),
            pltpu.VMEM((HD, HD), f32),
            pltpu.VMEM((8, HD), f32),
            pltpu.SemaphoreType.DMA((2, blocks)),
        ],
    )


def split(values):
    high = values.astype(bf16).astype(f32)
    middle = (values - high).astype(bf16).astype(f32)
    return high, middle, (values - high) - middle


def merge_core_kernel(mine, other, dec_mine, dec_other, *outs):
    full = dec_mine.shape[1]
    width = full - HD
    heads = width // HD
    half = mine.shape[1]
    tok = half // len(outs)

    def put(where, turned, dec):
        value = turned.T.astype(bf16)
        for index, out in enumerate(outs):
            out[0:tok, where] = value[index * tok : (index + 1) * tok]
            out[tok : tok + DPAD, where] = dec.astype(bf16)

    place = lax.broadcasted_iota(jnp.int32, (DPAD, HD), 1)
    packed = jnp.zeros((DPAD, HD), f32)
    stats_a = dec_mine[:, width:]
    stats_b = dec_other[:, width:]
    top_rows = slice(width, width + heads)
    total_rows = slice(width + heads, width + 2 * heads)
    best = jnp.maximum(mine[top_rows, :], other[top_rows, :])
    scale_a = jnp.exp(mine[top_rows, :] - best)
    scale_b = jnp.exp(other[top_rows, :] - best)
    total = mine[total_rows, :] * scale_a + other[total_rows, :] * scale_b
    for head in range(heads):
        one = slice(head, head + 1)
        two = slice(heads + head, heads + head + 1)
        turned = mine[lanes(head), :] * scale_a[one] + other[lanes(head), :] * scale_b[one]
        dec_best = jnp.maximum(stats_a[:, one], stats_b[:, one])
        dec_a = jnp.exp(stats_a[:, one] - dec_best)
        dec_b = jnp.exp(stats_b[:, one] - dec_best)
        packed = jnp.where(place == head, dec_best, packed)
        packed = jnp.where(place == heads + head, stats_a[:, two] * dec_a + stats_b[:, two] * dec_b, packed)
        put(lanes(head), turned, dec_mine[:, lanes(head)] * dec_a + dec_other[:, lanes(head)] * dec_b)
    coded = [*split(jnp.concatenate([best, total], axis=0))]
    coded.append(jnp.zeros((HD - 6 * heads, half), f32))
    high, middle, low = split(packed)
    put(
        slice(width, full),
        jnp.concatenate(coded, axis=0),
        high + pltpu.roll(middle, 2 * heads, 1) + pltpu.roll(low, 4 * heads, 1),
    )


def merge_core(mine, other, dec_mine, dec_other, parts):
    full = dec_mine.shape[1]
    tok = mine.shape[1] // parts
    return call(
        merge_core_kernel,
        (((tok + DPAD, full), bf16),) * parts,
        [VMEM] * 4,
        (mine, other, dec_mine, dec_other),
        "merge_core",
        12,
    )


def load_kernel(count, *refs):
    sources, targets, sems = refs[:count], refs[count + 1 : -1], refs[-1]
    copies = []
    for source, target in zip(sources, targets):
        depth = source.shape[-2] // 4
        for lead in range(source.shape[0]) if len(source.shape) == 3 else (None,):
            for part in range(4):
                here = pl.ds(part * depth, depth)
                where = here if lead is None else (lead, here)
                copies.append(
                    pltpu.make_async_copy(source.at[where], target.at[where], sems.at[len(copies)])
                )
    for copy in copies:
        copy.start()
    for copy in copies:
        copy.wait()


def load(arrays, after, name):
    size = sum(arr.size for arr in arrays) * 2
    count = sum(4 * (arr.shape[0] if arr.ndim == 3 else 1) for arr in arrays)
    return call(
        functools.partial(load_kernel, len(arrays)),
        tuple((arr.shape, arr.dtype) for arr in arrays),
        [HBM] * len(arrays) + [VMEM],
        (*arrays, after),
        name,
        1,
        [pltpu.SemaphoreType.DMA((count,))],
        pl.CostEstimate(flops=0, transcendentals=0, bytes_accessed=2 * size),
    )


def project_kernel(parts, head_ref, *refs):
    pieces = refs[:parts]
    weight = refs[parts]
    outs = refs[parts + 1 : -2]
    arranged, product = refs[-2:]
    rows, full = pieces[0].shape
    width = full - HD
    heads = width // HD
    group_rows = outs[0].shape[0]
    places = len(outs)
    share = (rows - DPAD) // places
    dec_share = DEC // places
    stats = []
    for piece in pieces:
        coded = piece[:, width:].astype(f32)
        stats.append(
            (coded + pltpu.roll(coded, HD - 2 * heads, 1)) + pltpu.roll(coded, HD - 4 * heads, 1)
        )
    arranged[...] = jnp.zeros_like(arranged)
    for head in range(heads):
        tops = [s[:, head : head + 1] for s in stats]
        best = functools.reduce(jnp.maximum, tops)
        scales = [jnp.exp(top - best) for top in tops]
        total = tree_sum([s[:, heads + head : heads + head + 1] * c for s, c in zip(stats, scales)])
        acc = tree_sum([piece[:, lanes(head)].astype(f32) * c for piece, c in zip(pieces, scales)])
        attended = acc / total
        for place in range(places):
            row = group_rows * place
            arranged[row : row + share, lanes(head)] = attended[share * place : share * (place + 1)]
            start = rows - DPAD + dec_share * place
            arranged[row + share : row + share + dec_share, lanes(head)] = attended[start : start + dec_share]
    product[...] = jnp.dot(arranged[...].astype(bf16), weight[...], preferred_element_type=f32)
    for offset, out in enumerate(outs):
        out[...] = product[span(lax.bitwise_xor(head_ref[0], offset), group_rows), :].astype(out.dtype)


def project_out(pieces, w_output, head_index, head_count):
    rows = pieces[0].shape[0]
    share = (rows - DPAD) // head_count + 8
    width, columns = w_output.shape
    return call(
        functools.partial(project_kernel, len(pieces)),
        (((share, columns), f32),) + (((share, columns), bf16),) * (head_count - 1),
        [SMEM] + [VMEM] * (len(pieces) + 1),
        (head_index, *pieces, w_output),
        "project_out",
        8,
        [pltpu.VMEM((share * head_count, width), f32), pltpu.VMEM((share * head_count, columns), f32)],
    )


def norm_kernel(parts, head_ref, pre_hbm, dec_pad, gain, *refs):
    arrived = refs[:parts]
    tokens, dec = refs[parts : parts + 2]
    mids = refs[parts + 2 : 2 * parts + 2]
    rows, mid, sem = refs[2 * parts + 2 :]
    share = rows.shape[0]
    head = head_ref[0]
    copy = pltpu.make_async_copy(pre_hbm.at[span(head, share)], rows, sem)
    copy.start()
    total = tree_sum([part[...].astype(f32) for part in arrived])
    copy.wait()
    mid[0:share, :] = rows[...].astype(f32) + total[:share]
    mid[share:, :] = dec_pad[span(head, 8), :] + total[share:]
    for offset, out in enumerate(mids):
        out[...] = mid[:, span(lax.bitwise_xor(head, offset), out.shape[1])]
    values = mid[...]
    meansq = jnp.mean(values * values, axis=-1, keepdims=True)
    scaled = values * lax.rsqrt(meansq + eps_norm) * gain[...]
    tokens[...] = scaled[:share].astype(bf16)
    dec[...] = scaled[share:].astype(bf16)


def experts_kernel(offsets, chunks, chips, scalar_ref, *refs):
    count = len(offsets)
    data = refs[:count]
    query, table_d = refs[count : count + 2]
    weights = refs[count + 2 : count + 8]
    outs = refs[count + 8 : count + 8 + chunks]
    rows_in, table = refs[count + 8 + chunks :]
    each = weights[0].shape[0]
    experts = 2 * each
    piece, depth = data[0].shape
    width = depth // chunks
    long = piece - 8
    share = long // chips
    tok = share * chunks
    base = query.shape[1] - table_d.shape[1]
    rows = count * piece
    tile = rows if rows <= 320 else piece
    places = [lax.bitwise_xor(scalar_ref[0], offset) for offset in range(chunks)]
    for index, offset in enumerate(offsets):
        rows_in[long * index : long * (index + 1), :] = data[index][:long, :]
        row = long * count + 8 * index
        rows_in[row : row + 8, :] = data[index][long:, :]
        table[row : row + 8, :] = table_d[span(places[offset], 8), :]
        for chip in range(chips):
            row = long * index + share * chip
            start = pl.multiple_of(tok * chip + share * places[offset], share)
            table[row : row + share, :] = query[pl.ds(start, share), base:].astype(f32)
    lane = lax.broadcasted_iota(jnp.int32, (tile, table.shape[1]), 1)
    found = {}
    for row in range(0, rows, tile):
        here = slice(row, row + tile)
        block = rows_in[here, :]
        for expert in range(experts):
            w_gate, w_up, _ = weights[:3] if expert < each else weights[3:]
            local = expert % each
            number = lax.bitwise_xor(scalar_ref[1], expert // each) * each + local
            gate = jnp.dot(block, w_gate[local], preferred_element_type=f32)
            up = jnp.dot(block, w_up[local], preferred_element_type=f32)
            act = (gate / (1.0 + jnp.exp(-gate)) * up).astype(bf16)
            factor = jnp.sum(jnp.where(lane == number, table[here, :], 0.0), axis=-1, keepdims=True)
            found[row, expert] = act, factor
    dec_share = DEC // chunks
    for out, place in zip(outs, places):
        values = []
        for row in range(0, rows, tile):
            sums = []
            for first in (0, each):
                total = None
                for expert in range(first, first + each):
                    act, factor = found[row, expert]
                    w_down = weights[2 if first == 0 else 5]
                    down = jnp.dot(
                        act, w_down[expert % each, :, span(place, width)], preferred_element_type=f32
                    )
                    down = down.astype(bf16).astype(f32) * factor
                    total = down if total is None else total + down
                sums.append(total)
            values.append(sums[0] + sums[1])
        value = values[0] if len(values) == 1 else jnp.concatenate(values, axis=0)
        out[: long * count, :] = value[: long * count].astype(bf16)
        out[long * count :, :] = jnp.zeros_like(out[long * count :, :])
        for index in range(count):
            start = long * count + 8 * index
            row = long * count + dec_share * index
            out[row : row + dec_share, :] = value[start : start + dec_share].astype(bf16)


def run_experts(data, offsets, query, table_d, weights, scalars, chips, chunks, name):
    count = len(data)
    piece, depth = data[0].shape
    width = depth // chunks
    tail = -(-(DEC // chunks) * count // 8) * 8
    return list(
        call(
            functools.partial(experts_kernel, offsets, chunks, chips),
            ((((piece - 8) * count + tail, width), bf16),) * chunks,
            [SMEM] + [VMEM] * (count + 8),
            (scalars, *data, query, table_d, *weights),
            name,
            28,
            [
                pltpu.VMEM((count * piece, depth), bf16),
                pltpu.VMEM((count * piece, table_d.shape[1]), f32),
            ],
            pl.CostEstimate(
                flops=12 * count * piece * depth * weights[0].shape[2],
                transcendentals=0,
                bytes_accessed=2 * sum(w.size for w in weights),
            ),
        )
    )


def head_sum_kernel(parts, share, *refs):
    early, late, outs = refs[:parts], refs[parts : 2 * parts], refs[2 * parts :]
    chips = len(outs)
    long = share * chips
    tok = share * parts
    dec_share = DEC // parts
    for out in outs:
        out[tok:, :] = jnp.zeros_like(out[tok:, :])
    for mine in range(parts):
        found, found_d = [], []
        for sender in range(parts):
            index = mine ^ sender
            source, count = early[sender], parts - 1
            if index == parts - 1:
                source, index, count = late[sender], 0, 1
            found.append(source[long * index : long * (index + 1), :].astype(f32))
            row = long * count + dec_share * index
            found_d.append(source[row : row + dec_share, :].astype(f32))
        total = tree_sum(found).astype(bf16)
        total_d = tree_sum(found_d).astype(bf16)
        for chip, out in enumerate(outs):
            out[share * mine : share * (mine + 1), :] = total[share * chip : share * (chip + 1)]
            out[tok + dec_share * mine : tok + dec_share * (mine + 1), :] = total_d


def final_kernel(parts, head_ref, *refs):
    mids, pieces = refs[:parts], refs[parts:-4]
    hidden, dec, packed, placed = refs[-4:]
    tok = hidden.shape[0]
    share = tok // parts
    dec_share = DEC // parts
    total = tree_sum([piece[...].astype(f32) for piece in pieces])
    packed[...] = jnp.zeros_like(packed)
    for offset, mid in enumerate(mids):
        place = lax.bitwise_xor(head_ref[0], offset)
        hidden[span(place, share), :] = (
            mid[0:share, :] + total[share * offset : share * (offset + 1)]
        ).astype(bf16)
        start = tok + dec_share * offset
        packed[8 * offset : 8 * offset + dec_share, :] = (
            mid[share : share + dec_share, :] + total[start : start + dec_share]
        )
        placed[span(place, 8), :] = packed[8 * offset : 8 * offset + 8, :]
    for place in range(parts):
        dec[dec_share * place : dec_share * (place + 1), :] = placed[
            8 * place : 8 * place + dec_share, :
        ].astype(bf16)


def per_device(
    pre_tokens, dec_tokens, attn_gain, w_query, w_key, w_value, w_output, cache_keys, cache_values,
    block_request, block_slot, cache_lens, moe_gain, expert_ids, expert_gates, dec_expert_ids,
    dec_expert_gates, w_gate, w_up, w_down,
):
    tok, model_width = pre_tokens.shape
    width = w_query.shape[1]
    blk_count = lax.axis_size("blk")
    blk_index = lax.axis_index("blk").astype(jnp.int32)
    head_count = lax.axis_size("head")
    head_index = lax.axis_index("head").astype(jnp.int32)
    chips = blk_count // 2
    head_scalar = head_index.reshape(1)
    scalars = jnp.stack([head_index, blk_index])
    part_width = model_width // head_count
    tables = -(-w_gate.shape[0] * blk_count // HD) * HD
    rows = tok + DPAD

    row = jnp.arange(rows, dtype=jnp.int32)
    request = jnp.maximum(row - tok + PRE, 0)[:, None] == jnp.arange(REQS, dtype=jnp.int32)
    positions = jnp.sum(jnp.where(request, cache_lens, 0), axis=1)
    positions = positions + jnp.where(row < tok, blk_index * tok + row, 0)
    frequencies = rope_base ** (-jnp.arange(HD // 2, dtype=f32) / (HD // 2))
    angles = positions.astype(f32)[:, None] * frequencies[None, :]
    cosine = jnp.cos(angles)
    sine = jnp.sin(angles)
    cosine = jnp.concatenate([cosine, cosine], axis=1)
    sine = jnp.concatenate([-sine, sine], axis=1)

    dec_rows = 8 * head_count
    sources = (
        pre_tokens, dec_tokens, attn_gain[None, :], w_query,
        expert_ids.T, expert_gates.T, dec_expert_ids.T, dec_expert_gates.T,
    )
    message, query_d, table_d, normed, dec_pad = call(
        query_kernel,
        (
            ((tok, width + tables), bf16),
            ((DPAD, width), bf16),
            ((dec_rows, tables), f32),
            ((rows, model_width), bf16),
            ((dec_rows, model_width), f32),
        ),
        [HBM] * 8 + [VMEM] * 2,
        (*sources, cosine, sine),
        "queries",
        16,
        [
            *(pltpu.VMEM(source.shape, source.dtype) for source in sources),
            pltpu.VMEM((dec_rows, model_width), f32),
            pltpu.SemaphoreType.DMA((len(sources) + 3,)),
        ],
    )

    def exchange(pieces, axis, step):
        return [pieces[0]] + [swap(pieces[o], axis, step * o) for o in range(1, len(pieces))]

    new_cache, dec_cache, *new = call(
        key_kernel,
        (
            ((2, tok, width), bf16),
            ((2, DEC, width), bf16),
            ((tok, width), bf16),
            ((tok, width), bf16),
            ((DPAD, width), bf16),
            ((DPAD, width), bf16),
        ),
        [VMEM] + [HBM] * 2 + [VMEM] * 2,
        (normed, w_key, w_value, cosine, sine),
        "keys",
        16,
        [
            pltpu.VMEM(w_key.shape, bf16),
            pltpu.VMEM(w_value.shape, bf16),
            pltpu.SemaphoreType.DMA((2,)),
        ],
        pl.CostEstimate(
            flops=4 * rows * model_width * width,
            transcendentals=0,
            bytes_accessed=4 * model_width * width,
        ),
    )
    gate_other = swap(w_gate, "blk", 1)
    pieces = exchange([message] * chips, "blk", 2)
    new_cache, *pieces = lax.optimization_barrier((new_cache, *pieces))
    query_a = jnp.concatenate(pieces, axis=0)
    query_b = swap(query_a, "blk", 1)
    query_b, gate_other = lax.optimization_barrier((query_b, gate_other))

    keep, send, dec = attention(
        query_a, query_b, query_d, new, cache_keys, cache_values,
        (block_request, block_slot, cache_lens, blk_index.reshape(1)),
    )
    pieces = merge_core(keep, swap(send, "blk", 1), dec, swap(dec, "blk", 1), chips)
    *pieces, up_source = lax.optimization_barrier((*pieces, w_up))
    up_other = swap(up_source, "blk", 1)
    (weight,) = load((w_output,), pieces[0], "load_output")
    pieces = exchange(pieces, "blk", 2)
    pieces[-1], weight, up_other = lax.optimization_barrier((pieces[-1], weight, up_other))
    partial = project_out(pieces, weight, head_scalar, head_count)
    *partial, down_source = lax.optimization_barrier((*partial, w_down))
    down_other = swap(down_source, "blk", 1)
    partial = exchange(partial, "head", 1)
    partial[-1], down_other = lax.optimization_barrier((partial[-1], down_other))
    share = tok // head_count
    moe_tok, moe_dec, *mids = call(
        functools.partial(norm_kernel, head_count),
        (
            ((share, model_width), bf16),
            ((8, model_width), bf16),
            *(((share + 8, part_width), f32),) * head_count,
        ),
        [SMEM, HBM] + [VMEM] * (2 + head_count),
        (head_scalar, pre_tokens, dec_pad, moe_gain[None, :], *partial),
        "moe_norm",
        8,
        [
            pltpu.VMEM((share, model_width), bf16),
            pltpu.VMEM((share + 8, model_width), f32),
            pltpu.SemaphoreType.DMA,
        ],
    )
    spread = exchange([moe_tok] * chips, "blk", 2)
    mids[1:-1] = [swap(mids[o], "head", o) for o in range(1, head_count - 1)]
    spread[-1], *mids[1:-1] = lax.optimization_barrier((spread[-1], *mids[1:-1]))
    gathered = jnp.concatenate([*spread, moe_dec], axis=0)
    data = [gathered, swap(gathered, "head", 1), swap(gathered, "head", 2)]
    weights = load((w_gate, w_up, w_down), gathered, "load_experts")
    data[1], data[2], *weights = lax.optimization_barrier((data[1], data[2], *weights))
    cut = gathered.shape[0] // 16 * 8
    relayed = [swap(data[1][:cut], "head", 2), swap(data[2][cut:], "head", 1)]
    data.append(jnp.concatenate(relayed, axis=0))
    weights = (*weights, gate_other, up_other, down_other)
    offsets = tuple(range(head_count))
    shared = (query_a, table_d, weights, scalars, chips, head_count)
    early = run_experts(data[:-1], offsets[:-1], *shared, "experts_early")
    late = run_experts(data[-1:], offsets[-1:], *shared, "experts_late")
    early = exchange(early, "head", 1)
    late[1], early[1] = lax.optimization_barrier((late[1], early[1]))
    late = exchange(late, "head", 1)
    final = call(
        functools.partial(head_sum_kernel, head_count, share),
        (((rows, part_width), bf16),) * chips,
        [VMEM] * (2 * head_count),
        (*early, *late),
        "head_sum",
        8,
    )
    final = list(final)
    *final, mids[-1] = lax.optimization_barrier((*final, mids[-1]))
    final = exchange(final, "blk", 2)
    mids[-1] = swap(mids[-1], "head", head_count - 1)
    hidden, dec_hidden = call(
        functools.partial(final_kernel, head_count),
        (((tok, part_width), bf16), ((DEC, part_width), bf16)),
        [SMEM] + [VMEM] * (head_count + chips),
        (head_scalar, *mids, *final),
        "final",
        8,
        [pltpu.VMEM((dec_rows, part_width), f32), pltpu.VMEM((dec_rows, part_width), f32)],
    )
    return (hidden, dec_hidden, new_cache, dec_cache)


def solution(mesh):
    placed = (
        P("blk", None),
        P(),
        P(),
        P(None, "head"),
        P(None, "head"),
        P(None, "head"),
        P("head", None),
        P("blk", None, "head"),
        P("blk", None, "head"),
        P("blk"),
        P("blk"),
        P(),
        P(),
        P("blk", None),
        P("blk", None),
        P(),
        P(),
        P("blk", None, "head"),
        P("blk", None, "head"),
        P("blk", "head", None),
    )
    return jax.shard_map(
        per_device,
        mesh=mesh,
        in_specs=placed,
        out_specs=(
            P("blk", "head"),
            P(None, "head"),
            P(None, "blk", "head"),
            P(None, None, "head"),
        ),
        check_vma=False,
    )
```

```python
import functools

import jax
import jax.numpy as jnp
from jax import lax
from jax.experimental import pallas as pl
from jax.experimental.pallas import tpu as pltpu
from jax.sharding import PartitionSpec as P

HD = 128
PRE = 1
DEC = 12
REQS = 13
DPAD = 16
TILE = 256

eps_norm = 1e-06
rope_base = 50000.0
neg_fill = -1e30
LOG2E = 1.4426950408889634
bf16 = jnp.bfloat16
f32 = jnp.float32


def swap(value, axis, mask):
    count = lax.axis_size(axis)
    return lax.ppermute(value, axis, [(i, i ^ mask) for i in range(count)])


def span(index, size):
    return pl.ds(pl.multiple_of(index * size, size), size)


def lanes(head):
    return slice(head * HD, (head + 1) * HD)


def tree_sum(values):
    values = list(values)
    while len(values) > 1:
        values = [a + b for a, b in zip(values[::2], values[1::2])]
    return values[0]


VMEM = pl.BlockSpec(memory_space=pltpu.VMEM)
SMEM = pl.BlockSpec(memory_space=pltpu.SMEM)
HBM = pl.BlockSpec(memory_space=pltpu.HBM)


def call(body, outs, ins, args, name, limit, scratch=(), cost=None):
    args = [
        pltpu.with_memory_space_constraint(arg, pltpu.HBM) if spec is HBM else arg
        for spec, arg in zip(ins, args)
    ]
    return pl.pallas_call(
        body,
        out_shape=tuple(jax.ShapeDtypeStruct(shape, dtype) for shape, dtype in outs),
        in_specs=list(ins),
        out_specs=tuple(VMEM for _ in outs),
        scratch_shapes=list(scratch),
        compiler_params=pltpu.CompilerParams(vmem_limit_bytes=limit << 20),
        cost_estimate=cost,
        name=name,
    )(*args)


def turn(flat, cosine, sine):
    heads = []
    for head in range(flat.shape[1] // HD):
        block = flat[:, lanes(head)]
        heads.append(block * cosine + pltpu.roll(block, HD // 2, 1) * sine)
    return jnp.concatenate(heads, axis=1).astype(bf16)


def gate_lanes(ids, gates, width):
    names = ids[...]
    values = gates[...].astype(f32)
    place = lax.broadcasted_iota(jnp.int32, (width, names.shape[1]), 0)
    table = jnp.zeros(place.shape, f32)
    for k in range(names.shape[0]):
        table = jnp.where(place == names[k : k + 1], values[k : k + 1], table)
    shape = (width, width)
    eye = lax.broadcasted_iota(jnp.int32, shape, 0) == lax.broadcasted_iota(jnp.int32, shape, 1)
    return lax.dot_general(
        table.astype(bf16),
        eye.astype(f32).astype(bf16),
        (((0,), (0,)), ((), ())),
        preferred_element_type=f32,
    )


def query_kernel(
    pre_hbm, dec_hbm, gain_hbm, weight_hbm, ids_hbm, gates_hbm, dec_ids_hbm, dec_gates_hbm, cosine, sine,
    message, query_d, table_d, normed, dec_pad,
    pre, dec, gain, weight, ids, gates, dec_ids, dec_gates, rows, sems,
):
    sources = (pre_hbm, dec_hbm, gain_hbm, ids_hbm, gates_hbm, dec_ids_hbm, dec_gates_hbm)
    targets = (pre, dec, gain, ids, gates, dec_ids, dec_gates)
    copies = [
        pltpu.make_async_copy(source, target, sems.at[index])
        for index, (source, target) in enumerate(zip(sources, targets))
    ]
    depth = weight.shape[0] // 4
    for part in range(4):
        here = pl.ds(part * depth, depth)
        copies.append(
            pltpu.make_async_copy(weight_hbm.at[here], weight.at[here], sems.at[len(sources) + part])
        )
    for copy in copies:
        copy.start()
    tok = pre.shape[0]
    width = weight.shape[1]
    heads = dec_pad.shape[0] // 8
    share = DEC // heads
    for copy in copies[:7]:
        copy.wait()

    def norm(values):
        meansq = jnp.mean(values * values, axis=-1, keepdims=True)
        return (values * lax.rsqrt(meansq + eps_norm) * gain[...]).astype(bf16)

    dec_rows = dec[...].astype(f32)
    normed[0:tok, :] = norm(pre[...].astype(f32))
    normed[tok:, :] = jnp.zeros_like(normed[tok:, :])
    normed[tok : tok + DEC, :] = norm(dec_rows)
    dec_table = gate_lanes(dec_ids, dec_gates, table_d.shape[1])
    message[:, width:] = gate_lanes(ids, gates, message.shape[1] - width).astype(bf16)
    for out, source in ((dec_pad, dec_rows), (table_d, dec_table)):
        rows[...] = jnp.zeros_like(rows)
        for head in range(heads):
            rows[8 * head : 8 * head + share, : source.shape[1]] = source[share * head : share * (head + 1)]
        out[...] = rows[:, : source.shape[1]].astype(out.dtype)
    for copy in copies[7:]:
        copy.wait()
    query = jnp.dot(normed[...], weight[...], preferred_element_type=f32)
    query = turn(query, cosine[...], sine[...])
    message[:, :width] = query[:tok]
    query_d[...] = query[tok:]


def key_kernel(
    normed, key_hbm, value_hbm, cosine, sine, new, dec, key_n, value_n, key_d, value_d, w_key, w_value, sems
):
    tok = new.shape[1]
    copies = [
        pltpu.make_async_copy(key_hbm, w_key, sems.at[0]),
        pltpu.make_async_copy(value_hbm, w_value, sems.at[1]),
    ]
    for copy in copies:
        copy.start()
    for copy in copies:
        copy.wait()
    key = turn(jnp.dot(normed[...], w_key[...], preferred_element_type=f32), cosine[...], sine[...])
    value = jnp.dot(normed[...], w_value[...], preferred_element_type=f32).astype(bf16)
    for index, (rows, plain, padded) in enumerate(((key, key_n, key_d), (value, value_n, value_d))):
        new[index] = rows[:tok]
        plain[...] = rows[:tok]
        dec[index] = rows[tok : tok + DEC]
        padded[...] = rows[tok:]


def group_turned(keys, turned_query, turned_values, live):
    scores = jnp.dot(keys, turned_query, preferred_element_type=f32)
    top = jnp.max(
        scores if live is None else jnp.where(live, scores, neg_fill), axis=0, keepdims=True
    )
    weights = jnp.exp2((scores - top) * (HD ** (-0.5) * LOG2E))
    if live is not None:
        weights = jnp.where(live, weights, 0.0)
    total = jnp.sum(weights, axis=0, keepdims=True)
    acc = jnp.dot(turned_values, weights.astype(bf16), preferred_element_type=f32)
    return top * HD ** (-0.5), total, acc


def turned(values):
    return values.astype(f32).T.astype(bf16)


def attention_kernel(
    owner_ref, slot_ref, lens_ref, blk_ref, query_a, query_b, query_d, key_new, value_new, key_dec, value_dec,
    cache_k, cache_v, keep, send, dec, key_buf, value_buf, turn_a, turn_b, spread, dec_acc, dec_stats, sems,
):
    blocks, block_len, width = cache_k.shape
    heads = width // HD
    half = query_a.shape[0]
    tile = min(TILE, half)
    sides = ((turn_a, keep), (turn_b, send))

    def copies(index):
        return (
            pltpu.make_async_copy(cache_k.at[index], key_buf.at[index], sems.at[0, index]),
            pltpu.make_async_copy(cache_v.at[index], value_buf.at[index], sems.at[1, index]),
        )

    for index in range(blocks):

        @pl.when(owner_ref[index] < REQS)
        def _():
            for copy in copies(index):
                copy.start()

    for query, turn_ref in ((query_a, turn_a), (query_b, turn_b)):
        for row in range(0, half, tile):
            turn_ref[:, row : row + tile] = turned(query[row : row + tile, :width])

    def over_tiles(keys, values, body):
        for head in range(heads):
            key_head = keys[:, lanes(head)]
            value_head = turned(values[:, lanes(head)])
            for query, state in sides:
                for row in range(0, half, tile):
                    columns = slice(row, row + tile)
                    body(key_head, query[lanes(head), columns], value_head, state, columns, head)

    def start(keys, query, values, state, columns, head):
        top, total, acc = group_turned(keys, query, values, None)
        state[width + head : width + head + 1, columns] = top
        state[width + heads + head : width + heads + head + 1, columns] = total
        state[lanes(head), columns] = acc

    over_tiles(key_new, value_new, start)

    lines = lax.broadcasted_iota(jnp.int32, (DPAD, width), 1)
    spread[...] = jnp.zeros_like(spread)
    for head in range(heads):
        here = (lines >= head * HD) & (lines < (head + 1) * HD)
        spread[head * DPAD : (head + 1) * DPAD, :] = jnp.where(
            here, query_d[...].astype(f32), 0.0
        ).astype(bf16)
    dec_acc[...] = jnp.zeros_like(dec_acc)
    dec_stats[0:1, :] = jnp.full((1, HD), neg_fill, f32)
    dec_stats[1:, :] = jnp.zeros_like(dec_stats[1:, :])

    @pl.loop(0, blocks)
    def _(index):
        owner = owner_ref[index]

        @pl.when(owner < REQS)
        def _():
            for copy in copies(index):
                copy.wait()

        length = lens_ref[jnp.minimum(owner, REQS - 1)]
        count = jnp.clip(length - slot_ref[index] * block_len, 0, block_len)

        def add(live, keys, query, values, state, columns, head):
            top, total, acc = group_turned(keys, query, values, live)
            top_row = slice(width + head, width + head + 1)
            total_row = slice(width + heads + head, width + heads + head + 1)
            old_top = state[top_row, columns]
            best = jnp.maximum(old_top, top)
            old_scale = jnp.exp(old_top - best)
            scale = jnp.exp(top - best)
            state[top_row, columns] = best
            state[total_row, columns] = state[total_row, columns] * old_scale + total * scale
            state[lanes(head), columns] = state[lanes(head), columns] * old_scale + acc * scale

        @pl.when((owner < PRE) & (count == block_len))
        def _():
            over_tiles(key_buf.at[index], value_buf.at[index], functools.partial(add, None))

        @pl.when((owner < PRE) & (count < block_len))
        def _():
            live = lax.broadcasted_iota(jnp.int32, (block_len, tile), 0) < count
            over_tiles(key_buf.at[index], value_buf.at[index], functools.partial(add, live))

        @pl.when((owner >= PRE) & (owner < REQS))
        def _():
            shape = (block_len, HD)
            lane = lax.broadcasted_iota(jnp.int32, shape, 1)
            live = (lax.broadcasted_iota(jnp.int32, shape, 0) < count) & (
                lax.rem(lane, DPAD) == owner - PRE
            ) & (lane < heads * DPAD)
            scores = lax.dot_general(
                key_buf[index], spread[...], (((1,), (1,)), ((), ())), preferred_element_type=f32
            )
            top = jnp.max(jnp.where(live, scores, neg_fill), axis=0, keepdims=True)
            weights = jnp.where(live, jnp.exp2((scores - top) * (HD ** (-0.5) * LOG2E)), 0.0)
            top = top * HD ** (-0.5)
            total = jnp.sum(weights, axis=0, keepdims=True)
            mixed = lax.dot_general(
                value_buf[index], weights.astype(bf16), (((0,), (0,)), ((), ())), preferred_element_type=f32
            )
            place = lax.broadcasted_iota(jnp.int32, (HD, HD), 1)
            acc = jnp.zeros((HD, HD), f32)
            for head in range(heads):
                here = (place >= head * DPAD) & (place < (head + 1) * DPAD)
                acc = jnp.where(here, mixed[lanes(head)], acc)
            old_top = dec_stats[0:1, :]
            best = jnp.maximum(old_top, top)
            old_scale = jnp.exp(old_top - best)
            scale = jnp.exp(top - best)
            dec_stats[0:1, :] = best
            dec_stats[1:2, :] = dec_stats[1:2, :] * old_scale + total * scale
            dec_acc[...] = dec_acc[...] * old_scale + acc * scale

    mine = blk_ref[0] == 0
    plain = dec_acc[...].T
    stats = jnp.concatenate([dec_stats[...], jnp.zeros((HD - 8, HD), f32)], axis=0).T
    place = lax.broadcasted_iota(jnp.int32, (DPAD, HD), 1)
    packed = jnp.zeros((DPAD, HD), f32)
    for head in range(heads):
        rows = slice(head * DPAD, (head + 1) * DPAD)
        own = jnp.sum(
            query_d[:, lanes(head)].astype(f32) * key_dec[:, lanes(head)].astype(f32),
            axis=-1,
            keepdims=True,
        ) * HD ** (-0.5)
        own = jnp.where(mine, own, neg_fill)
        top = stats[rows, 0:1]
        best = jnp.maximum(top, own)
        scale = jnp.exp(top - best)
        own_scale = jnp.where(mine, jnp.exp(own - best), 0.0)
        packed = jnp.where(place == head, best, packed)
        packed = jnp.where(place == heads + head, stats[rows, 1:2] * scale + own_scale, packed)
        dec[:, lanes(head)] = plain[rows] * scale + value_dec[:, lanes(head)].astype(f32) * own_scale
    dec[:, width:] = packed


def attention(query_a, query_b, query_d, new, cache_keys, cache_values, scalars):
    half = query_a.shape[0]
    blocks, block_len, width = cache_keys.shape
    heads = width // HD
    state = ((width + 2 * heads, half), f32)
    return call(
        attention_kernel,
        (state, state, ((DPAD, width + HD), f32)),
        [SMEM] * 4 + [VMEM] * 7 + [HBM] * 2,
        (*scalars, query_a, query_b, query_d, *new, cache_keys, cache_values),
        "attention",
        24,
        [
            pltpu.VMEM((blocks, block_len, width), bf16),
            pltpu.VMEM((blocks, block_len, width), bf16),
            pltpu.VMEM((width, half), bf16),
            pltpu.VMEM((width, half), bf16),
            pltpu.VMEM((HD, width), bf16),
            pltpu.VMEM((HD, HD), f32),
            pltpu.VMEM((8, HD), f32),
            pltpu.SemaphoreType.DMA((2, blocks)),
        ],
    )


def split(values):
    high = values.astype(bf16).astype(f32)
    middle = (values - high).astype(bf16).astype(f32)
    return high, middle, (values - high) - middle


def merge_core_kernel(mine, other, dec_mine, dec_other, *outs):
    full = dec_mine.shape[1]
    width = full - HD
    heads = width // HD
    half = mine.shape[1]
    tok = half // len(outs)

    def put(where, turned, dec):
        value = turned.T.astype(bf16)
        for index, out in enumerate(outs):
            out[0:tok, where] = value[index * tok : (index + 1) * tok]
            out[tok : tok + DPAD, where] = dec.astype(bf16)

    place = lax.broadcasted_iota(jnp.int32, (DPAD, HD), 1)
    packed = jnp.zeros((DPAD, HD), f32)
    stats_a = dec_mine[:, width:]
    stats_b = dec_other[:, width:]
    top_rows = slice(width, width + heads)
    total_rows = slice(width + heads, width + 2 * heads)
    best = jnp.maximum(mine[top_rows, :], other[top_rows, :])
    scale_a = jnp.exp(mine[top_rows, :] - best)
    scale_b = jnp.exp(other[top_rows, :] - best)
    total = mine[total_rows, :] * scale_a + other[total_rows, :] * scale_b
    for head in range(heads):
        one = slice(head, head + 1)
        two = slice(heads + head, heads + head + 1)
        turned = mine[lanes(head), :] * scale_a[one] + other[lanes(head), :] * scale_b[one]
        dec_best = jnp.maximum(stats_a[:, one], stats_b[:, one])
        dec_a = jnp.exp(stats_a[:, one] - dec_best)
        dec_b = jnp.exp(stats_b[:, one] - dec_best)
        packed = jnp.where(place == head, dec_best, packed)
        packed = jnp.where(place == heads + head, stats_a[:, two] * dec_a + stats_b[:, two] * dec_b, packed)
        put(lanes(head), turned, dec_mine[:, lanes(head)] * dec_a + dec_other[:, lanes(head)] * dec_b)
    coded = [*split(jnp.concatenate([best, total], axis=0))]
    coded.append(jnp.zeros((HD - 6 * heads, half), f32))
    high, middle, low = split(packed)
    put(
        slice(width, full),
        jnp.concatenate(coded, axis=0),
        high + pltpu.roll(middle, 2 * heads, 1) + pltpu.roll(low, 4 * heads, 1),
    )


def merge_core(mine, other, dec_mine, dec_other, parts):
    full = dec_mine.shape[1]
    tok = mine.shape[1] // parts
    return call(
        merge_core_kernel,
        (((tok + DPAD, full), bf16),) * parts,
        [VMEM] * 4,
        (mine, other, dec_mine, dec_other),
        "merge_core",
        12,
    )


def load_kernel(count, *refs):
    sources, targets, sems = refs[:count], refs[count + 1 : -1], refs[-1]
    copies = []
    for source, target in zip(sources, targets):
        depth = source.shape[-2] // 4
        for lead in range(source.shape[0]) if len(source.shape) == 3 else (None,):
            for part in range(4):
                here = pl.ds(part * depth, depth)
                where = here if lead is None else (lead, here)
                copies.append(
                    pltpu.make_async_copy(source.at[where], target.at[where], sems.at[len(copies)])
                )
    for copy in copies:
        copy.start()
    for copy in copies:
        copy.wait()


def load(arrays, after, name):
    size = sum(arr.size for arr in arrays) * 2
    count = sum(4 * (arr.shape[0] if arr.ndim == 3 else 1) for arr in arrays)
    return call(
        functools.partial(load_kernel, len(arrays)),
        tuple((arr.shape, arr.dtype) for arr in arrays),
        [HBM] * len(arrays) + [VMEM],
        (*arrays, after),
        name,
        1,
        [pltpu.SemaphoreType.DMA((count,))],
        pl.CostEstimate(flops=0, transcendentals=0, bytes_accessed=2 * size),
    )


def project_kernel(parts, head_ref, *refs):
    pieces = refs[:parts]
    weight = refs[parts]
    outs = refs[parts + 1 : -2]
    arranged, product = refs[-2:]
    rows, full = pieces[0].shape
    width = full - HD
    heads = width // HD
    group_rows = outs[0].shape[0]
    places = len(outs)
    share = (rows - DPAD) // places
    dec_share = DEC // places
    stats = []
    for piece in pieces:
        coded = piece[:, width:].astype(f32)
        stats.append(
            (coded + pltpu.roll(coded, HD - 2 * heads, 1)) + pltpu.roll(coded, HD - 4 * heads, 1)
        )
    arranged[...] = jnp.zeros_like(arranged)
    for head in range(heads):
        tops = [s[:, head : head + 1] for s in stats]
        best = functools.reduce(jnp.maximum, tops)
        scales = [jnp.exp(top - best) for top in tops]
        total = tree_sum([s[:, heads + head : heads + head + 1] * c for s, c in zip(stats, scales)])
        acc = tree_sum([piece[:, lanes(head)].astype(f32) * c for piece, c in zip(pieces, scales)])
        attended = acc / total
        for place in range(places):
            row = group_rows * place
            arranged[row : row + share, lanes(head)] = attended[share * place : share * (place + 1)]
            start = rows - DPAD + dec_share * place
            arranged[row + share : row + share + dec_share, lanes(head)] = attended[start : start + dec_share]
    product[...] = jnp.dot(arranged[...].astype(bf16), weight[...], preferred_element_type=f32)
    for offset, out in enumerate(outs):
        out[...] = product[span(lax.bitwise_xor(head_ref[0], offset), group_rows), :].astype(out.dtype)


def project_out(pieces, w_output, head_index, head_count):
    rows = pieces[0].shape[0]
    share = (rows - DPAD) // head_count + 8
    width, columns = w_output.shape
    return call(
        functools.partial(project_kernel, len(pieces)),
        (((share, columns), f32),) + (((share, columns), bf16),) * (head_count - 1),
        [SMEM] + [VMEM] * (len(pieces) + 1),
        (head_index, *pieces, w_output),
        "project_out",
        8,
        [pltpu.VMEM((share * head_count, width), f32), pltpu.VMEM((share * head_count, columns), f32)],
    )


def norm_kernel(parts, head_ref, pre_hbm, dec_pad, gain, *refs):
    arrived = refs[:parts]
    tokens, dec = refs[parts : parts + 2]
    mids = refs[parts + 2 : 2 * parts + 2]
    rows, mid, sem = refs[2 * parts + 2 :]
    share = rows.shape[0]
    head = head_ref[0]
    copy = pltpu.make_async_copy(pre_hbm.at[span(head, share)], rows, sem)
    copy.start()
    total = tree_sum([part[...].astype(f32) for part in arrived])
    copy.wait()
    mid[0:share, :] = rows[...].astype(f32) + total[:share]
    mid[share:, :] = dec_pad[span(head, 8), :] + total[share:]
    for offset, out in enumerate(mids):
        out[...] = mid[:, span(lax.bitwise_xor(head, offset), out.shape[1])]
    values = mid[...]
    meansq = jnp.mean(values * values, axis=-1, keepdims=True)
    scaled = values * lax.rsqrt(meansq + eps_norm) * gain[...]
    tokens[...] = scaled[:share].astype(bf16)
    dec[...] = scaled[share:].astype(bf16)


def experts_kernel(offsets, chunks, chips, scalar_ref, *refs):
    count = len(offsets)
    data = refs[:count]
    query, table_d = refs[count : count + 2]
    weights = refs[count + 2 : count + 8]
    outs = refs[count + 8 : count + 8 + chunks]
    rows_in, table = refs[count + 8 + chunks :]
    each = weights[0].shape[0]
    experts = 2 * each
    piece, depth = data[0].shape
    width = depth // chunks
    long = piece - 8
    share = long // chips
    tok = share * chunks
    base = query.shape[1] - table_d.shape[1]
    rows = count * piece
    tile = rows if rows <= 320 else piece
    places = [lax.bitwise_xor(scalar_ref[0], offset) for offset in range(chunks)]
    for index, offset in enumerate(offsets):
        rows_in[long * index : long * (index + 1), :] = data[index][:long, :]
        row = long * count + 8 * index
        rows_in[row : row + 8, :] = data[index][long:, :]
        table[row : row + 8, :] = table_d[span(places[offset], 8), :]
        for chip in range(chips):
            row = long * index + share * chip
            start = pl.multiple_of(tok * chip + share * places[offset], share)
            table[row : row + share, :] = query[pl.ds(start, share), base:].astype(f32)
    lane = lax.broadcasted_iota(jnp.int32, (tile, table.shape[1]), 1)
    found = {}
    for row in range(0, rows, tile):
        here = slice(row, row + tile)
        block = rows_in[here, :]
        for expert in range(experts):
            w_gate, w_up, _ = weights[:3] if expert < each else weights[3:]
            local = expert % each
            number = lax.bitwise_xor(scalar_ref[1], expert // each) * each + local
            gate = jnp.dot(block, w_gate[local], preferred_element_type=f32)
            up = jnp.dot(block, w_up[local], preferred_element_type=f32)
            act = (gate / (1.0 + jnp.exp(-gate)) * up).astype(bf16)
            factor = jnp.sum(jnp.where(lane == number, table[here, :], 0.0), axis=-1, keepdims=True)
            found[row, expert] = act, factor
    dec_share = DEC // chunks
    for out, place in zip(outs, places):
        values = []
        for row in range(0, rows, tile):
            sums = []
            for first in (0, each):
                total = None
                for expert in range(first, first + each):
                    act, factor = found[row, expert]
                    w_down = weights[2 if first == 0 else 5]
                    down = jnp.dot(
                        act, w_down[expert % each, :, span(place, width)], preferred_element_type=f32
                    )
                    down = down.astype(bf16).astype(f32) * factor
                    total = down if total is None else total + down
                sums.append(total)
            values.append(sums[0] + sums[1])
        value = values[0] if len(values) == 1 else jnp.concatenate(values, axis=0)
        out[: long * count, :] = value[: long * count].astype(bf16)
        out[long * count :, :] = jnp.zeros_like(out[long * count :, :])
        for index in range(count):
            start = long * count + 8 * index
            row = long * count + dec_share * index
            out[row : row + dec_share, :] = value[start : start + dec_share].astype(bf16)


def run_experts(data, offsets, query, table_d, weights, scalars, chips, chunks, name):
    count = len(data)
    piece, depth = data[0].shape
    width = depth // chunks
    tail = -(-(DEC // chunks) * count // 8) * 8
    return list(
        call(
            functools.partial(experts_kernel, offsets, chunks, chips),
            ((((piece - 8) * count + tail, width), bf16),) * chunks,
            [SMEM] + [VMEM] * (count + 8),
            (scalars, *data, query, table_d, *weights),
            name,
            28,
            [
                pltpu.VMEM((count * piece, depth), bf16),
                pltpu.VMEM((count * piece, table_d.shape[1]), f32),
            ],
            pl.CostEstimate(
                flops=12 * count * piece * depth * weights[0].shape[2],
                transcendentals=0,
                bytes_accessed=2 * sum(w.size for w in weights),
            ),
        )
    )


def head_sum_kernel(parts, share, *refs):
    early, late, outs = refs[:parts], refs[parts : 2 * parts], refs[2 * parts :]
    chips = len(outs)
    long = share * chips
    tok = share * parts
    dec_share = DEC // parts
    for out in outs:
        out[tok:, :] = jnp.zeros_like(out[tok:, :])
    for mine in range(parts):
        found, found_d = [], []
        for sender in range(parts):
            index = mine ^ sender
            source, count = early[sender], parts - 1
            if index == parts - 1:
                source, index, count = late[sender], 0, 1
            found.append(source[long * index : long * (index + 1), :].astype(f32))
            row = long * count + dec_share * index
            found_d.append(source[row : row + dec_share, :].astype(f32))
        total = tree_sum(found).astype(bf16)
        total_d = tree_sum(found_d).astype(bf16)
        for chip, out in enumerate(outs):
            out[share * mine : share * (mine + 1), :] = total[share * chip : share * (chip + 1)]
            out[tok + dec_share * mine : tok + dec_share * (mine + 1), :] = total_d


def final_kernel(parts, head_ref, *refs):
    mids, pieces = refs[:parts], refs[parts:-4]
    hidden, dec, packed, placed = refs[-4:]
    tok = hidden.shape[0]
    share = tok // parts
    dec_share = DEC // parts
    total = tree_sum([piece[...].astype(f32) for piece in pieces])
    packed[...] = jnp.zeros_like(packed)
    for offset, mid in enumerate(mids):
        place = lax.bitwise_xor(head_ref[0], offset)
        hidden[span(place, share), :] = (
            mid[0:share, :] + total[share * offset : share * (offset + 1)]
        ).astype(bf16)
        start = tok + dec_share * offset
        packed[8 * offset : 8 * offset + dec_share, :] = (
            mid[share : share + dec_share, :] + total[start : start + dec_share]
        )
        placed[span(place, 8), :] = packed[8 * offset : 8 * offset + 8, :]
    for place in range(parts):
        dec[dec_share * place : dec_share * (place + 1), :] = placed[
            8 * place : 8 * place + dec_share, :
        ].astype(bf16)


def per_device(
    pre_tokens, dec_tokens, attn_gain, w_query, w_key, w_value, w_output, cache_keys, cache_values,
    block_request, block_slot, cache_lens, moe_gain, expert_ids, expert_gates, dec_expert_ids,
    dec_expert_gates, w_gate, w_up, w_down,
):
    tok, model_width = pre_tokens.shape
    width = w_query.shape[1]
    blk_count = lax.axis_size("blk")
    blk_index = lax.axis_index("blk").astype(jnp.int32)
    head_count = lax.axis_size("head")
    head_index = lax.axis_index("head").astype(jnp.int32)
    chips = blk_count // 2
    head_scalar = head_index.reshape(1)
    scalars = jnp.stack([head_index, blk_index])
    part_width = model_width // head_count
    tables = -(-w_gate.shape[0] * blk_count // HD) * HD
    rows = tok + DPAD

    row = jnp.arange(rows, dtype=jnp.int32)
    request = jnp.maximum(row - tok + PRE, 0)[:, None] == jnp.arange(REQS, dtype=jnp.int32)
    positions = jnp.sum(jnp.where(request, cache_lens, 0), axis=1)
    positions = positions + jnp.where(row < tok, blk_index * tok + row, 0)
    frequencies = rope_base ** (-jnp.arange(HD // 2, dtype=f32) / (HD // 2))
    angles = positions.astype(f32)[:, None] * frequencies[None, :]
    cosine = jnp.cos(angles)
    sine = jnp.sin(angles)
    cosine = jnp.concatenate([cosine, cosine], axis=1)
    sine = jnp.concatenate([-sine, sine], axis=1)

    dec_rows = 8 * head_count
    sources = (
        pre_tokens, dec_tokens, attn_gain[None, :], w_query,
        expert_ids.T, expert_gates.T, dec_expert_ids.T, dec_expert_gates.T,
    )
    message, query_d, table_d, normed, dec_pad = call(
        query_kernel,
        (
            ((tok, width + tables), bf16),
            ((DPAD, width), bf16),
            ((dec_rows, tables), f32),
            ((rows, model_width), bf16),
            ((dec_rows, model_width), f32),
        ),
        [HBM] * 8 + [VMEM] * 2,
        (*sources, cosine, sine),
        "queries",
        16,
        [
            *(pltpu.VMEM(source.shape, source.dtype) for source in sources),
            pltpu.VMEM((dec_rows, model_width), f32),
            pltpu.SemaphoreType.DMA((len(sources) + 3,)),
        ],
    )

    def exchange(pieces, axis, step):
        return [pieces[0]] + [swap(pieces[o], axis, step * o) for o in range(1, len(pieces))]

    new_cache, dec_cache, *new = call(
        key_kernel,
        (
            ((2, tok, width), bf16),
            ((2, DEC, width), bf16),
            ((tok, width), bf16),
            ((tok, width), bf16),
            ((DPAD, width), bf16),
            ((DPAD, width), bf16),
        ),
        [VMEM] + [HBM] * 2 + [VMEM] * 2,
        (normed, w_key, w_value, cosine, sine),
        "keys",
        16,
        [
            pltpu.VMEM(w_key.shape, bf16),
            pltpu.VMEM(w_value.shape, bf16),
            pltpu.SemaphoreType.DMA((2,)),
        ],
        pl.CostEstimate(
            flops=4 * rows * model_width * width,
            transcendentals=0,
            bytes_accessed=4 * model_width * width,
        ),
    )
    gate_other = swap(w_gate, "blk", 1)
    pieces = exchange([message] * chips, "blk", 2)
    new_cache, *pieces = lax.optimization_barrier((new_cache, *pieces))
    query_a = jnp.concatenate(pieces, axis=0)
    query_b = swap(query_a, "blk", 1)
    query_b, gate_other = lax.optimization_barrier((query_b, gate_other))

    keep, send, dec = attention(
        query_a, query_b, query_d, new, cache_keys, cache_values,
        (block_request, block_slot, cache_lens, blk_index.reshape(1)),
    )
    pieces = merge_core(keep, swap(send, "blk", 1), dec, swap(dec, "blk", 1), chips)
    *pieces, up_source = lax.optimization_barrier((*pieces, w_up))
    up_other = swap(up_source, "blk", 1)
    (weight,) = load((w_output,), pieces[0], "load_output")
    pieces = exchange(pieces, "blk", 2)
    pieces[-1], weight, up_other = lax.optimization_barrier((pieces[-1], weight, up_other))
    partial = project_out(pieces, weight, head_scalar, head_count)
    *partial, down_source = lax.optimization_barrier((*partial, w_down))
    down_other = swap(down_source, "blk", 1)
    partial = exchange(partial, "head", 1)
    partial[-1], down_other = lax.optimization_barrier((partial[-1], down_other))
    share = tok // head_count
    moe_tok, moe_dec, *mids = call(
        functools.partial(norm_kernel, head_count),
        (
            ((share, model_width), bf16),
            ((8, model_width), bf16),
            *(((share + 8, part_width), f32),) * head_count,
        ),
        [SMEM, HBM] + [VMEM] * (2 + head_count),
        (head_scalar, pre_tokens, dec_pad, moe_gain[None, :], *partial),
        "moe_norm",
        8,
        [
            pltpu.VMEM((share, model_width), bf16),
            pltpu.VMEM((share + 8, model_width), f32),
            pltpu.SemaphoreType.DMA,
        ],
    )
    spread = exchange([moe_tok] * chips, "blk", 2)
    mids[1:-1] = [swap(mids[o], "head", o) for o in range(1, head_count - 1)]
    spread[-1], *mids[1:-1] = lax.optimization_barrier((spread[-1], *mids[1:-1]))
    gathered = jnp.concatenate([*spread, moe_dec], axis=0)
    data = [gathered, swap(gathered, "head", 1), swap(gathered, "head", 2)]
    weights = load((w_gate, w_up, w_down), gathered, "load_experts")
    data[1], data[2], *weights = lax.optimization_barrier((data[1], data[2], *weights))
    cut = gathered.shape[0] // 16 * 8
    relayed = [swap(data[1][:cut], "head", 2), swap(data[2][cut:], "head", 1)]
    data.append(jnp.concatenate(relayed, axis=0))
    weights = (*weights, gate_other, up_other, down_other)
    offsets = tuple(range(head_count))
    shared = (query_a, table_d, weights, scalars, chips, head_count)
    early = run_experts(data[:-1], offsets[:-1], *shared, "experts_early")
    late = run_experts(data[-1:], offsets[-1:], *shared, "experts_late")
    early = exchange(early, "head", 1)
    late[1], early[1] = lax.optimization_barrier((late[1], early[1]))
    late = exchange(late, "head", 1)
    final = call(
        functools.partial(head_sum_kernel, head_count, share),
        (((rows, part_width), bf16),) * chips,
        [VMEM] * (2 * head_count),
        (*early, *late),
        "head_sum",
        8,
    )
    final = list(final)
    *final, mids[-1] = lax.optimization_barrier((*final, mids[-1]))
    final = exchange(final, "blk", 2)
    mids[-1] = swap(mids[-1], "head", head_count - 1)
    hidden, dec_hidden = call(
        functools.partial(final_kernel, head_count),
        (((tok, part_width), bf16), ((DEC, part_width), bf16)),
        [SMEM] + [VMEM] * (head_count + chips),
        (head_scalar, *mids, *final),
        "final",
        8,
        [pltpu.VMEM((dec_rows, part_width), f32), pltpu.VMEM((dec_rows, part_width), f32)],
    )
    return (hidden, dec_hidden, new_cache, dec_cache)


def solution(mesh):
    placed = (
        P("blk", None),
        P(),
        P(),
        P(None, "head"),
        P(None, "head"),
        P(None, "head"),
        P("head", None),
        P("blk", None, "head"),
        P("blk", None, "head"),
        P("blk"),
        P("blk"),
        P(),
        P(),
        P("blk", None),
        P("blk", None),
        P(),
        P(),
        P("blk", None, "head"),
        P("blk", None, "head"),
        P("blk", "head", None),
    )
    return jax.shard_map(
        per_device,
        mesh=mesh,
        in_specs=placed,
        out_specs=(
            P("blk", "head"),
            P(None, "head"),
            P(None, "blk", "head"),
            P(None, None, "head"),
        ),
        check_vma=False,
    )
```
